256 devices in a mesh: segment: 8 (over x, core), dp: 32 (over z, y).
Axes of the slice: x: 4, y: 4, z: 8, core: 2. Of those that a mesh axis runs over, the one named last changes fastest.
Arguments:
- images: bfloat16 [32, 14, 14, 384], P('dp'), may hold values from -6 to 6
- cotangent: bfloat16 [2, 32, 14, 14, 384], P(None, 'dp'), may hold values from -6 to 6
- picks: int32 [2, 16], P(None, 'segment'), may hold values from 0 to 47
- section_sizes: int32 [8], P('segment'), may hold values from 1 to 2, 12 in all
- kernels: bfloat16 [16, 48, 25, 384], P('segment'), may hold values from -1.1953125 to 1.1953125
- weights: bfloat16 [16, 48, 384, 384], P('segment', None, 'dp'), may hold values from -0.15625 to 0.15625
- first_moment: float32 [16, 48, 384, 384], P('segment', None, 'dp'), may hold values from -0.006 to 0.006
- second_moment: float32 [16, 48, 384, 384], P('segment', None, 'dp'), may hold values from 1e-08 to 1e-07
Outputs:
- new_weights: bfloat16 [2, 16, 384, 384], P(None, 'segment', 'dp')
- new_first: float32 [2, 16, 384, 384], P(None, 'segment', 'dp')
- new_second: float32 [2, 16, 384, 384], P(None, 'segment', 'dp')
The draws below stay inside these ranges and needn't reach their ends.
Inputs may be any that keep to these rules, and one draw needn't show every extreme that they name: `section_sizes`: the counts sum to 12, and one of them equals 2.
All inputs are finite; a program needn't handle non-finite values. No bound on the sum of `section_sizes` on one device may be relied on, other than what follows from the above.
Results may differ from the reference program's by a relative error of at most 0.03.
Values may be sent and summed in bfloat16 or wider, within the bound.
No kernel may reach another device: no remote copies, remote signals or barrier semaphores. Data moves between devices by JAX's collectives and lax.ppermute only.
A program may use at most 128 MiB of HBM per device.

```python
import math
import jax
import jax.numpy as jnp
import numpy as np
from jax import lax

C = 384
OPS = 48
SIDE = 14
SLOTS = 2
BLOCKS = 16
IMAGES = 32
N_SEGMENT = 8


def draw_picks(key, part):
    first_key = jax.random.fold_in(key, 11)
    second_key = jax.random.fold_in(key, 12)
    coin_key = jax.random.fold_in(key, 13)
    forced_key = jax.random.fold_in(key, 14)
    first = jax.random.randint(first_key, (BLOCKS,), 0, OPS)
    second = jax.random.randint(second_key, (BLOCKS,), 0, OPS)
    coins = jax.random.randint(coin_key, (BLOCKS,), 0, 4)
    sections = BLOCKS // SLOTS
    forced = jax.random.randint(forced_key, (), 0, sections) * SLOTS
    same = (coins == 0) | (jnp.arange(BLOCKS) == forced)
    second = jnp.where(same, first, second)
    return jnp.stack([first, second]).astype(jnp.int32)


def level_of(own_key, shape, split, low, top_value):
    def one(dim, blocks):
        heights = jax.random.uniform(jax.random.fold_in(jax.random.fold_in(own_key, 6), dim), (blocks,), jnp.float32, low / len(split), top_value / len(split))
        return jnp.repeat(jnp.exp(heights), shape[dim] // blocks).reshape((-1,) + (1,) * (len(shape) - dim - 1))

    loudness = one(*split[0])
    for cut in split[1:]:
        loudness = loudness * one(*cut)
    return loudness


def profile(amount, total, most, lean):
    portions = [(1 << 20) // math.isqrt(rank ** lean) + 1 for rank in range(2, amount + 1)]
    surplus, given = total - most - (amount - 1), [1] * (amount - 1)
    while surplus > 0:
        movable = [i for i in range(amount - 1) if given[i] < most]
        whole, remaining = sum([portions[i] for i in movable]), surplus
        for i in movable:
            addition = min(most - given[i], max(1, remaining * portions[i] // whole), surplus)
            given[i] = given[i] + addition
            surplus = surplus - addition
    return np.array([most] + given)


def uneven_parts(key, count, total, reach, lean):
    if count == 2:
        one = jax.random.randint(key, (), max(1, total - reach), min(reach, total - 1) + 1)
        return jnp.stack([one, total - one])
    lengths = jnp.asarray(profile(count, total, reach, lean), jnp.int32)
    twos = (count - 1) // 2
    source_of, taker = lengths[1:1 + 2 * twos:2], lengths[2:2 + 2 * twos:2]
    room = jnp.minimum(source_of - 1, reach - taker)
    moved = jax.random.randint(jax.random.fold_in(key, 1), (twos,), 0, 1 << 20) % (room + 1)
    lengths = lengths.at[1:1 + 2 * twos:2].set(source_of - moved).at[2:2 + 2 * twos:2].set(taker + moved)
    return lengths[jax.random.permutation(jax.random.fold_in(key, 2), count)]


def scatter_about(own_key, dims, scale, reach, shards=(), dtype=jnp.bfloat16):
    entries = scale * jax.random.normal(own_key, dims, jnp.float32)
    if shards:
        entries = entries * level_of(own_key, dims, shards, -0.22, 0.18)
    return jnp.clip(entries, -reach, reach).astype(dtype)


def setup_inputs(seed: int = 0) -> dict:
    splits = jax.random.split(jax.random.key(seed), 9)
    return {
        "images": scatter_about(splits[0], (IMAGES, SIDE, SIDE, C), 1.0, 6.0, ((0, 32),)),
        "cotangent": scatter_about(splits[1], (2, IMAGES, SIDE, SIDE, C), 1.0, 6.0, ((1, 32),)),
        "picks": draw_picks(jax.random.fold_in(splits[8], 71), 0),
        "section_sizes": uneven_parts(splits[3], N_SEGMENT, 3 * N_SEGMENT // 2, SLOTS, 2).astype(jnp.int32),
        "kernels": scatter_about(splits[4], (BLOCKS, OPS, 25, C), 0.2, 1.1953125, ((0, 8),)),
        "weights": scatter_about(splits[5], (BLOCKS, OPS, C, C), (4 * C) ** -0.5, 0.15625, ((0, 8), (2, 32))),
        "first_moment": scatter_about(splits[6], (BLOCKS, OPS, C, C), 0.001, 0.006, ((0, 8), (2, 32)), jnp.float32),
        "second_moment": jnp.clip(jnp.exp(math.log(1.0000000116860974e-07) - 2.3025851 * jax.random.uniform(splits[7], (BLOCKS, OPS, C, C), jnp.float32) ** level_of(splits[7], (BLOCKS, OPS, C, C), ((0, 8), (2, 32)), -0.2, 0.2)), 9.99999993922529e-09, 1.0000000116860974e-07),
    }


first_decay = 0.9
second_decay = 0.999
learn_rate = 0.01
adam_epsilon = 1e-08
first_bias = 1.0 - 0.9 ** 10
second_bias = 1.0 - 0.999 ** 10

def spatial(field, kernel, flipped):
    side = field.shape[1]
    padded = jnp.pad(field, ((0, 0), (2, 2), (2, 2), (0, 0)))
    total = jnp.zeros(field.shape, jnp.float32)
    for row_tap in range(5):
        for col_tap in range(5):
            row_start = 4 - row_tap if flipped else row_tap
            col_start = 4 - col_tap if flipped else col_tap
            window = padded[:, row_start:row_start + side, col_start:col_start + side, :]
            total = total + kernel[row_tap * 5 + col_tap].astype(jnp.float32) * window
    return total

def block_forward(inputs, kernel, weight):
    width = inputs.shape[-1]
    mixed = spatial(inputs.astype(jnp.float32), kernel, False)
    hidden = jax.nn.silu(mixed).astype(jnp.bfloat16)
    update = jnp.dot(hidden.reshape(-1, width), weight, preferred_element_type=jnp.float32)
    return (inputs.astype(jnp.float32) + update.reshape(inputs.shape)).astype(jnp.bfloat16)

def block_backward(inputs, upstream, kernel, weight):
    width = inputs.shape[-1]
    mixed = spatial(inputs.astype(jnp.float32), kernel, False)
    hidden = jax.nn.silu(mixed).astype(jnp.bfloat16)
    flat_up = upstream.reshape(-1, width)
    back_hidden = lax.dot_general(flat_up, weight, (((1,), (1,)), ((), ())), preferred_element_type=jnp.float32)
    back_hidden = back_hidden.reshape(inputs.shape)
    sigma = jax.nn.sigmoid(mixed)
    back_mixed = back_hidden * sigma * (1.0 + mixed * (1.0 - sigma))
    back_inputs = (upstream.astype(jnp.float32) + spatial(back_mixed, kernel, True)).astype(jnp.bfloat16)
    return (back_inputs, hidden)

def reference(images, cotangent, picks, section_sizes, kernels, weights, first_moment, second_moment):
    total_rows = images.shape[0] * images.shape[1] * images.shape[2]
    width = images.shape[-1]
    active = [block_index % SLOTS < section_sizes[block_index // SLOTS] for block_index in range(BLOCKS)]
    sums = []
    for subnet in range(2):
        current = images
        stored = []
        for block_index in range(BLOCKS):
            chosen = picks[subnet, block_index]
            kernel = kernels[block_index, chosen]
            weight = weights[block_index, chosen]
            stored.append(current)
            current = lax.cond(active[block_index], lambda value: block_forward(value, kernel, weight), lambda value: value, current)
        upstream = cotangent[subnet]
        grads = [None] * BLOCKS
        for block_index in reversed(range(BLOCKS)):
            chosen = picks[subnet, block_index]
            kernel = kernels[block_index, chosen]
            weight = weights[block_index, chosen]

            def taken(pair):
                back_inputs, hidden = block_backward(pair[0], pair[1], kernel, weight)
                summed = lax.dot_general(hidden.reshape(-1, width), pair[1].reshape(-1, width), (((0,), (0,)), ((), ())), preferred_element_type=jnp.float32)
                return (back_inputs, summed)

            def skipped(pair):
                return (pair[1], jnp.zeros((width, width), jnp.float32))
            upstream, summed = lax.cond(active[block_index], taken, skipped, (stored[block_index], upstream))
            grads[block_index] = summed
        sums.append(grads)
    out_weights, out_first, out_second = ([], [], [])
    for subnet in range(2):
        row_w, row_m, row_v = ([], [], [])
        for block_index in range(BLOCKS):
            chosen = picks[subnet, block_index]
            other = picks[1 - subnet, block_index]
            grad = (sums[subnet][block_index] + jnp.where(other == chosen, sums[1 - subnet][block_index], jnp.zeros_like(sums[subnet][block_index]))) / total_rows
            weight = weights[block_index, chosen]
            moment_one = first_moment[block_index, chosen]
            moment_two = second_moment[block_index, chosen]
            next_one = first_decay * moment_one + (1.0 - first_decay) * grad
            next_two = second_decay * moment_two + (1.0 - second_decay) * grad * grad
            next_weight = (weight.astype(jnp.float32) - learn_rate * (next_one / first_bias) / (jnp.sqrt(next_two / second_bias) + adam_epsilon)).astype(jnp.bfloat16)
            live = active[block_index]
            row_w.append(jnp.where(live, next_weight, weight))
            row_m.append(jnp.where(live, next_one, moment_one))
            row_v.append(jnp.where(live, next_two, moment_two))
        out_weights.append(jnp.stack(row_w))
        out_first.append(jnp.stack(row_m))
        out_second.append(jnp.stack(row_v))
    return (jnp.stack(out_weights), jnp.stack(out_first), jnp.stack(out_second))
```

```python
import functools

import jax
import jax.numpy as jnp
from jax import lax
from jax.experimental import pallas as pl
from jax.experimental.pallas import tpu as pltpu
from jax.sharding import PartitionSpec as P

first_decay = 0.9
second_decay = 0.999
learn_rate = 0.01
adam_epsilon = 1e-08
first_bias = 1.0 - 0.9**10
second_bias = 1.0 - 0.999**10

SIDE = 14
PITCH = 16
ROWS = SIDE * PITCH
LANES = 128
HEAD = 8 + 2 * PITCH
PADDED = 8 + (SIDE + 4) * PITCH + 8
BF = jnp.bfloat16
F32 = jnp.float32

ANY = pl.BlockSpec(memory_space=pl.ANY)
SMEM = pl.BlockSpec(memory_space=pltpu.SMEM)
PARAMS = pltpu.CompilerParams(vmem_limit_bytes=24 << 20)


def call(kernel, outs, in_specs, scratch, aliases=None, cost=2_000_000_000):
    return pl.pallas_call(
        kernel,
        out_shape=[jax.ShapeDtypeStruct(s, d) for s, d in outs],
        in_specs=in_specs,
        out_specs=[ANY] * len(outs),
        scratch_shapes=scratch,
        input_output_aliases=aliases or {},
        compiler_params=PARAMS,
        cost_estimate=pl.CostEstimate(flops=cost, bytes_accessed=1_000_000, transcendentals=0),
    )


def expand(slot, tall):
    shape = (768, 384) if tall else (384, 768)
    row = lax.broadcasted_iota(jnp.int32, shape, 1 if tall else 0)
    place = lax.broadcasted_iota(jnp.int32, shape, 0 if tall else 1)
    target = row + 12 * ((row * 10923) >> 17) + 12 * slot
    return jnp.where(place == target, 1.0, 0.0).astype(BF)


def keep_mask(shape):
    return (lax.broadcasted_iota(jnp.int32, shape, 0) & (PITCH - 1)) < SIDE


def conv_rows(pad, taps, group, flipped, emit):
    sign = -1 if flipped else 1
    cols = pl.ds(group * LANES, LANES)
    weights = [jnp.broadcast_to(taps[pl.ds(i, 1), cols], (PITCH, LANES)) for i in range(25)]
    for p in range(0, SIDE, 2):
        totals = [None, None]
        for da in range(-2, 4):
            for e in range(-2, 3):
                start = HEAD + PITCH * (p + da) + e
                window = pad[group, pl.ds(start, PITCH), :]
                for k in range(2):
                    a = da - k
                    if -2 <= a <= 2:
                        tap = (sign * a + 2) * 5 + (sign * e + 2)
                        term = weights[tap] * window
                        totals[k] = term if totals[k] is None else totals[k] + term
        emit(p, totals[0])
        emit(p + 1, totals[1])


def clear_pad(pad):
    for g in range(3):
        pad[g, pl.ds(0, HEAD), :] = jnp.zeros((HEAD, LANES), F32)
        pad[g, pl.ds(HEAD + ROWS, PADDED - HEAD - ROWS), :] = jnp.zeros(
            (PADDED - HEAD - ROWS, LANES), F32
        )


def fill_pad(pad, value):
    for g in range(3):
        pad[g, pl.ds(HEAD, ROWS), :] = value[:, g * LANES : (g + 1) * LANES]


def spread(image, flat):
    flat[...] = jnp.zeros(flat.shape, flat.dtype)
    for p in range(SIDE):
        flat[pl.ds(p * PITCH, SIDE), :] = image[p]


def live_of(meta, t):
    odd = (t & 1) == 1
    count = jnp.where(t < 2, meta[2], meta[3])
    return jnp.logical_or(jnp.logical_not(odd), count == 2)


def run_forward(meta, pad, flat, wsc, taps, hsc, dsc, after, skip_last):
    last = 1 + meta[3] if False else jnp.where(meta[3] == 2, 3, 2)
    fill_pad(pad, flat[...].astype(F32))

    def slot(t, carry):
        @pl.when(live_of(meta, t))
        def _():
            for g in range(3):

                def emit(p, u, g=g):
                    rows, cols = pl.ds(p * PITCH, PITCH), pl.ds(g * LANES, LANES)
                    s = 0.5 * jnp.tanh(0.5 * u) + 0.5
                    us = u * s
                    hsc[t, rows, cols] = us.astype(BF)
                    dsc[t, rows, cols] = s * (1.0 + (u - us))

                conv_rows(pad, taps.at[t], g, False, emit)
            after(t)

            def update():
                value = jnp.dot(hsc[t], wsc[t], preferred_element_type=F32)
                value = flat[...].astype(F32) + value
                rounded = jnp.where(keep_mask(value.shape), value, 0.0).astype(BF)
                flat[...] = rounded
                fill_pad(pad, rounded.astype(F32))

            if skip_last:
                pl.when(t != last)(update)
            else:
                update()

        return carry

    lax.fori_loop(0, 4, slot, 0)


def run_backward(meta, pad, flat, wsc, taps, dsc, ysc, before, after, skip_first):
    def slot(i, carry):
        t = 3 - i

        @pl.when(live_of(meta, t))
        def _():
            ysc[t] = flat[...]
            after(t)

            def chain():
                before(t)
                dh = lax.dot_general(
                    flat[...], wsc[t], (((1,), (1,)), ((), ())), preferred_element_type=F32
                )
                fill_pad(pad, dh * dsc[t])
                for g in range(3):

                    def emit(p, total, g=g):
                        rows, cols = pl.ds(p * PITCH, PITCH), pl.ds(g * LANES, LANES)
                        value = ysc[t, rows, cols].astype(F32) + total
                        keep = lax.broadcasted_iota(jnp.int32, value.shape, 0) < SIDE
                        flat[rows, cols] = jnp.where(keep, value, 0.0).astype(BF)

                    conv_rows(pad, taps.at[t], g, True, emit)

            if skip_first:
                pl.when(t != 0)(chain)
            else:
                chain()

        return carry

    lax.fori_loop(0, 4, slot, 0)


def each_live(meta, action):
    def slot(t, carry):
        pl.when(live_of(meta, t))(functools.partial(action, t))
        return carry

    lax.fori_loop(0, 4, slot, 0)


def first_kernel(meta, img, packed, kown, koth, y, wout, tout, hs, ds,
                 imsc, rsc, kbuf, wsc, taps, flat, pad, hsc, dsc, sems, hsems, dsems):
    core = meta[1]
    active = meta[0] == 0
    copies = [
        pltpu.make_async_copy(packed, rsc, sems.at[0]),
        pltpu.make_async_copy(kown, kbuf.at[0], sems.at[1]),
        pltpu.make_async_copy(koth, kbuf.at[1], sems.at[2]),
        pltpu.make_async_copy(img.at[0], imsc, sems.at[3]),
    ]
    for c in copies:
        c.start()
    clear_pad(pad)
    for c in copies[1:]:
        c.wait()
    for o in range(2):
        for j in range(2):
            taps[(2 * o + j + 2 * core) & 3] = kbuf[o, j].astype(F32)
    tcopy = pltpu.make_async_copy(taps, tout, sems.at[1])
    tcopy.start()
    copies[0].wait()
    for j in range(2):
        pick = expand(j, False)
        for o in range(2):
            rows = rsc[:, pl.ds(24 * o, 24), :].reshape(768, 384)
            wsc[(2 * o + j + 2 * core) & 3] = jnp.dot(
                pick, rows, preferred_element_type=F32
            ).astype(BF)
    wcopy = pltpu.make_async_copy(wsc, wout, sems.at[0])
    wcopy.start()

    def hcopy(t):
        return pltpu.make_async_copy(hsc.at[t], hs.at[t], hsems.at[t])

    def dcopy(t):
        return pltpu.make_async_copy(dsc.at[t], ds.at[t], dsems.at[t])

    @pl.when(active)
    def _():
        spread(imsc, flat)

        def after(t):
            hcopy(t).start()
            dcopy(t).start()

        run_forward(meta, pad, flat, wsc, taps, hsc, dsc, after, False)
        ycopy = pltpu.make_async_copy(flat, y, sems.at[3])
        ycopy.start()
        ycopy.wait()

        def finish(t):
            hcopy(t).wait()
            dcopy(t).wait()

        each_live(meta, finish)

    tcopy.wait()
    wcopy.wait()


def forward_kernel(step, meta, cur, win, tin, hin, din, y, hs, ds,
                   wsc, taps, flat, pad, hsc, dsc, sems, hsems, dsems):
    del hin, din

    def hcopy(t):
        return pltpu.make_async_copy(hsc.at[t], hs.at[t], hsems.at[t])

    def dcopy(t):
        return pltpu.make_async_copy(dsc.at[t], ds.at[t], dsems.at[t])

    @pl.when(meta[0] == step)
    def _():
        copies = [
            pltpu.make_async_copy(cur, flat, sems.at[0]),
            pltpu.make_async_copy(tin, taps, sems.at[1]),
            pltpu.make_async_copy(win, wsc, sems.at[2]),
        ]
        for c in copies:
            c.start()
        clear_pad(pad)
        for c in copies:
            c.wait()

        def after(t):
            hcopy(t).start()
            dcopy(t).start()

        run_forward(meta, pad, flat, wsc, taps, hsc, dsc, after, False)
        ycopy = pltpu.make_async_copy(flat, y, sems.at[0])
        ycopy.start()
        ycopy.wait()

        def finish(t):
            hcopy(t).wait()
            dcopy(t).wait()

        each_live(meta, finish)


def middle_kernel(step, meta, cur, cot, win, tin, hin, y, hs, ys,
                  imsc, wsc, taps, flat, pad, hsc, dsc, ysc, sems, hsems, ysems):
    del hin

    def hcopy(t):
        return pltpu.make_async_copy(hsc.at[t], hs.at[t], hsems.at[t])

    def yscopy(t):
        return pltpu.make_async_copy(ysc.at[t], ys.at[t], ysems.at[t])

    @pl.when(meta[0] == step)
    def _():
        copies = [
            pltpu.make_async_copy(cur, flat, sems.at[0]),
            pltpu.make_async_copy(tin, taps, sems.at[1]),
            pltpu.make_async_copy(win, wsc, sems.at[2]),
            pltpu.make_async_copy(cot.at[meta[1], 0], imsc, sems.at[3]),
        ]
        for c in copies:
            c.start()
        clear_pad(pad)
        for c in copies:
            c.wait()
        run_forward(
            meta, pad, flat, wsc, taps, hsc, dsc, lambda t: hcopy(t).start(), True
        )
        spread(imsc, flat)
        run_backward(
            meta, pad, flat, wsc, taps, dsc, ysc, lambda t: None, lambda t: yscopy(t).start(), False
        )
        ycopy = pltpu.make_async_copy(flat, y, sems.at[0])
        ycopy.start()
        ycopy.wait()

        def finish(t):
            hcopy(t).wait()
            yscopy(t).wait()

        each_live(meta, finish)


def backward_kernel(step, meta, cur, win, tin, ds, yin, y, ys,
                    wsc, taps, flat, pad, dsc, ysc, sems, dsems, ysems):
    del yin

    def dcopy(t):
        return pltpu.make_async_copy(ds.at[t], dsc.at[t], dsems.at[t])

    def yscopy(t):
        return pltpu.make_async_copy(ysc.at[t], ys.at[t], ysems.at[t])

    @pl.when(meta[0] == step)
    def _():
        copies = [
            pltpu.make_async_copy(cur, flat, sems.at[0]),
            pltpu.make_async_copy(win, wsc, sems.at[2]),
            pltpu.make_async_copy(tin, taps, sems.at[1]),
        ]
        for c in copies:
            c.start()
        each_live(meta, lambda t: dcopy(t).start())
        clear_pad(pad)
        for c in copies:
            c.wait()
        run_backward(
            meta, pad, flat, wsc, taps, dsc, ysc,
            lambda t: dcopy(t).wait(), lambda t: yscopy(t).start(), False,
        )
        ycopy = pltpu.make_async_copy(flat, y, sems.at[0])
        ycopy.start()
        ycopy.wait()
        each_live(meta, lambda t: yscopy(t).wait())


def last_kernel(meta, cur, win, tin, ds, hs, ys, send,
                wsc, taps, flat, pad, dsc, hsc, ysc, total, gsc, sems, dsems):
    core = meta[1]
    active = meta[0] == 0

    def dcopy(t):
        return pltpu.make_async_copy(ds.at[t], dsc.at[t], dsems.at[t])

    hcopy = pltpu.make_async_copy(hs, hsc, sems.at[3])
    hcopy.start()

    @pl.when(active)
    def _():
        copies = [
            pltpu.make_async_copy(cur, flat, sems.at[0]),
            pltpu.make_async_copy(win, wsc, sems.at[2]),
            pltpu.make_async_copy(tin, taps, sems.at[1]),
        ]
        for c in copies:
            c.start()
        each_live(meta, lambda t: dcopy(t).start())
        clear_pad(pad)
        for c in copies:
            c.wait()

        run_backward(
            meta, pad, flat, wsc, taps, dsc, ysc,
            lambda t: dcopy(t).wait(), lambda t: None, True,
        )
        dcopy(0).wait()

    @pl.when(jnp.logical_not(active))
    def _():
        copy = pltpu.make_async_copy(ys, ysc, sems.at[0])
        copy.start()
        copy.wait()

    hcopy.wait()

    def term(t, j):
        turned = lax.dot_general(
            expand(j, True), hsc[t], (((1,), (1,)), ((), ())), preferred_element_type=F32
        ).astype(BF)
        return jnp.dot(turned, ysc[t], preferred_element_type=F32)

    for o in range(2):
        base = (2 * o + 2 * core) & 3
        total[...] = term(base, 0)

        @pl.when(live_of(meta, base + 1))
        def _():
            total[...] += term(base + 1, 1)

        gsc[:, pl.ds(24 * o, 24), :] = total[...].astype(BF).reshape(32, 24, 384)
    out = pltpu.make_async_copy(gsc, send, sems.at[0])
    out.start()
    out.wait()


def prepare_kernel(meta, picks, weights, kernels, first, second, wown, woth, kown, koth,
                   wrows, frows, srows, sems):
    core = meta[1]
    copies = []

    def add(src, dst):
        copies.append(pltpu.make_async_copy(src, dst, sems.at[len(copies)]))

    for j in range(2):
        mine, theirs = picks[core, j], picks[1 - core, j]
        add(weights.at[j, mine], wown.at[j])
        add(weights.at[j, theirs], woth.at[j])
        add(kernels.at[j, mine], kown.at[j])
        add(kernels.at[j, theirs], koth.at[j])
        for n in range(2):
            add(weights.at[j, picks[n, j]], wrows.at[n, j])
            add(first.at[j, picks[n, j]], frows.at[n, j])
            add(second.at[j, picks[n, j]], srows.at[n, j])
    for c in copies:
        c.start()
    for c in copies:
        c.wait()


def sum_kernel(packed, own, other, rsc, osc, sem):
    copy = pltpu.make_async_copy(packed, rsc, sem.at[0])
    copy.start()
    copy.wait()
    total = rsc[0].astype(F32)
    for d in range(1, 32):
        total = total + rsc[d].astype(F32)
    osc[...] = total
    outs = [
        pltpu.make_async_copy(osc.at[pl.ds(0, 24)], own, sem.at[0]),
        pltpu.make_async_copy(osc.at[pl.ds(24, 24)], other, sem.at[1]),
    ]
    for c in outs:
        c.start()
    for c in outs:
        c.wait()


def adam_kernel(total_rows, meta, picks, own, other, wrows, frows, srows, new_w, new_f, new_s):
    core = meta[1]
    count = jnp.where(core == 0, meta[2], meta[3])
    for j in range(2):
        mine = own[pl.ds(12 * j, 12), :]
        theirs = other[pl.ds(12 * j, 12), :]
        same = picks[0, j] == picks[1, j]
        live = count > j
        for n in range(2):
            here = core == n
            grad = jnp.where(here, mine, theirs)
            rest = jnp.where(here, theirs, mine)
            grad = (grad + jnp.where(same, rest, jnp.zeros_like(rest))) / total_rows
            weight, one, two = wrows[n, j], frows[n, j], srows[n, j]
            next_one = first_decay * one + (1.0 - first_decay) * grad
            next_two = second_decay * two + (1.0 - second_decay) * grad * grad
            next_weight = (
                weight.astype(F32)
                - learn_rate
                * (next_one / first_bias)
                / (jnp.sqrt(next_two / second_bias) + adam_epsilon)
            ).astype(BF)
            new_w[n, j] = jnp.where(live, next_weight, weight)
            new_f[n, j] = jnp.where(live, next_one, one)
            new_s[n, j] = jnp.where(live, next_two, two)


def body(images, cotangent, picks, section_sizes, kernels, weights, first_moment, second_moment):
    width = images.shape[-1]
    own_segment = lax.axis_index("segment")
    segments = lax.axis_size("segment")
    parts = lax.axis_size("dp")
    total_rows = images.shape[0] * images.shape[1] * images.shape[2] * parts
    swap = [(s, s ^ 1) for s in range(segments)]
    ahead = [(s, (s + 2) % segments) for s in range(segments)]
    behind = [(s, (s - 2) % segments) for s in range(segments)]

    DMA = pltpu.SemaphoreType.DMA
    V = pltpu.VMEM
    state = (4, ROWS, width)
    flat_shape = (ROWS, width)
    s_w, s_t, s_flat = V((4, width, width), BF), V((4, 25, width), F32), V(flat_shape, BF)
    s_pad, s_h, s_d, s_y = V((3, PADDED, LANES), F32), V(state, BF), V(state, F32), V(state, BF)
    s_im, s_r = V((SIDE, SIDE, width), BF), V((32, 48, width), BF)

    core = own_segment & 1
    place = lax.broadcasted_iota(jnp.int32, (4,), 0)
    sizes_other = lax.ppermute(section_sizes, "segment", swap)
    early = jnp.where(place == 0, own_segment >> 1, core)

    rows_shape, kern_shape = (2, 12, width), (2, 25, width)
    four = (2, 2, 12, width)
    wown, woth, kown, koth_send, wrows, frows, srows = call(
        prepare_kernel,
        [(rows_shape, BF), (rows_shape, BF), (kern_shape, BF), (kern_shape, BF),
         (four, BF), (four, F32), (four, F32)],
        [SMEM, SMEM, ANY, ANY, ANY, ANY],
        [DMA((20,))],
        cost=1000,
    )(early, picks, weights, kernels, first_moment, second_moment)
    wrecv = lax.ppermute(woth, "segment", swap)
    koth = lax.ppermute(koth_send, "segment", swap)
    size_low = jnp.where(core == 0, section_sizes[0], sizes_other[0])
    size_high = jnp.where(core == 0, sizes_other[0], section_sizes[0])
    meta = jnp.where(place < 2, early, jnp.where(place == 2, size_low, size_high))

    message = jnp.concatenate([wown, wrecv], axis=0).reshape(1, 48, width)
    packed = lax.all_to_all(jnp.broadcast_to(message, (parts, 48, width)), "dp", 0, 0)

    y, wall, taps, hs, ds = call(
        first_kernel,
        [(flat_shape, BF), ((4, width, width), BF), ((4, 25, width), F32), (state, BF), (state, F32)],
        [SMEM, ANY, ANY, ANY, ANY],
        [s_im, s_r, V((2, 2, 25, width), BF), s_w, s_t, s_flat, s_pad, s_h, s_d,
         DMA((4,)), DMA((4,)), DMA((4,))],
    )(meta, images, packed, kown, koth)
    cur = lax.ppermute(y, "segment", ahead)
    for step in (1, 2):
        y, hs, ds = call(
            functools.partial(forward_kernel, step),
            [(flat_shape, BF), (state, BF), (state, F32)],
            [SMEM] + [ANY] * 5,
            [s_w, s_t, s_flat, s_pad, s_h, s_d, DMA((3,)), DMA((4,)), DMA((4,))],
            {4: 1, 5: 2},
        )(meta, cur, wall, taps, hs, ds)
        cur = lax.ppermute(y, "segment", ahead)
    y, hs, ys = call(
        functools.partial(middle_kernel, 3),
        [(flat_shape, BF), (state, BF), (state, BF)],
        [SMEM] + [ANY] * 5,
        [s_im, s_w, s_t, s_flat, s_pad, s_h, s_d, s_y, DMA((4,)), DMA((4,)), DMA((4,))],
        {5: 1},
    )(meta, cur, cotangent, wall, taps, hs)
    cur = lax.ppermute(y, "segment", behind)
    for step in (2, 1):
        y, ys = call(
            functools.partial(backward_kernel, step),
            [(flat_shape, BF), (state, BF)],
            [SMEM] + [ANY] * 5,
            [s_w, s_t, s_flat, s_pad, s_d, s_y, DMA((3,)), DMA((4,)), DMA((4,))],
            {5: 1},
        )(meta, cur, wall, taps, ds, ys)
        cur = lax.ppermute(y, "segment", behind)
    (send,) = call(
        last_kernel,
        [((32, 48, width), BF)],
        [SMEM] + [ANY] * 6,
        [s_w, s_t, s_flat, s_pad, s_d, s_h, s_y, V((768, width), F32), s_r, DMA((4,)), DMA((4,))],
    )(meta, cur, wall, taps, ds, hs, ys)
    landed = lax.all_to_all(send, "dp", 0, 0)
    own, for_other = call(
        sum_kernel,
        [((24, width), F32), ((24, width), F32)],
        [ANY],
        [s_r, V((48, width), F32), DMA((2,))],
    )(landed)
    other = lax.ppermute(for_other, "segment", swap)
    whole = pl.BlockSpec(memory_space=pltpu.VMEM)
    new_w, new_f, new_s = pl.pallas_call(
        functools.partial(adam_kernel, float(total_rows)),
        out_shape=[
            jax.ShapeDtypeStruct(four, BF),
            jax.ShapeDtypeStruct(four, F32),
            jax.ShapeDtypeStruct(four, F32),
        ],
        in_specs=[SMEM, SMEM] + [whole] * 5,
        out_specs=[whole] * 3,
        compiler_params=PARAMS,
    )(meta, picks, own, other, wrows, frows, srows)
    return (new_w, new_f, new_s)


def solution(mesh):
    return jax.shard_map(
        body,
        mesh=mesh,
        in_specs=(
            P("dp", None, None, None),
            P(None, "dp", None, None, None),
            P(None, "segment"),
            P("segment"),
            P("segment", None, None, None),
            P("segment", None, "dp", None),
            P("segment", None, "dp", None),
            P("segment", None, "dp", None),
        ),
        out_specs=(
            P(None, "segment", "dp", None),
            P(None, "segment", "dp", None),
            P(None, "segment", "dp", None),
        ),
        check_vma=False,
    )
```

```python
import functools

import jax
import jax.numpy as jnp
from jax import lax
from jax.experimental import pallas as pl
from jax.experimental.pallas import tpu as pltpu
from jax.sharding import PartitionSpec as P

first_decay = 0.9
second_decay = 0.999
learn_rate = 0.01
adam_epsilon = 1e-08
first_bias = 1.0 - 0.9**10
second_bias = 1.0 - 0.999**10

SIDE = 14
PITCH = 16
ROWS = SIDE * PITCH
LANES = 128
HEAD = 8 + 2 * PITCH
PADDED = 8 + (SIDE + 4) * PITCH + 8
BF = jnp.bfloat16
F32 = jnp.float32

ANY = pl.BlockSpec(memory_space=pl.ANY)
SMEM = pl.BlockSpec(memory_space=pltpu.SMEM)
PARAMS = pltpu.CompilerParams(vmem_limit_bytes=24 << 20)


VMEM = pl.BlockSpec(memory_space=pltpu.VMEM)


def call(kernel, outs, in_specs, scratch, aliases=None, cost=2_000_000_000):
    return pl.pallas_call(
        kernel,
        out_shape=[jax.ShapeDtypeStruct(s, d) for s, d in outs],
        in_specs=in_specs,
        out_specs=[VMEM] * len(outs),
        scratch_shapes=scratch,
        input_output_aliases=aliases or {},
        compiler_params=PARAMS,
        cost_estimate=pl.CostEstimate(flops=cost, bytes_accessed=1_000_000, transcendentals=0),
    )


def keep_mask(shape):
    return (lax.broadcasted_iota(jnp.int32, shape, 0) & (PITCH - 1)) < SIDE


def conv_rows(pad, taps, group, flipped, emit):
    sign = -1 if flipped else 1
    cols = pl.ds(group * LANES, LANES)
    weights = [jnp.broadcast_to(taps[pl.ds(i, 1), cols], (PITCH, LANES)) for i in range(25)]
    for p in range(0, SIDE, 2):
        totals = [None, None]
        for da in range(-2, 4):
            for e in range(-2, 3):
                start = HEAD + PITCH * (p + da) + e
                window = pad[group, pl.ds(start, PITCH), :]
                for k in range(2):
                    a = da - k
                    if -2 <= a <= 2:
                        tap = (sign * a + 2) * 5 + (sign * e + 2)
                        term = weights[tap] * window
                        totals[k] = term if totals[k] is None else totals[k] + term
        emit(p, totals[0])
        emit(p + 1, totals[1])


def clear_pad(pad):
    for g in range(3):
        pad[g, pl.ds(0, HEAD), :] = jnp.zeros((HEAD, LANES), F32)
        pad[g, pl.ds(HEAD + ROWS, PADDED - HEAD - ROWS), :] = jnp.zeros(
            (PADDED - HEAD - ROWS, LANES), F32
        )


def fill_pad(pad, value):
    for g in range(3):
        pad[g, pl.ds(HEAD, ROWS), :] = value[:, g * LANES : (g + 1) * LANES]


def live_of(meta, t):
    odd = (t & 1) == 1
    count = jnp.where(t < 2, meta[2], meta[3])
    return jnp.logical_or(jnp.logical_not(odd), count == 2)


def run_forward(meta, pad, flat, wall, taps, hs, ds, skip_last):
    last = jnp.where(meta[3] == 2, 3, 2)
    fill_pad(pad, flat[...].astype(F32))

    def slot(t, carry):
        @pl.when(live_of(meta, t))
        def _():
            for g in range(3):

                def emit(p, u, g=g):
                    rows, cols = pl.ds(p * PITCH, PITCH), pl.ds(g * LANES, LANES)
                    s = 0.5 * jnp.tanh(0.5 * u) + 0.5
                    us = u * s
                    hs[t, rows, cols] = us.astype(BF)
                    ds[t, rows, cols] = s * (1.0 + (u - us))

                conv_rows(pad, taps.at[t], g, False, emit)

            def update():
                value = jnp.dot(hs[t], wall[t], preferred_element_type=F32)
                value = flat[...].astype(F32) + value
                rounded = jnp.where(keep_mask(value.shape), value, 0.0).astype(BF)
                flat[...] = rounded
                fill_pad(pad, rounded.astype(F32))

            if skip_last:
                pl.when(t != last)(update)
            else:
                update()

        return carry

    lax.fori_loop(0, 4, slot, 0)


def run_backward(meta, pad, flat, wall, taps, ds, ys, skip_first):
    def slot(i, carry):
        t = 3 - i

        @pl.when(live_of(meta, t))
        def _():
            ys[t] = flat[...]

            def chain():
                dh = lax.dot_general(
                    flat[...], wall[t], (((1,), (1,)), ((), ())), preferred_element_type=F32
                )
                fill_pad(pad, dh * ds[t])
                for g in range(3):

                    def emit(p, total, g=g):
                        rows, cols = pl.ds(p * PITCH, PITCH), pl.ds(g * LANES, LANES)
                        value = ys[t, rows, cols].astype(F32) + total
                        keep = lax.broadcasted_iota(jnp.int32, value.shape, 0) < SIDE
                        flat[rows, cols] = jnp.where(keep, value, 0.0).astype(BF)

                    conv_rows(pad, taps.at[t], g, True, emit)

            if skip_first:
                pl.when(t != 0)(chain)
            else:
                chain()

        return carry

    lax.fori_loop(0, 4, slot, 0)


def first_kernel(meta, img, packed, kown, koth, y, wall, taps, hs, ds, pad):
    core = meta[1]
    for o, kref in enumerate((kown, koth)):
        for j in range(2):
            taps[(2 * o + j + 2 * core) & 3] = kref[j].astype(F32)
    for o in range(2):
        base = (2 * o + 2 * core) & 3
        for i in range(16):
            one = packed[2 * i, pl.ds(24 * o, 24), :].astype(F32)
            two = packed[2 * i + 1, pl.ds(24 * o, 24), :].astype(F32)
            rows = pl.ds(24 * i, 24)
            wall[base, rows, :] = jnp.concatenate([one[:12], two[:12]], axis=0).astype(BF)
            wall[base + 1, rows, :] = jnp.concatenate([one[12:], two[12:]], axis=0).astype(BF)

    @pl.when(meta[0] == 0)
    def _():
        clear_pad(pad)
        y[...] = img[...]
        run_forward(meta, pad, y, wall, taps, hs, ds, False)


def forward_kernel(step, meta, cur, wall, taps, hin, din, y, hs, ds, pad):
    del hin, din

    @pl.when(meta[0] == step)
    def _():
        clear_pad(pad)
        y[...] = cur[...]
        run_forward(meta, pad, y, wall, taps, hs, ds, False)


def middle_kernel(step, meta, cur, cot, wall, taps, hin, din, y, hs, ys, ds, pad):
    del hin, din

    @pl.when(meta[0] == step)
    def _():
        clear_pad(pad)
        y[...] = cur[...]
        run_forward(meta, pad, y, wall, taps, hs, ds, True)
        y[...] = cot[...]
        run_backward(meta, pad, y, wall, taps, ds, ys, False)


def backward_kernel(step, meta, cur, wall, taps, ds, yin, y, ys, pad):
    del yin

    @pl.when(meta[0] == step)
    def _():
        clear_pad(pad)
        y[...] = cur[...]
        run_backward(meta, pad, y, wall, taps, ds, ys, False)


def last_kernel(meta, cur, wall, taps, ds, hs, yin, send, ys, flat, pad, total):
    del yin
    core = meta[1]

    @pl.when(meta[0] == 0)
    def _():
        clear_pad(pad)
        flat[...] = cur[...]
        run_backward(meta, pad, flat, wall, taps, ds, ys, True)

    def term(t):
        return lax.dot_general(
            hs[t], ys[t], (((0,), (0,)), ((), ())), preferred_element_type=F32
        )

    for o in range(2):
        base = (2 * o + 2 * core) & 3
        live = live_of(meta, base + 1)
        total[0] = term(base)

        @pl.when(live)
        def _():
            total[1] = term(base + 1)

        @pl.when(jnp.logical_not(live))
        def _():
            total[1] = jnp.zeros(total.shape[1:], F32)

        for i in range(16):
            rows = pl.ds(24 * i, 24)
            one, two = total[0, rows, :], total[1, rows, :]
            place = pl.ds(24 * o, 24)
            send[2 * i, place, :] = jnp.concatenate([one[:12], two[:12]], axis=0).astype(BF)
            send[2 * i + 1, place, :] = jnp.concatenate([one[12:], two[12:]], axis=0).astype(BF)


def weight_kernel(meta, picks, weights, own, oth, buf, wide, rows, sems):
    core = meta[1]
    copies = []
    for k, out in enumerate((own, oth)):
        for j in range(2):
            op = picks[core if k == 0 else 1 - core, j]
            group = pl.ds(pl.multiple_of((op >> 3) << 3, 8), 8)
            copies.append(
                pltpu.make_async_copy(
                    weights.at[j, :, group, :], buf.at[2 * k + j], sems.at[2 * k + j]
                )
            )
            copies[-1].start()
    for k, out in enumerate((own, oth)):
        for j in range(2):
            op = picks[core if k == 0 else 1 - core, j]
            copies[2 * k + j].wait()
            wide[...] = buf[2 * k + j].astype(F32)
            for r in range(12):
                rows[k, pl.ds(12 * j + r, 1), :] = wide[r, pl.ds(op & 7, 1), :]
        out[...] = rows[k].astype(BF)


def table_kernel(meta, picks, kernels, first, second, kown, koth, fown, foth, sown, soth,
                 kbuf, kwide, krows, mbuf, sems):
    core = meta[1]
    picked = []
    for k, (kout, fout, sout) in enumerate(((kown, fown, sown), (koth, foth, soth))):
        for j in range(2):
            op = picks[core if k == 0 else 1 - core, j]
            group = pl.ds(pl.multiple_of((op >> 3) << 3, 8), 8)
            i = 2 * k + j
            copies = [
                pltpu.make_async_copy(kernels.at[j, :, group, :], kbuf.at[i], sems.at[i]),
                pltpu.make_async_copy(first.at[j, :, group, :], mbuf.at[i], sems.at[4 + i]),
                pltpu.make_async_copy(second.at[j, :, group, :], mbuf.at[4 + i], sems.at[8 + i]),
            ]
            picked.append((copies, op & 7, kout, fout, sout, i, j))
            for c in copies:
                c.start()
    for copies, lane, kout, fout, sout, i, j in picked:
        copies[0].wait()
        kwide[...] = kbuf[i].astype(F32)
        for r in range(25):
            krows[pl.ds(r, 1), :] = kwide[r, pl.ds(lane, 1), :]
        kout[j] = krows[...].astype(BF)
        copies[1].wait()
        copies[2].wait()
        for r in range(12):
            fout[pl.ds(2 * r + j, 1), :] = mbuf[i, r, pl.ds(lane, 1), :]
            sout[pl.ds(2 * r + j, 1), :] = mbuf[4 + i, r, pl.ds(lane, 1), :]


def message_kernel(own, recv, out):
    for o, ref in enumerate((own, recv)):
        value = ref[...]
        for d in range(32):
            out[d, pl.ds(24 * o, 24), :] = value


def sum_kernel(packed, own, other, wide):
    total = packed[0].astype(F32)
    for d in range(1, 32):
        total = total + packed[d].astype(F32)
    wide[...] = total
    for o, out in enumerate((own, other)):
        for j in range(2):
            for r in range(12):
                out[pl.ds(2 * r + j, 1), :] = wide[pl.ds(24 * o + 12 * j + r, 1), :]


def adam_kernel(total_rows, meta, picks, mine, theirs, wown, woth, fown, foth, sown, soth,
                new_w, new_f, new_s, wide):
    core = meta[1]
    count = jnp.where(core == 0, meta[2], meta[3])
    odd = (lax.broadcasted_iota(jnp.int32, mine.shape, 0) & 1) == 1
    same_first = jnp.where(picks[0, 0] == picks[1, 0], 1.0, 0.0)
    same_second = jnp.where(picks[0, 1] == picks[1, 1], 1.0, 0.0)
    same = jnp.where(odd, same_second, same_first) > 0.5
    live = jnp.where(odd, count, 2) == 2
    for k, (wref, fref, sref) in enumerate(((wown, fown, sown), (woth, foth, soth))):
        n = core if k == 0 else 1 - core
        grad, rest = (mine[...], theirs[...]) if k == 0 else (theirs[...], mine[...])
        grad = (grad + jnp.where(same, rest, jnp.zeros_like(rest))) / total_rows
        source = wref[...].astype(F32)
        for j in range(2):
            for r in range(12):
                wide[pl.ds(2 * r + j, 1), :] = source[12 * j + r : 12 * j + r + 1, :]
        weight, one, two = wide[...], fref[...], sref[...]
        next_one = first_decay * one + (1.0 - first_decay) * grad
        next_two = second_decay * two + (1.0 - second_decay) * grad * grad
        next_weight = weight - learn_rate * (next_one / first_bias) / (
            jnp.sqrt(next_two / second_bias) + adam_epsilon
        )
        out_w = jnp.where(live, next_weight, weight)
        out_f = jnp.where(live, next_one, one)
        out_s = jnp.where(live, next_two, two)
        for r in range(12):
            new_w[n, r] = out_w[2 * r : 2 * r + 2].astype(BF)
            new_f[n, r] = out_f[2 * r : 2 * r + 2]
            new_s[n, r] = out_s[2 * r : 2 * r + 2]


def body(images, cotangent, picks, section_sizes, kernels, weights, first_moment, second_moment):
    width = images.shape[-1]
    own_segment = lax.axis_index("segment")
    segments = lax.axis_size("segment")
    parts = lax.axis_size("dp")
    total_rows = images.shape[0] * images.shape[1] * images.shape[2] * parts
    swap = [(s, s ^ 1) for s in range(segments)]
    ahead = [(s, (s + 2) % segments) for s in range(segments)]
    behind = [(s, (s - 2) % segments) for s in range(segments)]

    DMA = pltpu.SemaphoreType.DMA
    V = pltpu.VMEM
    state = (4, ROWS, width)
    flat_shape = (ROWS, width)
    s_pad = V((3, PADDED, LANES), F32)
    pair, square, tap_shape = (24, width), (4, width, width), (4, 25, width)

    core = own_segment & 1
    place = lax.broadcasted_iota(jnp.int32, (4,), 0)
    early = jnp.where(place == 0, own_segment >> 1, core)
    sizes_other = lax.ppermute(section_sizes, "segment", swap)

    wown, woth = call(
        weight_kernel,
        [(pair, BF), (pair, BF)],
        [SMEM, SMEM, ANY],
        [V((4, 12, 8, width), BF), V((12, 8, width), F32), V((2, 24, width), F32), DMA((4,))],
        cost=1000,
    )(early, picks, weights.transpose(0, 2, 1, 3))
    wrecv = lax.ppermute(woth, "segment", swap)
    (message,) = call(message_kernel, [((32, 48, width), BF)], [VMEM, VMEM], [], cost=1000)(
        wown, wrecv
    )
    packed = lax.all_to_all(message, "dp", 0, 0)
    kown, kother, fown, foth, sown, soth = call(
        table_kernel,
        [((2, 25, width), BF)] * 2 + [(pair, F32)] * 4,
        [SMEM, SMEM, ANY, ANY, ANY],
        [V((4, 25, 8, width), BF), V((25, 8, width), F32), V((25, width), F32),
         V((8, 12, 8, width), F32), DMA((12,))],
    )(
        early,
        picks,
        kernels.transpose(0, 2, 1, 3),
        first_moment.transpose(0, 2, 1, 3),
        second_moment.transpose(0, 2, 1, 3),
    )
    koth = lax.ppermute(kother, "segment", swap)
    size_low = jnp.where(core == 0, section_sizes[0], sizes_other[0])
    size_high = jnp.where(core == 0, sizes_other[0], section_sizes[0])
    meta = jnp.where(place < 2, early, jnp.where(place == 2, size_low, size_high))
    edges = ((0, 0), (0, PITCH - SIDE), (0, 0))
    img = jnp.pad(images[0], edges).reshape(flat_shape)
    chosen = lax.dynamic_index_in_dim(cotangent[:, 0], core, 0, keepdims=False)
    cot = jnp.pad(chosen, edges).reshape(flat_shape)

    y, wall, taps, hs, ds = call(
        first_kernel,
        [(flat_shape, BF), (square, BF), (tap_shape, F32), (state, BF), (state, F32)],
        [SMEM] + [VMEM] * 4,
        [s_pad],
    )(meta, img, packed, kown, koth)
    cur = lax.ppermute(y, "segment", ahead)
    for step in (1, 2):
        y, hs, ds = call(
            functools.partial(forward_kernel, step),
            [(flat_shape, BF), (state, BF), (state, F32)],
            [SMEM] + [VMEM] * 5,
            [s_pad],
            {4: 1, 5: 2},
        )(meta, cur, wall, taps, hs, ds)
        cur = lax.ppermute(y, "segment", ahead)
    y, hs, ys, ds = call(
        functools.partial(middle_kernel, 3),
        [(flat_shape, BF), (state, BF), (state, BF), (state, F32)],
        [SMEM] + [VMEM] * 6,
        [s_pad],
        {5: 1, 6: 3},
    )(meta, cur, cot, wall, taps, hs, ds)
    cur = lax.ppermute(y, "segment", behind)
    for step in (2, 1):
        y, ys = call(
            functools.partial(backward_kernel, step),
            [(flat_shape, BF), (state, BF)],
            [SMEM] + [VMEM] * 5,
            [s_pad],
            {5: 1},
        )(meta, cur, wall, taps, ds, ys)
        cur = lax.ppermute(y, "segment", behind)
    send, _ = call(
        last_kernel,
        [((32, 48, width), BF), (state, BF)],
        [SMEM] + [VMEM] * 6,
        [V(flat_shape, BF), s_pad, V((2, width, width), F32)],
        {6: 1},
    )(meta, cur, wall, taps, ds, hs, ys)
    landed = lax.all_to_all(send, "dp", 0, 0)
    own, for_other = call(
        sum_kernel, [(pair, F32), (pair, F32)], [VMEM], [V((48, width), F32)]
    )(landed)
    other = lax.ppermute(for_other, "segment", swap)
    rows = (2, 12, 2, width)
    news = call(
        functools.partial(adam_kernel, float(total_rows)),
        [(rows, BF), (rows, F32), (rows, F32)],
        [SMEM, SMEM] + [VMEM] * 8,
        [V(pair, F32)],
    )(meta, picks, own, other, wown, woth, fown, foth, sown, soth)
    return tuple(new.transpose(0, 2, 1, 3) for new in news)


def solution(mesh):
    return jax.shard_map(
        body,
        mesh=mesh,
        in_specs=(
            P("dp", None, None, None),
            P(None, "dp", None, None, None),
            P(None, "segment"),
            P("segment"),
            P("segment", None, None, None),
            P("segment", None, "dp", None),
            P("segment", None, "dp", None),
            P("segment", None, "dp", None),
        ),
        out_specs=(
            P(None, "segment", "dp", None),
            P(None, "segment", "dp", None),
            P(None, "segment", "dp", None),
        ),
        check_vma=False,
    )
```

```python
import functools

import jax
import jax.numpy as jnp
from jax import lax
from jax.experimental import pallas as pl
from jax.experimental.pallas import tpu as pltpu
from jax.sharding import PartitionSpec as P

first_decay = 0.9
second_decay = 0.999
learn_rate = 0.01
adam_epsilon = 1e-08
first_bias = 1.0 - 0.9**10
second_bias = 1.0 - 0.999**10

SIDE = 14
PITCH = 16
ROWS = SIDE * PITCH
LANES = 128
HEAD = 8 + 2 * PITCH
PADDED = 8 + (SIDE + 4) * PITCH + 8
BF = jnp.bfloat16
F32 = jnp.float32

HBM = pl.BlockSpec(memory_space=pltpu.HBM)
SMEM = pl.BlockSpec(memory_space=pltpu.SMEM)
PARAMS = pltpu.CompilerParams(vmem_limit_bytes=8 << 20)


VMEM = pl.BlockSpec(memory_space=pltpu.VMEM)


def call(kernel, outs, in_specs, scratch, aliases=None, cost=2_000_000_000):
    return pl.pallas_call(
        kernel,
        out_shape=[jax.ShapeDtypeStruct(s, d) for s, d in outs],
        in_specs=in_specs,
        out_specs=[VMEM] * len(outs),
        scratch_shapes=scratch,
        input_output_aliases=aliases or {},
        compiler_params=PARAMS,
        cost_estimate=pl.CostEstimate(flops=cost, bytes_accessed=1_000_000, transcendentals=0),
    )


def keep_mask(shape):
    return (lax.broadcasted_iota(jnp.int32, shape, 0) & (PITCH - 1)) < SIDE


def conv_rows(pad, taps, group, flipped, emit):
    sign = -1 if flipped else 1
    cols = pl.ds(group * LANES, LANES)
    weights = [jnp.broadcast_to(taps[pl.ds(i, 1), cols], (PITCH, LANES)) for i in range(25)]
    for p in range(0, SIDE, 2):
        totals = [None, None]
        for da in range(-2, 4):
            for e in range(-2, 3):
                start = HEAD + PITCH * (p + da) + e
                window = pad[group, pl.ds(start, PITCH), :]
                for k in range(2):
                    a = da - k
                    if -2 <= a <= 2:
                        tap = (sign * a + 2) * 5 + (sign * e + 2)
                        term = weights[tap] * window
                        totals[k] = term if totals[k] is None else totals[k] + term
        emit(p, totals[0])
        emit(p + 1, totals[1])


def clear_pad(pad):
    for g in range(3):
        pad[g, pl.ds(0, HEAD), :] = jnp.zeros((HEAD, LANES), F32)
        pad[g, pl.ds(HEAD + ROWS, PADDED - HEAD - ROWS), :] = jnp.zeros(
            (PADDED - HEAD - ROWS, LANES), F32
        )


def fill_pad(pad, value):
    for g in range(3):
        pad[g, pl.ds(HEAD, ROWS), :] = value[:, g * LANES : (g + 1) * LANES]


def live_of(meta, t):
    odd = (t & 1) == 1
    count = jnp.where(t < 2, meta[2], meta[3])
    return jnp.logical_or(jnp.logical_not(odd), count == 2)


def run_forward(meta, pad, flat, wall, taps, hs, ds, skip_last):
    last = jnp.where(meta[3] == 2, 3, 2)
    fill_pad(pad, flat[...].astype(F32))

    def slot(t, carry):
        @pl.when(live_of(meta, t))
        def _():
            for g in range(3):

                def emit(p, u, g=g):
                    rows, cols = pl.ds(p * PITCH, PITCH), pl.ds(g * LANES, LANES)
                    s = 0.5 * jnp.tanh(0.5 * u) + 0.5
                    us = u * s
                    hs[t, rows, cols] = us.astype(BF)
                    ds[t, rows, cols] = s * (1.0 + (u - us))

                conv_rows(pad, taps.at[t], g, False, emit)

            def update():
                value = jnp.dot(hs[t], wall[t], preferred_element_type=F32)
                value = flat[...].astype(F32) + value
                rounded = jnp.where(keep_mask(value.shape), value, 0.0).astype(BF)
                flat[...] = rounded
                fill_pad(pad, rounded.astype(F32))

            if skip_last:
                pl.when(t != last)(update)
            else:
                update()

        return carry

    lax.fori_loop(0, 4, slot, 0)


def run_backward(meta, pad, flat, wall, taps, ds, ys, skip_first):
    def slot(i, carry):
        t = 3 - i

        @pl.when(live_of(meta, t))
        def _():
            ys[t] = flat[...]

            def chain():
                dh = lax.dot_general(
                    flat[...], wall[t], (((1,), (1,)), ((), ())), preferred_element_type=F32
                )
                fill_pad(pad, dh * ds[t])
                for g in range(3):

                    def emit(p, total, g=g):
                        rows, cols = pl.ds(p * PITCH, PITCH), pl.ds(g * LANES, LANES)
                        value = ys[t, rows, cols].astype(F32) + total
                        keep = lax.broadcasted_iota(jnp.int32, value.shape, 0) < SIDE
                        flat[rows, cols] = jnp.where(keep, value, 0.0).astype(BF)

                    conv_rows(pad, taps.at[t], g, True, emit)

            if skip_first:
                pl.when(t != 0)(chain)
            else:
                chain()

        return carry

    lax.fori_loop(0, 4, slot, 0)


def first_kernel(meta, img, near, ahead1, ahead2, ahead3, kown, koth, y, wall, taps, hs, ds, pad, packed):
    core, z, yy = meta[1], meta[4], meta[5]
    for shift, ref in enumerate((near, ahead1, ahead2, ahead3)):
        packed[(yy - shift) & 3] = ref[...]
    for o, kref in enumerate((kown, koth)):
        for j in range(2):
            taps[(2 * o + j + 2 * core) & 3] = kref[j].astype(F32)
    for o in range(2):
        base = (2 * o + 2 * core) & 3
        place = pl.ds(24 * o, 24)
        for i in range(16):
            shift = (z - i // 2) & 7
            one = packed[2 * (i % 2), shift, place, :].astype(F32)
            two = packed[2 * (i % 2) + 1, shift, place, :].astype(F32)
            rows = pl.ds(24 * i, 24)
            wall[base, rows, :] = jnp.concatenate([one[:12], two[:12]], axis=0).astype(BF)
            wall[base + 1, rows, :] = jnp.concatenate([one[12:], two[12:]], axis=0).astype(BF)

    @pl.when(meta[0] == 0)
    def _():
        clear_pad(pad)
        y[...] = img[...]
        run_forward(meta, pad, y, wall, taps, hs, ds, False)


def forward_kernel(step, meta, cur, wall, taps, hin, din, y, hs, ds, pad):
    del hin, din

    @pl.when(meta[0] == step)
    def _():
        clear_pad(pad)
        y[...] = cur[...]
        run_forward(meta, pad, y, wall, taps, hs, ds, False)


def middle_kernel(step, meta, cur, cot, wall, taps, hin, din, y, hs, ys, ds, pad):
    del hin, din

    @pl.when(meta[0] == step)
    def _():
        clear_pad(pad)
        y[...] = cur[...]
        run_forward(meta, pad, y, wall, taps, hs, ds, True)
        y[...] = cot[...]
        run_backward(meta, pad, y, wall, taps, ds, ys, False)


def backward_kernel(step, meta, cur, wall, taps, ds, yin, y, ys, pad):
    del yin

    @pl.when(meta[0] == step)
    def _():
        clear_pad(pad)
        y[...] = cur[...]
        run_backward(meta, pad, y, wall, taps, ds, ys, False)


def last_kernel(meta, cur, wall, taps, ds, hs, yin, near, ahead1, ahead2, ahead3, ys,
                flat, pad, total, send):
    del yin
    core, z, yy = meta[1], meta[4], meta[5]

    @pl.when(meta[0] == 0)
    def _():
        clear_pad(pad)
        flat[...] = cur[...]
        run_backward(meta, pad, flat, wall, taps, ds, ys, True)

    def term(t):
        return lax.dot_general(
            hs[t], ys[t], (((0,), (0,)), ((), ())), preferred_element_type=F32
        )

    for o in range(2):
        base = (2 * o + 2 * core) & 3
        live = live_of(meta, base + 1)
        total[0] = term(base)

        @pl.when(live)
        def _():
            total[1] = term(base + 1)

        @pl.when(jnp.logical_not(live))
        def _():
            total[1] = jnp.zeros(total.shape[1:], F32)

        for i in range(16):
            rows = pl.ds(24 * i, 24)
            one, two = total[0, rows, :], total[1, rows, :]
            place = pl.ds(24 * o, 24)
            shift = (i // 2 - z) & 7
            send[2 * (i % 2), shift, place, :] = jnp.concatenate(
                [one[:12], two[:12]], axis=0
            ).astype(BF)
            send[2 * (i % 2) + 1, shift, place, :] = jnp.concatenate(
                [one[12:], two[12:]], axis=0
            ).astype(BF)
    for shift, ref in enumerate((near, ahead1, ahead2, ahead3)):
        ref[...] = send[(yy + shift) & 3]


def weight_kernel(meta, picks, weights, own, oth, buf, wide, rows, sems):
    core = meta[1]
    copies = []
    for k, out in enumerate((own, oth)):
        for j in range(2):
            op = picks[core if k == 0 else 1 - core, j]
            group = pl.ds(pl.multiple_of((op >> 3) << 3, 8), 8)
            copies.append(
                pltpu.make_async_copy(
                    weights.at[j, :, group, :], buf.at[2 * k + j], sems.at[2 * k + j]
                )
            )
            copies[-1].start()
    for k, out in enumerate((own, oth)):
        for j in range(2):
            op = picks[core if k == 0 else 1 - core, j]
            copies[2 * k + j].wait()
            wide[...] = buf[2 * k + j].astype(F32)
            for r in range(12):
                rows[k, pl.ds(12 * j + r, 1), :] = wide[r, pl.ds(op & 7, 1), :]
        out[...] = rows[k].astype(BF)


def table_kernel(meta, picks, kernels, first, second, kown, koth, fown, foth, sown, soth,
                 kbuf, kwide, krows, mbuf, sems):
    core = meta[1]
    picked = []
    for k, (kout, fout, sout) in enumerate(((kown, fown, sown), (koth, foth, soth))):
        for j in range(2):
            op = picks[core if k == 0 else 1 - core, j]
            group = pl.ds(pl.multiple_of((op >> 3) << 3, 8), 8)
            i = 2 * k + j
            copies = [
                pltpu.make_async_copy(kernels.at[j, :, group, :], kbuf.at[i], sems.at[i]),
                pltpu.make_async_copy(first.at[j, :, group, :], mbuf.at[i], sems.at[4 + i]),
                pltpu.make_async_copy(second.at[j, :, group, :], mbuf.at[4 + i], sems.at[8 + i]),
            ]
            picked.append((copies, op & 7, kout, fout, sout, i, j))
            for c in copies:
                c.start()
    for copies, lane, kout, fout, sout, i, j in picked:
        copies[0].wait()
        kwide[...] = kbuf[i].astype(F32)
        for r in range(25):
            krows[pl.ds(r, 1), :] = kwide[r, pl.ds(lane, 1), :]
        kout[j] = krows[...].astype(BF)
        copies[1].wait()
        copies[2].wait()
        for r in range(12):
            fout[pl.ds(2 * r + j, 1), :] = mbuf[i, r, pl.ds(lane, 1), :]
            sout[pl.ds(2 * r + j, 1), :] = mbuf[4 + i, r, pl.ds(lane, 1), :]


def stack_kernel(*refs):
    out = refs[-1]
    for i, ref in enumerate(refs[:-1]):
        out[i] = ref[...]


def join_kernel(own, recv, out):
    out[pl.ds(0, 24), :] = own[...]
    out[pl.ds(24, 24), :] = recv[...]


def near_sum_kernel(a, b, c, d, own, *outs):
    for i in range(8):
        total = (a[i].astype(F32) + b[i].astype(F32)) + (c[i].astype(F32) + d[i].astype(F32))
        if i == 0:
            own[...] = total
        else:
            outs[i - 1][...] = total.astype(BF)


def sum_kernel(near, *refs):
    own, other, wide = refs[-3:]
    total = near[...]
    for ref in refs[:-3]:
        total = total + ref[...].astype(F32)
    wide[...] = total
    for o, out in enumerate((own, other)):
        for j in range(2):
            for r in range(12):
                out[pl.ds(2 * r + j, 1), :] = wide[pl.ds(24 * o + 12 * j + r, 1), :]


def adam_kernel(total_rows, meta, picks, mine, theirs, wown, woth, fown, foth, sown, soth,
                new_w, new_f, new_s, wide):
    core = meta[1]
    count = jnp.where(core == 0, meta[2], meta[3])
    odd = (lax.broadcasted_iota(jnp.int32, mine.shape, 0) & 1) == 1
    same_first = jnp.where(picks[0, 0] == picks[1, 0], 1.0, 0.0)
    same_second = jnp.where(picks[0, 1] == picks[1, 1], 1.0, 0.0)
    same = jnp.where(odd, same_second, same_first) > 0.5
    live = jnp.where(odd, count, 2) == 2
    for k, (wref, fref, sref) in enumerate(((wown, fown, sown), (woth, foth, soth))):
        n = core if k == 0 else 1 - core
        grad, rest = (mine[...], theirs[...]) if k == 0 else (theirs[...], mine[...])
        grad = (grad + jnp.where(same, rest, jnp.zeros_like(rest))) / total_rows
        source = wref[...].astype(F32)
        for j in range(2):
            for r in range(12):
                wide[pl.ds(2 * r + j, 1), :] = source[12 * j + r : 12 * j + r + 1, :]
        weight, one, two = wide[...], fref[...], sref[...]
        next_one = first_decay * one + (1.0 - first_decay) * grad
        next_two = second_decay * two + (1.0 - second_decay) * grad * grad
        next_weight = weight - learn_rate * (next_one / first_bias) / (
            jnp.sqrt(next_two / second_bias) + adam_epsilon
        )
        out_w = jnp.where(live, next_weight, weight)
        out_f = jnp.where(live, next_one, one)
        out_s = jnp.where(live, next_two, two)
        for r in range(12):
            new_w[n, r] = out_w[2 * r : 2 * r + 2].astype(BF)
            new_f[n, r] = out_f[2 * r : 2 * r + 2]
            new_s[n, r] = out_s[2 * r : 2 * r + 2]


def body(images, cotangent, picks, section_sizes, kernels, weights, first_moment, second_moment):
    width = images.shape[-1]
    own_segment = lax.axis_index("segment")
    segments = lax.axis_size("segment")
    parts = lax.axis_size("dp")
    total_rows = images.shape[0] * images.shape[1] * images.shape[2] * parts
    swap = [(s, s ^ 1) for s in range(segments)]
    ahead = [(s, (s + 2) % segments) for s in range(segments)]
    behind = [(s, (s - 2) % segments) for s in range(segments)]

    def along(value, dz, dy):
        pairs = [
            (4 * z + y, 4 * ((z + dz) % 8) + (y + dy) % 4) for z in range(8) for y in range(4)
        ]
        return lax.ppermute(value, "dp", pairs)

    far = (4, 3, 5, 2, 6, 1, 7)

    DMA = pltpu.SemaphoreType.DMA
    V = pltpu.VMEM
    state = (4, ROWS, width)
    flat_shape = (ROWS, width)
    s_pad = V((3, PADDED, LANES), F32)
    pair, square, tap_shape = (24, width), (4, width, width), (4, 25, width)

    core = own_segment & 1
    part = lax.axis_index("dp")
    place = lax.broadcasted_iota(jnp.int32, (6,), 0)
    early = lax.optimization_barrier(
        jnp.where(
            place == 0,
            own_segment >> 1,
            jnp.where(place == 4, part >> 2, jnp.where(place == 5, part & 3, core)),
        )
    )
    sizes_other = lax.ppermute(section_sizes, "segment", swap)

    wown, woth = call(
        weight_kernel,
        [(pair, BF), (pair, BF)],
        [SMEM, SMEM, HBM],
        [V((4, 12, 8, width), BF), V((12, 8, width), F32), V((2, 24, width), F32), DMA((4,))],
        cost=1000,
    )(early, picks, weights.transpose(0, 2, 1, 3))
    wrecv = lax.ppermute(woth, "segment", swap)
    (message,) = call(join_kernel, [((48, width), BF)], [VMEM, VMEM], [], cost=1000)(wown, wrecv)
    pieces = {0: message}
    for dz in far:
        pieces[dz] = along(message, dz, 0)
    (near,) = call(stack_kernel, [((8, 48, width), BF)], [VMEM] * 8, [], cost=1000)(
        *[pieces[i] for i in range(8)]
    )
    columns = {0: near}
    for dy in (2, 1, 3):
        columns[dy] = along(near, 0, dy)
    kown, kother, fown, foth, sown, soth = call(
        table_kernel,
        [((2, 25, width), BF)] * 2 + [(pair, F32)] * 4,
        [SMEM, SMEM, HBM, HBM, HBM],
        [V((4, 25, 8, width), BF), V((25, 8, width), F32), V((25, width), F32),
         V((8, 12, 8, width), F32), DMA((12,))],
    )(
        early,
        picks,
        kernels.transpose(0, 2, 1, 3),
        first_moment.transpose(0, 2, 1, 3),
        second_moment.transpose(0, 2, 1, 3),
    )
    koth = lax.ppermute(kother, "segment", swap)
    size_low = jnp.where(core == 0, section_sizes[0], sizes_other[0])
    size_high = jnp.where(core == 0, sizes_other[0], section_sizes[0])
    meta = jnp.where(place == 2, size_low, jnp.where(place == 3, size_high, early))
    edges = ((0, 0), (0, PITCH - SIDE), (0, 0))
    img = jnp.pad(images[0], edges).reshape(flat_shape)
    chosen = lax.dynamic_index_in_dim(cotangent[:, 0], core, 0, keepdims=False)
    cot = jnp.pad(chosen, edges).reshape(flat_shape)
    img, cot, koth = lax.optimization_barrier((img, cot, koth))

    y, wall, taps, hs, ds = call(
        first_kernel,
        [(flat_shape, BF), (square, BF), (tap_shape, F32), (state, BF), (state, F32)],
        [SMEM] + [VMEM] * 7,
        [s_pad, V((4, 8, 48, width), BF)],
    )(meta, img, *[columns[i] for i in range(4)], kown, koth)
    cur = lax.ppermute(y, "segment", ahead)
    for step in (1, 2):
        y, hs, ds = call(
            functools.partial(forward_kernel, step),
            [(flat_shape, BF), (state, BF), (state, F32)],
            [SMEM] + [VMEM] * 5,
            [s_pad],
            {4: 1, 5: 2},
        )(meta, cur, wall, taps, hs, ds)
        cur = lax.ppermute(y, "segment", ahead)
    y, hs, ys, ds = call(
        functools.partial(middle_kernel, 3),
        [(flat_shape, BF), (state, BF), (state, BF), (state, F32)],
        [SMEM] + [VMEM] * 6,
        [s_pad],
        {5: 1, 6: 3},
    )(meta, cur, cot, wall, taps, hs, ds)
    cur = lax.ppermute(y, "segment", behind)
    for step in (2, 1):
        y, ys = call(
            functools.partial(backward_kernel, step),
            [(flat_shape, BF), (state, BF)],
            [SMEM] + [VMEM] * 5,
            [s_pad],
            {5: 1},
        )(meta, cur, wall, taps, ds, ys)
        cur = lax.ppermute(y, "segment", behind)
    column = (8, 48, width)
    *sends, _ = call(
        last_kernel,
        [(column, BF)] * 4 + [(state, BF)],
        [SMEM] + [VMEM] * 6,
        [V(flat_shape, BF), s_pad, V((2, width, width), F32), V((4, 8, 48, width), BF)],
        {6: 4},
    )(meta, cur, wall, taps, ds, hs, ys)
    came = [along(sends[dy], 0, dy) for dy in (2, 1, 3)]
    near_own, *partial = call(
        near_sum_kernel,
        [((48, width), F32)] + [((48, width), BF)] * 7,
        [VMEM] * 4,
        [],
        cost=1000,
    )(sends[0], *came)
    landed = [along(partial[dz - 1], dz, 0) for dz in far]
    own, for_other = call(
        sum_kernel, [(pair, F32), (pair, F32)], [VMEM] * 8, [V((48, width), F32)], cost=1000
    )(near_own, *landed)
    other = lax.ppermute(for_other, "segment", swap)
    rows = (2, 12, 2, width)
    news = call(
        functools.partial(adam_kernel, float(total_rows)),
        [(rows, BF), (rows, F32), (rows, F32)],
        [SMEM, SMEM] + [VMEM] * 8,
        [V(pair, F32)],
    )(meta, picks, own, other, wown, woth, fown, foth, sown, soth)
    return tuple(new.transpose(0, 2, 1, 3) for new in news)


def solution(mesh):
    return jax.shard_map(
        body,
        mesh=mesh,
        in_specs=(
            P("dp", None, None, None),
            P(None, "dp", None, None, None),
            P(None, "segment"),
            P("segment"),
            P("segment", None, None, None),
            P("segment", None, "dp", None),
            P("segment", None, "dp", None),
            P("segment", None, "dp", None),
        ),
        out_specs=(
            P(None, "segment", "dp", None),
            P(None, "segment", "dp", None),
            P(None, "segment", "dp", None),
        ),
        check_vma=False,
    )
```

```python
import functools

import jax
import jax.numpy as jnp
from jax import lax
from jax.experimental import pallas as pl
from jax.experimental.pallas import tpu as pltpu
from jax.sharding import PartitionSpec as P

first_decay = 0.9
second_decay = 0.999
learn_rate = 0.01
adam_epsilon = 1e-08
first_bias = 1.0 - 0.9**10
second_bias = 1.0 - 0.999**10

SIDE = 14
PITCH = 16
ROWS = SIDE * PITCH
LANES = 128
HEAD = 8 + 2 * PITCH
PADDED = 8 + (SIDE + 4) * PITCH + 8
BF = jnp.bfloat16
F32 = jnp.float32

HBM = pl.BlockSpec(memory_space=pltpu.HBM)
SMEM = pl.BlockSpec(memory_space=pltpu.SMEM)
PARAMS = pltpu.CompilerParams(vmem_limit_bytes=8 << 20)


VMEM = pl.BlockSpec(memory_space=pltpu.VMEM)


def call(kernel, outs, in_specs, scratch, aliases=None, cost=2_000_000_000):
    return pl.pallas_call(
        kernel,
        out_shape=[jax.ShapeDtypeStruct(s, d) for s, d in outs],
        in_specs=in_specs,
        out_specs=[VMEM] * len(outs),
        scratch_shapes=scratch,
        input_output_aliases=aliases or {},
        compiler_params=PARAMS,
        cost_estimate=pl.CostEstimate(flops=cost, bytes_accessed=1_000_000, transcendentals=0),
    )


def keep_mask(shape):
    return (lax.broadcasted_iota(jnp.int32, shape, 0) & (PITCH - 1)) < SIDE


def conv_rows(pad, taps, group, flipped, emit):
    sign = -1 if flipped else 1
    cols = pl.ds(group * LANES, LANES)
    weights = [jnp.broadcast_to(taps[pl.ds(i, 1), cols], (PITCH, LANES)) for i in range(25)]
    for p in range(0, SIDE, 2):
        totals = [None, None]
        for da in range(-2, 4):
            for e in range(-2, 3):
                start = HEAD + PITCH * (p + da) + e
                window = pad[group, pl.ds(start, PITCH), :]
                for k in range(2):
                    a = da - k
                    if -2 <= a <= 2:
                        tap = (sign * a + 2) * 5 + (sign * e + 2)
                        term = weights[tap] * window
                        totals[k] = term if totals[k] is None else totals[k] + term
        emit(p, totals[0])
        emit(p + 1, totals[1])


def clear_pad(pad):
    for g in range(3):
        pad[g, pl.ds(0, HEAD), :] = jnp.zeros((HEAD, LANES), F32)
        pad[g, pl.ds(HEAD + ROWS, PADDED - HEAD - ROWS), :] = jnp.zeros(
            (PADDED - HEAD - ROWS, LANES), F32
        )


def fill_pad(pad, value):
    for g in range(3):
        pad[g, pl.ds(HEAD, ROWS), :] = value[:, g * LANES : (g + 1) * LANES]


def live_of(meta, t):
    odd = (t & 1) == 1
    count = jnp.where(t < 2, meta[2], meta[3])
    return jnp.logical_or(jnp.logical_not(odd), count == 2)


def run_forward(meta, pad, flat, wall, taps, hs, ds, skip_last):
    last = jnp.where(meta[3] == 2, 3, 2)
    fill_pad(pad, flat[...].astype(F32))

    def slot(t, carry):
        @pl.when(live_of(meta, t))
        def _():
            for g in range(3):

                def emit(p, u, g=g):
                    rows, cols = pl.ds(p * PITCH, PITCH), pl.ds(g * LANES, LANES)
                    s = 0.5 * jnp.tanh(0.5 * u) + 0.5
                    us = u * s
                    hs[t, rows, cols] = us.astype(BF)
                    ds[t, rows, cols] = s * (1.0 + (u - us))

                conv_rows(pad, taps.at[t], g, False, emit)

            def update():
                value = jnp.dot(hs[t], wall[t], preferred_element_type=F32)
                value = flat[...].astype(F32) + value
                rounded = jnp.where(keep_mask(value.shape), value, 0.0).astype(BF)
                flat[...] = rounded
                fill_pad(pad, rounded.astype(F32))

            if skip_last:
                pl.when(t != last)(update)
            else:
                update()

        return carry

    lax.fori_loop(0, 4, slot, 0)


def run_backward(meta, pad, flat, wall, taps, ds, ys, skip_first):
    def slot(i, carry):
        t = 3 - i

        @pl.when(live_of(meta, t))
        def _():
            ys[t] = flat[...]

            def chain():
                dh = lax.dot_general(
                    flat[...], wall[t], (((1,), (1,)), ((), ())), preferred_element_type=F32
                )
                fill_pad(pad, dh * ds[t])
                for g in range(3):

                    def emit(p, total, g=g):
                        rows, cols = pl.ds(p * PITCH, PITCH), pl.ds(g * LANES, LANES)
                        value = ys[t, rows, cols].astype(F32) + total
                        keep = lax.broadcasted_iota(jnp.int32, value.shape, 0) < SIDE
                        flat[rows, cols] = jnp.where(keep, value, 0.0).astype(BF)

                    conv_rows(pad, taps.at[t], g, True, emit)

            if skip_first:
                pl.when(t != 0)(chain)
            else:
                chain()

        return carry

    lax.fori_loop(0, 4, slot, 0)


def first_kernel(meta, img, near, ahead1, ahead2, ahead3, kown, koth, y, wall, taps, hs, ds, pad, packed):
    core, z, yy = meta[1], meta[4], meta[5]
    for shift, ref in enumerate((near, ahead1, ahead2, ahead3)):
        packed[(yy - shift) & 3] = ref[...]
    for o, kref in enumerate((kown, koth)):
        for j in range(2):
            taps[(2 * o + j + 2 * core) & 3] = kref[j].astype(F32)
    for o in range(2):
        base = (2 * o + 2 * core) & 3
        place = pl.ds(24 * o, 24)
        for i in range(16):
            shift = (z - i // 2) & 7
            one = packed[2 * (i % 2), shift, place, :].astype(F32)
            two = packed[2 * (i % 2) + 1, shift, place, :].astype(F32)
            rows = pl.ds(24 * i, 24)
            wall[base, rows, :] = jnp.concatenate([one[:12], two[:12]], axis=0).astype(BF)
            wall[base + 1, rows, :] = jnp.concatenate([one[12:], two[12:]], axis=0).astype(BF)

    @pl.when(meta[0] == 0)
    def _():
        clear_pad(pad)
        y[...] = img[...]
        run_forward(meta, pad, y, wall, taps, hs, ds, False)


def forward_kernel(step, meta, cur, wall, taps, hin, din, y, hs, ds, pad):
    del hin, din

    @pl.when(meta[0] == step)
    def _():
        clear_pad(pad)
        y[...] = cur[...]
        run_forward(meta, pad, y, wall, taps, hs, ds, False)


def middle_kernel(step, meta, cur, cot, wall, taps, hin, din, y, hs, ys, ds, pad):
    del hin, din

    @pl.when(meta[0] == step)
    def _():
        clear_pad(pad)
        y[...] = cur[...]
        run_forward(meta, pad, y, wall, taps, hs, ds, True)
        y[...] = cot[...]
        run_backward(meta, pad, y, wall, taps, ds, ys, False)


def backward_kernel(step, meta, cur, wall, taps, ds, yin, y, ys, pad):
    del yin

    @pl.when(meta[0] == step)
    def _():
        clear_pad(pad)
        y[...] = cur[...]
        run_backward(meta, pad, y, wall, taps, ds, ys, False)


def last_kernel(meta, cur, wall, taps, ds, hs, yin, near, ahead1, ahead2, ahead3, ys,
                flat, pad, total, send):
    del yin
    core, z, yy = meta[1], meta[4], meta[5]

    @pl.when(meta[0] == 0)
    def _():
        clear_pad(pad)
        flat[...] = cur[...]
        run_backward(meta, pad, flat, wall, taps, ds, ys, True)

    def term(t):
        return lax.dot_general(
            hs[t], ys[t], (((0,), (0,)), ((), ())), preferred_element_type=F32
        )

    for o in range(2):
        base = (2 * o + 2 * core) & 3
        live = live_of(meta, base + 1)
        total[0] = term(base)

        @pl.when(live)
        def _():
            total[1] = term(base + 1)

        @pl.when(jnp.logical_not(live))
        def _():
            total[1] = jnp.zeros(total.shape[1:], F32)

        for i in range(16):
            rows = pl.ds(24 * i, 24)
            one, two = total[0, rows, :], total[1, rows, :]
            place = pl.ds(24 * o, 24)
            shift = (i // 2 - z) & 7
            send[2 * (i % 2), shift, place, :] = jnp.concatenate(
                [one[:12], two[:12]], axis=0
            ).astype(BF)
            send[2 * (i % 2) + 1, shift, place, :] = jnp.concatenate(
                [one[12:], two[12:]], axis=0
            ).astype(BF)
    for shift, ref in enumerate((near, ahead1, ahead2, ahead3)):
        ref[...] = send[(yy + shift) & 3]


def picked(meta, n, j):
    return meta[6 + 2 * n + j]


def weight_kernel(meta, weights, own, oth, buf, wide, rows, sems):
    core = meta[1]
    copies = []
    for k, out in enumerate((own, oth)):
        for j in range(2):
            op = picked(meta, core if k == 0 else 1 - core, j)
            group = pl.ds(pl.multiple_of((op >> 3) << 3, 8), 8)
            copies.append(
                pltpu.make_async_copy(
                    weights.at[j, :, group, :], buf.at[2 * k + j], sems.at[2 * k + j]
                )
            )
            copies[-1].start()
    for k, out in enumerate((own, oth)):
        for j in range(2):
            op = picked(meta, core if k == 0 else 1 - core, j)
            copies[2 * k + j].wait()
            wide[...] = buf[2 * k + j].astype(F32)
            for r in range(12):
                rows[k, pl.ds(12 * j + r, 1), :] = wide[r, pl.ds(op & 7, 1), :]
        out[...] = rows[k].astype(BF)


def table_kernel(meta, kernels, first, second, kown, koth, fown, foth, sown, soth,
                 kbuf, kwide, krows, mbuf, sems):
    core = meta[1]
    chosen = []
    for k, (kout, fout, sout) in enumerate(((kown, fown, sown), (koth, foth, soth))):
        for j in range(2):
            op = picked(meta, core if k == 0 else 1 - core, j)
            group = pl.ds(pl.multiple_of((op >> 3) << 3, 8), 8)
            i = 2 * k + j
            copies = [
                pltpu.make_async_copy(kernels.at[j, :, group, :], kbuf.at[i], sems.at[i]),
                pltpu.make_async_copy(first.at[j, :, group, :], mbuf.at[i], sems.at[4 + i]),
                pltpu.make_async_copy(second.at[j, :, group, :], mbuf.at[4 + i], sems.at[8 + i]),
            ]
            chosen.append((copies, op & 7, kout, fout, sout, i, j))
            for c in copies:
                c.start()
    for copies, lane, kout, fout, sout, i, j in chosen:
        copies[0].wait()
        kwide[...] = kbuf[i].astype(F32)
        for r in range(25):
            krows[pl.ds(r, 1), :] = kwide[r, pl.ds(lane, 1), :]
        kout[j] = krows[...].astype(BF)
        copies[1].wait()
        copies[2].wait()
        for r in range(12):
            fout[pl.ds(2 * r + j, 1), :] = mbuf[i, r, pl.ds(lane, 1), :]
            sout[pl.ds(2 * r + j, 1), :] = mbuf[4 + i, r, pl.ds(lane, 1), :]


def stack_kernel(*refs):
    out = refs[-1]
    for i, ref in enumerate(refs[:-1]):
        out[i] = ref[...]


def gather_kernel(own, two, one, back, out):
    for shift, ref in ((0, own), (2, two), (1, one), (7, back)):
        for i in range(2):
            out[(shift + 4 * i) & 7] = ref[i]


def join_kernel(own, recv, out):
    out[pl.ds(0, 24), :] = own[...]
    out[pl.ds(24, 24), :] = recv[...]


def near_sum_kernel(a, b, c, d, own, two, one, back):
    for shift, ref in ((0, own), (2, two), (1, one), (7, back)):
        for i in range(2):
            k = (shift + 4 * i) & 7
            total = (a[k].astype(F32) + b[k].astype(F32)) + (c[k].astype(F32) + d[k].astype(F32))
            ref[i] = total.astype(ref.dtype)


def middle_sum_kernel(own, two, one, back, stays, goes):
    for i, ref in enumerate((stays, goes)):
        total = own[i] + two[i].astype(F32) + one[i].astype(F32) + back[i].astype(F32)
        ref[...] = total.astype(ref.dtype)


def sum_kernel(near, *refs):
    own, other, wide = refs[-3:]
    total = near[...]
    for ref in refs[:-3]:
        total = total + ref[...].astype(F32)
    wide[...] = total
    for o, out in enumerate((own, other)):
        for j in range(2):
            for r in range(12):
                out[pl.ds(2 * r + j, 1), :] = wide[pl.ds(24 * o + 12 * j + r, 1), :]


def adam_kernel(total_rows, meta, mine, theirs, wown, woth, fown, foth, sown, soth,
                new_w, new_f, new_s, wide):
    core = meta[1]
    count = jnp.where(core == 0, meta[2], meta[3])
    odd = (lax.broadcasted_iota(jnp.int32, mine.shape, 0) & 1) == 1
    same_first = jnp.where(picked(meta, 0, 0) == picked(meta, 1, 0), 1.0, 0.0)
    same_second = jnp.where(picked(meta, 0, 1) == picked(meta, 1, 1), 1.0, 0.0)
    same = jnp.where(odd, same_second, same_first) > 0.5
    live = jnp.where(odd, count, 2) == 2
    for k, (wref, fref, sref) in enumerate(((wown, fown, sown), (woth, foth, soth))):
        n = core if k == 0 else 1 - core
        grad, rest = (mine[...], theirs[...]) if k == 0 else (theirs[...], mine[...])
        grad = (grad + jnp.where(same, rest, jnp.zeros_like(rest))) / total_rows
        source = wref[...].astype(F32)
        for j in range(2):
            for r in range(12):
                wide[pl.ds(2 * r + j, 1), :] = source[12 * j + r : 12 * j + r + 1, :]
        weight, one, two = wide[...], fref[...], sref[...]
        next_one = first_decay * one + (1.0 - first_decay) * grad
        next_two = second_decay * two + (1.0 - second_decay) * grad * grad
        next_weight = weight - learn_rate * (next_one / first_bias) / (
            jnp.sqrt(next_two / second_bias) + adam_epsilon
        )
        out_w = jnp.where(live, next_weight, weight)
        out_f = jnp.where(live, next_one, one)
        out_s = jnp.where(live, next_two, two)
        for r in range(12):
            new_w[n, r] = out_w[2 * r : 2 * r + 2].astype(BF)
            new_f[n, r] = out_f[2 * r : 2 * r + 2]
            new_s[n, r] = out_s[2 * r : 2 * r + 2]


def body(images, cotangent, picks, section_sizes, kernels, weights, first_moment, second_moment):
    width = images.shape[-1]
    own_segment = lax.axis_index("segment")
    segments = lax.axis_size("segment")
    parts = lax.axis_size("dp")
    total_rows = images.shape[0] * images.shape[1] * images.shape[2] * parts
    swap = [(s, s ^ 1) for s in range(segments)]
    ahead = [(s, (s + 2) % segments) for s in range(segments)]
    behind = [(s, (s - 2) % segments) for s in range(segments)]

    def along(value, dz, dy):
        pairs = [
            (4 * z + y, 4 * ((z + dz) % 8) + (y + dy) % 4) for z in range(8) for y in range(4)
        ]
        return lax.ppermute(value, "dp", pairs)

    far = (2, 1, 7)

    DMA = pltpu.SemaphoreType.DMA
    V = pltpu.VMEM
    state = (4, ROWS, width)
    flat_shape = (ROWS, width)
    s_pad = V((3, PADDED, LANES), F32)
    pair, square, tap_shape = (24, width), (4, width, width), (4, 25, width)

    core = own_segment & 1
    part = lax.axis_index("dp")
    place = lax.broadcasted_iota(jnp.int32, (10,), 0)
    early = jnp.pad(picks.reshape(4), (6, 0))
    for i, value in ((0, own_segment >> 1), (1, core), (4, part >> 2), (5, part & 3)):
        early = jnp.where(place == i, value, early)
    early = lax.optimization_barrier(early)
    sizes_other = lax.ppermute(section_sizes, "segment", swap)

    wown, woth = call(
        weight_kernel,
        [(pair, BF), (pair, BF)],
        [SMEM, HBM],
        [V((4, 12, 8, width), BF), V((12, 8, width), F32), V((2, 24, width), F32), DMA((4,))],
        cost=1000,
    )(early, weights.transpose(0, 2, 1, 3))
    wrecv = lax.ppermute(woth, "segment", swap)
    (message,) = call(join_kernel, [((48, width), BF)], [VMEM, VMEM], [], cost=1000)(wown, wrecv)
    (couple,) = call(stack_kernel, [((2, 48, width), BF)], [VMEM] * 2, [], cost=1000)(
        message, along(message, 4, 0)
    )
    (near,) = call(gather_kernel, [((8, 48, width), BF)], [VMEM] * 4, [], cost=1000)(
        couple, *[along(couple, dz, 0) for dz in far]
    )
    late, near = lax.optimization_barrier((early, near))
    columns = {0: near}
    for dy in (2, 1, 3):
        columns[dy] = along(near, 0, dy)
    kown, kother, fown, foth, sown, soth = call(
        table_kernel,
        [((2, 25, width), BF)] * 2 + [(pair, F32)] * 4,
        [SMEM, HBM, HBM, HBM],
        [V((4, 25, 8, width), BF), V((25, 8, width), F32), V((25, width), F32),
         V((8, 12, 8, width), F32), DMA((12,))],
    )(
        late,
        kernels.transpose(0, 2, 1, 3),
        first_moment.transpose(0, 2, 1, 3),
        second_moment.transpose(0, 2, 1, 3),
    )
    koth = lax.ppermute(kother, "segment", swap)
    size_low = jnp.where(core == 0, section_sizes[0], sizes_other[0])
    size_high = jnp.where(core == 0, sizes_other[0], section_sizes[0])
    meta = jnp.where(place == 2, size_low, jnp.where(place == 3, size_high, early))
    edges = ((0, 0), (0, PITCH - SIDE), (0, 0))
    img = jnp.pad(images[0], edges).reshape(flat_shape)
    chosen = lax.dynamic_index_in_dim(cotangent[:, 0], core, 0, keepdims=False)
    cot = jnp.pad(chosen, edges).reshape(flat_shape)
    img, cot, koth = lax.optimization_barrier((img, cot, koth))

    y, wall, taps, hs, ds = call(
        first_kernel,
        [(flat_shape, BF), (square, BF), (tap_shape, F32), (state, BF), (state, F32)],
        [SMEM] + [VMEM] * 7,
        [s_pad, V((4, 8, 48, width), BF)],
    )(meta, img, *[columns[i] for i in range(4)], kown, koth)
    cur = lax.ppermute(y, "segment", ahead)
    for step in (1, 2):
        y, hs, ds = call(
            functools.partial(forward_kernel, step),
            [(flat_shape, BF), (state, BF), (state, F32)],
            [SMEM] + [VMEM] * 5,
            [s_pad],
            {4: 1, 5: 2},
        )(meta, cur, wall, taps, hs, ds)
        cur = lax.ppermute(y, "segment", ahead)
    y, hs, ys, ds = call(
        functools.partial(middle_kernel, 3),
        [(flat_shape, BF), (state, BF), (state, BF), (state, F32)],
        [SMEM] + [VMEM] * 6,
        [s_pad],
        {5: 1, 6: 3},
    )(meta, cur, cot, wall, taps, hs, ds)
    cur = lax.ppermute(y, "segment", behind)
    for step in (2, 1):
        y, ys = call(
            functools.partial(backward_kernel, step),
            [(flat_shape, BF), (state, BF)],
            [SMEM] + [VMEM] * 5,
            [s_pad],
            {5: 1},
        )(meta, cur, wall, taps, ds, ys)
        cur = lax.ppermute(y, "segment", behind)
    column = (8, 48, width)
    *sends, _ = call(
        last_kernel,
        [(column, BF)] * 4 + [(state, BF)],
        [SMEM] + [VMEM] * 6,
        [V(flat_shape, BF), s_pad, V((2, width, width), F32), V((4, 8, 48, width), BF)],
        {6: 4},
    )(meta, cur, wall, taps, ds, hs, ys)
    came = [along(sends[dy], 0, dy) for dy in (2, 1, 3)]
    couple_shape, single = (2, 48, width), (48, width)
    couple, *partial = call(
        near_sum_kernel, [(couple_shape, F32)] + [(couple_shape, BF)] * 3, [VMEM] * 4, [], cost=1000
    )(sends[0], *came)
    stays, goes = call(
        middle_sum_kernel, [(single, F32), (single, BF)], [VMEM] * 4, [], cost=1000
    )(couple, *[along(value, dz, 0) for value, dz in zip(partial, far)])
    own, for_other = call(
        sum_kernel, [(pair, F32), (pair, F32)], [VMEM] * 2, [V((48, width), F32)], cost=1000
    )(stays, along(goes, 4, 0))
    other = lax.ppermute(for_other, "segment", swap)
    rows = (2, 12, 2, width)
    news = call(
        functools.partial(adam_kernel, float(total_rows)),
        [(rows, BF), (rows, F32), (rows, F32)],
        [SMEM] + [VMEM] * 8,
        [V(pair, F32)],
    )(meta, own, other, wown, woth, fown, foth, sown, soth)
    return tuple(new.transpose(0, 2, 1, 3) for new in news)


def solution(mesh):
    return jax.shard_map(
        body,
        mesh=mesh,
        in_specs=(
            P("dp", None, None, None),
            P(None, "dp", None, None, None),
            P(None, "segment"),
            P("segment"),
            P("segment", None, None, None),
            P("segment", None, "dp", None),
            P("segment", None, "dp", None),
            P("segment", None, "dp", None),
        ),
        out_specs=(
            P(None, "segment", "dp", None),
            P(None, "segment", "dp", None),
            P(None, "segment", "dp", None),
        ),
        check_vma=False,
    )
```

```python
import functools

import jax
import jax.numpy as jnp
from jax import lax
from jax.experimental import pallas as pl
from jax.experimental.pallas import tpu as pltpu
from jax.sharding import PartitionSpec as P

first_decay = 0.9
second_decay = 0.999
learn_rate = 0.01
adam_epsilon = 1e-08
first_bias = 1.0 - 0.9**10
second_bias = 1.0 - 0.999**10

SIDE = 14
PITCH = 16
ROWS = SIDE * PITCH
LANES = 128
HEAD = 8 + 2 * PITCH
PADDED = 8 + (SIDE + 4) * PITCH + 8
BF = jnp.bfloat16
F32 = jnp.float32

HBM = pl.BlockSpec(memory_space=pltpu.HBM)
SMEM = pl.BlockSpec(memory_space=pltpu.SMEM)


VMEM = pl.BlockSpec(memory_space=pltpu.VMEM)


def call(kernel, outs, in_specs, scratch, aliases=None, cost=2_000_000_000, grant=8 << 20):
    return pl.pallas_call(
        kernel,
        out_shape=[jax.ShapeDtypeStruct(s, d) for s, d in outs],
        in_specs=in_specs,
        out_specs=[VMEM] * len(outs),
        scratch_shapes=scratch,
        input_output_aliases=aliases or {},
        compiler_params=pltpu.CompilerParams(vmem_limit_bytes=grant),
        cost_estimate=pl.CostEstimate(flops=cost, bytes_accessed=1_000_000, transcendentals=0),
    )


def keep_mask(shape):
    return (lax.broadcasted_iota(jnp.int32, shape, 0) & (PITCH - 1)) < SIDE


def conv_rows(pad, taps, group, flipped, emit):
    sign = -1 if flipped else 1
    cols = pl.ds(group * LANES, LANES)
    weights = [jnp.broadcast_to(taps[pl.ds(i, 1), cols], (PITCH, LANES)) for i in range(25)]
    for p in range(0, SIDE, 2):
        totals = [None, None]
        for da in range(-2, 4):
            for e in range(-2, 3):
                start = HEAD + PITCH * (p + da) + e
                window = pad[group, pl.ds(start, PITCH), :]
                for k in range(2):
                    a = da - k
                    if -2 <= a <= 2:
                        tap = (sign * a + 2) * 5 + (sign * e + 2)
                        term = weights[tap] * window
                        totals[k] = term if totals[k] is None else totals[k] + term
        emit(p, totals[0])
        emit(p + 1, totals[1])


def clear_pad(pad):
    for g in range(3):
        pad[g, pl.ds(0, HEAD), :] = jnp.zeros((HEAD, LANES), F32)
        pad[g, pl.ds(HEAD + ROWS, PADDED - HEAD - ROWS), :] = jnp.zeros(
            (PADDED - HEAD - ROWS, LANES), F32
        )


def fill_pad(pad, value):
    for g in range(3):
        pad[g, pl.ds(HEAD, ROWS), :] = value[:, g * LANES : (g + 1) * LANES]


def live_of(meta, t):
    odd = (t & 1) == 1
    count = jnp.where(t < 2, meta[2], meta[3])
    return jnp.logical_or(jnp.logical_not(odd), count == 2)


def run_forward(meta, pad, flat, wall, taps, hs, ds, skip_last):
    last = jnp.where(meta[3] == 2, 3, 2)
    fill_pad(pad, flat[...].astype(F32))

    def slot(t, carry):
        @pl.when(live_of(meta, t))
        def _():
            for g in range(3):

                def emit(p, u, g=g):
                    rows, cols = pl.ds(p * PITCH, PITCH), pl.ds(g * LANES, LANES)
                    s = 0.5 * jnp.tanh(0.5 * u) + 0.5
                    us = u * s
                    hs[t, rows, cols] = us.astype(BF)
                    ds[t, rows, cols] = s * (1.0 + (u - us))

                conv_rows(pad, taps.at[t], g, False, emit)

            def update():
                value = jnp.dot(hs[t], wall[t], preferred_element_type=F32)
                value = flat[...].astype(F32) + value
                rounded = jnp.where(keep_mask(value.shape), value, 0.0).astype(BF)
                flat[...] = rounded
                fill_pad(pad, rounded.astype(F32))

            if skip_last:
                pl.when(t != last)(update)
            else:
                update()

        return carry

    lax.fori_loop(0, 4, slot, 0)


def run_backward(meta, pad, flat, wall, taps, ds, ys, skip_first):
    def slot(i, carry):
        t = 3 - i

        @pl.when(live_of(meta, t))
        def _():
            ys[t] = flat[...]

            def chain():
                dh = lax.dot_general(
                    flat[...], wall[t], (((1,), (1,)), ((), ())), preferred_element_type=F32
                )
                fill_pad(pad, dh * ds[t])
                for g in range(3):

                    def emit(p, total, g=g):
                        rows, cols = pl.ds(p * PITCH, PITCH), pl.ds(g * LANES, LANES)
                        value = ys[t, rows, cols].astype(F32) + total
                        keep = lax.broadcasted_iota(jnp.int32, value.shape, 0) < SIDE
                        flat[rows, cols] = jnp.where(keep, value, 0.0).astype(BF)

                    conv_rows(pad, taps.at[t], g, True, emit)

            if skip_first:
                pl.when(t != 0)(chain)
            else:
                chain()

        return carry

    lax.fori_loop(0, 4, slot, 0)


def first_kernel(meta, img, *refs):
    columns, (kown, koth, y, wall, taps, hs, ds, pad, packed) = refs[:8], refs[8:]
    core, z, yy = meta[1], meta[4], meta[5]
    for i, ref in enumerate(columns):
        packed[(yy - i // 2) & 3, pl.ds(4 * (i % 2), 4)] = ref[...]
    for o, kref in enumerate((kown, koth)):
        for j in range(2):
            taps[(2 * o + j + 2 * core) & 3] = kref[j].astype(F32)
    for o in range(2):
        base = (2 * o + 2 * core) & 3
        place = pl.ds(24 * o, 24)
        for i in range(16):
            shift = (z - i // 2) & 7
            one = packed[2 * (i % 2), shift, place, :].astype(F32)
            two = packed[2 * (i % 2) + 1, shift, place, :].astype(F32)
            rows = pl.ds(24 * i, 24)
            wall[base, rows, :] = jnp.concatenate([one[:12], two[:12]], axis=0).astype(BF)
            wall[base + 1, rows, :] = jnp.concatenate([one[12:], two[12:]], axis=0).astype(BF)

    @pl.when(meta[0] == 0)
    def _():
        clear_pad(pad)
        y[...] = img[...]
        run_forward(meta, pad, y, wall, taps, hs, ds, False)


def forward_kernel(step, meta, cur, wall, taps, hin, din, y, hs, ds, pad):
    del hin, din

    @pl.when(meta[0] == step)
    def _():
        clear_pad(pad)
        y[...] = cur[...]
        run_forward(meta, pad, y, wall, taps, hs, ds, False)


def middle_kernel(step, meta, cur, cot, wall, taps, hin, din, y, hs, ys, ds, pad):
    del hin, din

    @pl.when(meta[0] == step)
    def _():
        clear_pad(pad)
        y[...] = cur[...]
        run_forward(meta, pad, y, wall, taps, hs, ds, True)
        y[...] = cot[...]
        run_backward(meta, pad, y, wall, taps, ds, ys, False)


def backward_kernel(step, meta, cur, wall, taps, ds, yin, y, ys, pad):
    del yin

    @pl.when(meta[0] == step)
    def _():
        clear_pad(pad)
        y[...] = cur[...]
        run_backward(meta, pad, y, wall, taps, ds, ys, False)


def last_kernel(meta, cur, wall, taps, ds, hs, yin, near, ahead1, ahead2, ahead3, ys,
                flat, pad, total, send):
    del yin
    core, z, yy = meta[1], meta[4], meta[5]

    @pl.when(meta[0] == 0)
    def _():
        clear_pad(pad)
        flat[...] = cur[...]
        run_backward(meta, pad, flat, wall, taps, ds, ys, True)

    def term(t):
        return lax.dot_general(
            hs[t], ys[t], (((0,), (0,)), ((), ())), preferred_element_type=F32
        )

    for o in range(2):
        base = (2 * o + 2 * core) & 3
        live = live_of(meta, base + 1)
        total[0] = term(base)

        @pl.when(live)
        def _():
            total[1] = term(base + 1)

        @pl.when(jnp.logical_not(live))
        def _():
            total[1] = jnp.zeros(total.shape[1:], F32)

        for i in range(16):
            rows = pl.ds(24 * i, 24)
            one, two = total[0, rows, :], total[1, rows, :]
            place = pl.ds(24 * o, 24)
            shift = (i // 2 - z) & 7
            send[2 * (i % 2), shift, place, :] = jnp.concatenate(
                [one[:12], two[:12]], axis=0
            ).astype(BF)
            send[2 * (i % 2) + 1, shift, place, :] = jnp.concatenate(
                [one[12:], two[12:]], axis=0
            ).astype(BF)
    for shift, ref in enumerate((near, ahead1, ahead2, ahead3)):
        ref[...] = send[(yy + shift) & 3]


def picked(meta, n, j):
    return meta[6 + 2 * n + j]


def weight_kernel(meta, weights, own, oth, buf, wide, rows, sems):
    core = meta[1]
    copies = []
    for k, out in enumerate((own, oth)):
        for j in range(2):
            op = picked(meta, core if k == 0 else 1 - core, j)
            group = pl.ds(pl.multiple_of((op >> 3) << 3, 8), 8)
            copies.append(
                pltpu.make_async_copy(
                    weights.at[j, :, group, :], buf.at[2 * k + j], sems.at[2 * k + j]
                )
            )
            copies[-1].start()
    for k, out in enumerate((own, oth)):
        for j in range(2):
            op = picked(meta, core if k == 0 else 1 - core, j)
            copies[2 * k + j].wait()
            wide[...] = buf[2 * k + j].astype(F32)
            for r in range(12):
                rows[k, pl.ds(12 * j + r, 1), :] = wide[r, pl.ds(op & 7, 1), :]
        out[...] = rows[k].astype(BF)


def table_kernel(meta, kernels, first, second, kown, koth, fown, foth, sown, soth,
                 kbuf, kwide, krows, mbuf, sems):
    core = meta[1]
    chosen = []
    for k, (kout, fout, sout) in enumerate(((kown, fown, sown), (koth, foth, soth))):
        for j in range(2):
            op = picked(meta, core if k == 0 else 1 - core, j)
            group = pl.ds(pl.multiple_of((op >> 3) << 3, 8), 8)
            i = 2 * k + j
            copies = [
                pltpu.make_async_copy(kernels.at[j, :, group, :], kbuf.at[i], sems.at[i]),
                pltpu.make_async_copy(first.at[j, :, group, :], mbuf.at[i], sems.at[4 + i]),
                pltpu.make_async_copy(second.at[j, :, group, :], mbuf.at[4 + i], sems.at[8 + i]),
            ]
            chosen.append((copies, op & 7, kout, fout, sout, i, j))
            for c in copies:
                c.start()
    for copies, lane, kout, fout, sout, i, j in chosen:
        copies[0].wait()
        kwide[...] = kbuf[i].astype(F32)
        for r in range(25):
            krows[pl.ds(r, 1), :] = kwide[r, pl.ds(lane, 1), :]
        kout[j] = krows[...].astype(BF)
        copies[1].wait()
        copies[2].wait()
        for r in range(12):
            fout[pl.ds(2 * r + j, 1), :] = mbuf[i, r, pl.ds(lane, 1), :]
            sout[pl.ds(2 * r + j, 1), :] = mbuf[4 + i, r, pl.ds(lane, 1), :]


def stack_kernel(*refs):
    out = refs[-1]
    for i, ref in enumerate(refs[:-1]):
        out[i] = ref[...]


def gather_kernel(own, ahead, back, low, high):
    for refs, shifts in ((own, (1, 0, 7)), (ahead, (4, 3, 2)), (back, (6, 5))):
        for i, shift in enumerate(shifts):
            out = low if shift < 4 else high
            out[shift & 3] = refs[i]


def join_kernel(own, recv, out):
    out[pl.ds(0, 24), :] = own[...]
    out[pl.ds(24, 24), :] = recv[...]


def near_sum_kernel(a, b, c, d, own, plus, minus):
    for ref, shifts in ((own, (7, 0, 1)), (plus, (2, 3, 4)), (minus, (5, 6))):
        for i, k in enumerate(shifts):
            total = (a[k].astype(F32) + b[k].astype(F32)) + (c[k].astype(F32) + d[k].astype(F32))
            ref[i] = total.astype(ref.dtype)


def middle_sum_kernel(own, plus, minus, down, stays, up):
    for i, ref in enumerate((down, stays, up)):
        total = own[i] + plus[i].astype(F32)
        if i > 0:
            total = total + minus[i - 1].astype(F32)
        ref[...] = total.astype(ref.dtype)


def sum_kernel(near, *refs):
    own, other, wide = refs[-3:]
    total = near[...]
    for ref in refs[:-3]:
        total = total + ref[...].astype(F32)
    wide[...] = total
    for o, out in enumerate((own, other)):
        for j in range(2):
            for r in range(12):
                out[pl.ds(2 * r + j, 1), :] = wide[pl.ds(24 * o + 12 * j + r, 1), :]


def adam_kernel(total_rows, meta, mine, theirs, wown, woth, fown, foth, sown, soth,
                new_w, new_f, new_s, wide):
    core = meta[1]
    count = jnp.where(core == 0, meta[2], meta[3])
    odd = (lax.broadcasted_iota(jnp.int32, mine.shape, 0) & 1) == 1
    same_first = jnp.where(picked(meta, 0, 0) == picked(meta, 1, 0), 1.0, 0.0)
    same_second = jnp.where(picked(meta, 0, 1) == picked(meta, 1, 1), 1.0, 0.0)
    same = jnp.where(odd, same_second, same_first) > 0.5
    live = jnp.where(odd, count, 2) == 2
    for k, (wref, fref, sref) in enumerate(((wown, fown, sown), (woth, foth, soth))):
        n = core if k == 0 else 1 - core
        grad, rest = (mine[...], theirs[...]) if k == 0 else (theirs[...], mine[...])
        grad = (grad + jnp.where(same, rest, jnp.zeros_like(rest))) / total_rows
        source = wref[...].astype(F32)
        for j in range(2):
            for r in range(12):
                wide[pl.ds(2 * r + j, 1), :] = source[12 * j + r : 12 * j + r + 1, :]
        weight, one, two = wide[...], fref[...], sref[...]
        next_one = first_decay * one + (1.0 - first_decay) * grad
        next_two = second_decay * two + (1.0 - second_decay) * grad * grad
        next_weight = weight - learn_rate * (next_one / first_bias) / (
            jnp.sqrt(next_two / second_bias) + adam_epsilon
        )
        out_w = jnp.where(live, next_weight, weight)
        out_f = jnp.where(live, next_one, one)
        out_s = jnp.where(live, next_two, two)
        for r in range(12):
            new_w[n, r] = out_w[2 * r : 2 * r + 2].astype(BF)
            new_f[n, r] = out_f[2 * r : 2 * r + 2]
            new_s[n, r] = out_s[2 * r : 2 * r + 2]


def body(images, cotangent, picks, section_sizes, kernels, weights, first_moment, second_moment):
    width = images.shape[-1]
    own_segment = lax.axis_index("segment")
    segments = lax.axis_size("segment")
    parts = lax.axis_size("dp")
    total_rows = images.shape[0] * images.shape[1] * images.shape[2] * parts
    swap = [(s, s ^ 1) for s in range(segments)]
    ahead = [(s, (s + 2) % segments) for s in range(segments)]
    behind = [(s, (s - 2) % segments) for s in range(segments)]

    def along(value, dz, dy):
        pairs = [
            (4 * z + y, 4 * ((z + dz) % 8) + (y + dy) % 4) for z in range(8) for y in range(4)
        ]
        return lax.ppermute(value, "dp", pairs)


    DMA = pltpu.SemaphoreType.DMA
    V = pltpu.VMEM
    state = (4, ROWS, width)
    flat_shape = (ROWS, width)
    s_pad = V((3, PADDED, LANES), F32)
    pair, square, tap_shape = (24, width), (4, width, width), (4, 25, width)

    core = own_segment & 1
    part = lax.axis_index("dp")
    place = lax.broadcasted_iota(jnp.int32, (10,), 0)
    early = jnp.pad(picks.reshape(4), (6, 0))
    for i, value in ((0, own_segment >> 1), (1, core), (4, part >> 2), (5, part & 3)):
        early = jnp.where(place == i, value, early)
    early = lax.optimization_barrier(early)
    sizes_other = lax.ppermute(section_sizes, "segment", swap)

    wown, woth = call(
        weight_kernel,
        [(pair, BF), (pair, BF)],
        [SMEM, HBM],
        [V((4, 12, 8, width), BF), V((12, 8, width), F32), V((2, 24, width), F32), DMA((4,))],
        cost=1000,
    )(early, weights.transpose(0, 2, 1, 3))
    wrecv = lax.ppermute(woth, "segment", swap)
    (message,) = call(join_kernel, [((48, width), BF)], [VMEM, VMEM], [], cost=1000)(wown, wrecv)
    (triple,) = call(stack_kernel, [((3, 48, width), BF)], [VMEM] * 3, [], cost=1000)(
        along(message, 1, 0), message, along(message, 7, 0)
    )
    half = (4, 48, width)
    low, high = call(gather_kernel, [(half, BF)] * 2, [VMEM] * 3, [], cost=1000)(
        triple, along(triple, 3, 0), along(triple, 5, 0)
    )
    low_one, high_three = along(low, 0, 1), along(high, 0, 3)
    high_one, low_three = along(high, 0, 1), along(low, 0, 3)
    late, low_one, high_three = lax.optimization_barrier((early, low_one, high_three))
    low_two, high_two = along(low_one, 0, 1), along(high_three, 0, 3)
    columns = (low, high, low_one, high_one, low_two, high_two, low_three, high_three)
    kown, kother, fown, foth, sown, soth = call(
        table_kernel,
        [((2, 25, width), BF)] * 2 + [(pair, F32)] * 4,
        [SMEM, HBM, HBM, HBM],
        [V((4, 25, 8, width), BF), V((25, 8, width), F32), V((25, width), F32),
         V((8, 12, 8, width), F32), DMA((12,))],
    )(
        late,
        kernels.transpose(0, 2, 1, 3),
        first_moment.transpose(0, 2, 1, 3),
        second_moment.transpose(0, 2, 1, 3),
    )
    koth = lax.ppermute(kother, "segment", swap)
    size_low = jnp.where(core == 0, section_sizes[0], sizes_other[0])
    size_high = jnp.where(core == 0, sizes_other[0], section_sizes[0])
    meta = jnp.where(place == 2, size_low, jnp.where(place == 3, size_high, early))
    edges = ((0, 0), (0, PITCH - SIDE), (0, 0))
    img = jnp.pad(images[0], edges).reshape(flat_shape)
    chosen = lax.dynamic_index_in_dim(cotangent[:, 0], core, 0, keepdims=False)
    cot = jnp.pad(chosen, edges).reshape(flat_shape)
    img, cot, koth = lax.optimization_barrier((img, cot, koth))

    y, wall, taps, hs, ds = call(
        first_kernel,
        [(flat_shape, BF), (square, BF), (tap_shape, F32), (state, BF), (state, F32)],
        [SMEM] + [VMEM] * 11,
        [s_pad, V((4, 8, 48, width), BF)],
    )(meta, img, *columns, kown, koth)
    cur = lax.ppermute(y, "segment", ahead)
    for step in (1, 2):
        y, hs, ds = call(
            functools.partial(forward_kernel, step),
            [(flat_shape, BF), (state, BF), (state, F32)],
            [SMEM] + [VMEM] * 5,
            [s_pad],
            {4: 1, 5: 2},
        )(meta, cur, wall, taps, hs, ds)
        cur = lax.ppermute(y, "segment", ahead)
    y, hs, ys, ds = call(
        functools.partial(middle_kernel, 3),
        [(flat_shape, BF), (state, BF), (state, BF), (state, F32)],
        [SMEM] + [VMEM] * 6,
        [s_pad],
        {5: 1, 6: 3},
    )(meta, cur, cot, wall, taps, hs, ds)
    cur = lax.ppermute(y, "segment", behind)
    for step in (2, 1):
        y, ys = call(
            functools.partial(backward_kernel, step),
            [(flat_shape, BF), (state, BF)],
            [SMEM] + [VMEM] * 5,
            [s_pad],
            {5: 1},
        )(meta, cur, wall, taps, ds, ys)
        cur = lax.ppermute(y, "segment", behind)
    column = (8, 48, width)
    *sends, _ = call(
        last_kernel,
        [(column, BF)] * 4 + [(state, BF)],
        [SMEM] + [VMEM] * 6,
        [V(flat_shape, BF), s_pad, V((2, width, width), F32), V((4, 8, 48, width), BF)],
        {6: 4},
    )(meta, cur, wall, taps, ds, hs, ys)
    came = [along(sends[dy], 0, dy) for dy in (2, 1, 3)]
    triple_shape, single = (3, 48, width), (48, width)
    inner, plus, minus = call(
        near_sum_kernel,
        [(triple_shape, F32), (triple_shape, BF), ((2, 48, width), BF)],
        [VMEM] * 4,
        [],
        cost=1000,
    )(sends[0], *came)
    down, stays, up = call(
        middle_sum_kernel, [(single, BF), (single, F32), (single, BF)], [VMEM] * 3, [], cost=1000
    )(inner, along(plus, 3, 0), along(minus, 5, 0))
    own, for_other = call(
        sum_kernel, [(pair, F32), (pair, F32)], [VMEM] * 3, [V((48, width), F32)], cost=1000
    )(stays, along(up, 1, 0), along(down, 7, 0))
    other = lax.ppermute(for_other, "segment", swap)
    rows = (2, 12, 2, width)
    news = call(
        functools.partial(adam_kernel, float(total_rows)),
        [(rows, BF), (rows, F32), (rows, F32)],
        [SMEM] + [VMEM] * 8,
        [V(pair, F32)],
    )(meta, own, other, wown, woth, fown, foth, sown, soth)
    return tuple(new.transpose(0, 2, 1, 3) for new in news)


def solution(mesh):
    return jax.shard_map(
        body,
        mesh=mesh,
        in_specs=(
            P("dp", None, None, None),
            P(None, "dp", None, None, None),
            P(None, "segment"),
            P("segment"),
            P("segment", None, None, None),
            P("segment", None, "dp", None),
            P("segment", None, "dp", None),
            P("segment", None, "dp", None),
        ),
        out_specs=(
            P(None, "segment", "dp", None),
            P(None, "segment", "dp", None),
            P(None, "segment", "dp", None),
        ),
        check_vma=False,
    )
```

```python
import functools

import jax
import jax.numpy as jnp
from jax import lax
from jax.experimental import pallas as pl
from jax.experimental.pallas import tpu as pltpu
from jax.sharding import PartitionSpec as P

first_decay = 0.9
second_decay = 0.999
learn_rate = 0.01
adam_epsilon = 1e-08
first_bias = 1.0 - 0.9**10
second_bias = 1.0 - 0.999**10

SIDE = 14
PITCH = 16
ROWS = SIDE * PITCH
LANES = 128
HEAD = 8 + 2 * PITCH
PADDED = 8 + (SIDE + 4) * PITCH + 8
BF = jnp.bfloat16
F32 = jnp.float32

HBM = pl.BlockSpec(memory_space=pltpu.HBM)
SMEM = pl.BlockSpec(memory_space=pltpu.SMEM)


VMEM = pl.BlockSpec(memory_space=pltpu.VMEM)


def call(kernel, outs, in_specs, scratch, aliases=None, cost=2_000_000_000, grant=8 << 20):
    return pl.pallas_call(
        kernel,
        out_shape=[jax.ShapeDtypeStruct(s, d) for s, d in outs],
        in_specs=in_specs,
        out_specs=[VMEM] * len(outs),
        scratch_shapes=scratch,
        input_output_aliases=aliases or {},
        compiler_params=pltpu.CompilerParams(vmem_limit_bytes=grant),
        cost_estimate=pl.CostEstimate(flops=cost, bytes_accessed=1_000_000, transcendentals=0),
    )


def keep_mask(shape):
    return (lax.broadcasted_iota(jnp.int32, shape, 0) & (PITCH - 1)) < SIDE


def conv_rows(pad, taps, group, flipped, emit):
    sign = -1 if flipped else 1
    cols = pl.ds(group * LANES, LANES)
    weights = [jnp.broadcast_to(taps[pl.ds(i, 1), cols], (PITCH, LANES)) for i in range(25)]
    for p in range(0, SIDE, 2):
        totals = [None, None]
        for da in range(-2, 4):
            if not 0 <= p + da < SIDE:
                continue
            for e in range(-2, 3):
                start = HEAD + PITCH * (p + da) + e
                window = pad[group, pl.ds(start, PITCH), :]
                for k in range(2):
                    a = da - k
                    if -2 <= a <= 2:
                        tap = (sign * a + 2) * 5 + (sign * e + 2)
                        term = weights[tap] * window
                        totals[k] = term if totals[k] is None else totals[k] + term
        emit(p, totals[0])
        emit(p + 1, totals[1])


def clear_pad(pad):
    for g in range(3):
        pad[g, pl.ds(0, HEAD), :] = jnp.zeros((HEAD, LANES), F32)
        pad[g, pl.ds(HEAD + ROWS, PADDED - HEAD - ROWS), :] = jnp.zeros(
            (PADDED - HEAD - ROWS, LANES), F32
        )


def fill_pad(pad, value):
    for g in range(3):
        pad[g, pl.ds(HEAD, ROWS), :] = value[:, g * LANES : (g + 1) * LANES]


def live_of(meta, t):
    odd = (t & 1) == 1
    count = jnp.where(t < 2, meta[2], meta[3])
    return jnp.logical_or(jnp.logical_not(odd), count == 2)


def run_forward(meta, pad, flat, wall, taps, hs, ds, skip_last):
    last = jnp.where(meta[3] == 2, 3, 2)
    fill_pad(pad, flat[...].astype(F32))

    def slot(t, carry):
        @pl.when(live_of(meta, t))
        def _():
            for g in range(3):

                def emit(p, u, g=g):
                    rows, cols = pl.ds(p * PITCH, PITCH), pl.ds(g * LANES, LANES)
                    s = 0.5 * jnp.tanh(0.5 * u) + 0.5
                    us = u * s
                    hs[t, rows, cols] = us.astype(BF)
                    ds[t, rows, cols] = s * (1.0 + (u - us))

                conv_rows(pad, taps.at[t], g, False, emit)

            def update():
                value = jnp.dot(hs[t], wall[t], preferred_element_type=F32)
                value = flat[...].astype(F32) + value
                rounded = jnp.where(keep_mask(value.shape), value, 0.0).astype(BF)
                flat[...] = rounded
                fill_pad(pad, rounded.astype(F32))

            if skip_last:
                pl.when(t != last)(update)
            else:
                update()

        return carry

    lax.fori_loop(0, 4, slot, 0)


def run_backward(meta, pad, flat, wall, taps, ds, ys, skip_first):
    def slot(i, carry):
        t = 3 - i

        @pl.when(live_of(meta, t))
        def _():
            ys[t] = flat[...]

            def chain():
                dh = lax.dot_general(
                    flat[...], wall[t], (((1,), (1,)), ((), ())), preferred_element_type=F32
                )
                fill_pad(pad, dh * ds[t])
                for g in range(3):

                    def emit(p, total, g=g):
                        rows, cols = pl.ds(p * PITCH, PITCH), pl.ds(g * LANES, LANES)
                        value = ys[t, rows, cols].astype(F32) + total
                        keep = lax.broadcasted_iota(jnp.int32, value.shape, 0) < SIDE
                        flat[rows, cols] = jnp.where(keep, value, 0.0).astype(BF)

                    conv_rows(pad, taps.at[t], g, True, emit)

            if skip_first:
                pl.when(t != 0)(chain)
            else:
                chain()

        return carry

    lax.fori_loop(0, 4, slot, 0)


def first_kernel(meta, img, *refs):
    columns, (kown, koth, y, wall, taps, hs, ds, pad, packed) = refs[:4], refs[4:]
    core, z, yy = meta[1], meta[4], meta[5]
    for i, ref in enumerate(columns):
        packed[(yy - i) & 3] = ref[...]
    for o, kref in enumerate((kown, koth)):
        for j in range(2):
            taps[(2 * o + j + 2 * core) & 3] = kref[j].astype(F32)
    for o in range(2):
        base = (2 * o + 2 * core) & 3
        place = pl.ds(24 * o, 24)
        for i in range(16):
            shift = (z - i // 2) & 7
            one = packed[2 * (i % 2), shift, place, :].astype(F32)
            two = packed[2 * (i % 2) + 1, shift, place, :].astype(F32)
            rows = pl.ds(24 * i, 24)
            wall[base, rows, :] = jnp.concatenate([one[:12], two[:12]], axis=0).astype(BF)
            wall[base + 1, rows, :] = jnp.concatenate([one[12:], two[12:]], axis=0).astype(BF)

    @pl.when(meta[0] == 0)
    def _():
        clear_pad(pad)
        y[...] = img[...]
        run_forward(meta, pad, y, wall, taps, hs, ds, False)


def forward_kernel(step, meta, cur, wall, taps, hin, din, y, hs, ds, pad):
    del hin, din

    @pl.when(meta[0] == step)
    def _():
        clear_pad(pad)
        y[...] = cur[...]
        run_forward(meta, pad, y, wall, taps, hs, ds, False)


def middle_kernel(step, meta, cur, cot, wall, taps, hin, din, y, hs, ys, ds, pad):
    del hin, din

    @pl.when(meta[0] == step)
    def _():
        clear_pad(pad)
        y[...] = cur[...]
        run_forward(meta, pad, y, wall, taps, hs, ds, True)
        y[...] = cot[...]
        run_backward(meta, pad, y, wall, taps, ds, ys, False)


def backward_kernel(step, meta, cur, wall, taps, ds, yin, y, ys, pad):
    del yin

    @pl.when(meta[0] == step)
    def _():
        clear_pad(pad)
        y[...] = cur[...]
        run_backward(meta, pad, y, wall, taps, ds, ys, False)


def last_kernel(meta, cur, wall, taps, ds, hs, yin, near, ahead1, ahead2, ahead3, ys,
                flat, pad, total, send):
    del yin
    core, z, yy = meta[1], meta[4], meta[5]

    @pl.when(meta[0] == 0)
    def _():
        clear_pad(pad)
        flat[...] = cur[...]
        run_backward(meta, pad, flat, wall, taps, ds, ys, True)

    def term(t):
        return lax.dot_general(
            hs[t], ys[t], (((0,), (0,)), ((), ())), preferred_element_type=F32
        )

    for o in range(2):
        base = (2 * o + 2 * core) & 3
        live = live_of(meta, base + 1)
        total[0] = term(base)

        @pl.when(live)
        def _():
            total[1] = term(base + 1)

        @pl.when(jnp.logical_not(live))
        def _():
            total[1] = jnp.zeros(total.shape[1:], F32)

        for i in range(16):
            rows = pl.ds(24 * i, 24)
            one, two = total[0, rows, :], total[1, rows, :]
            place = pl.ds(24 * o, 24)
            shift = (i // 2 - z) & 7
            send[2 * (i % 2), shift, place, :] = jnp.concatenate(
                [one[:12], two[:12]], axis=0
            ).astype(BF)
            send[2 * (i % 2) + 1, shift, place, :] = jnp.concatenate(
                [one[12:], two[12:]], axis=0
            ).astype(BF)
    for shift, ref in enumerate((near, ahead1, ahead2, ahead3)):
        ref[...] = send[(yy + shift) & 3]


def picked(meta, n, j):
    return meta[6 + 2 * n + j]


def weight_kernel(meta, weights, own, oth, buf, wide, rows, sems):
    core = meta[1]
    copies = []
    for k, out in enumerate((own, oth)):
        for j in range(2):
            op = picked(meta, core if k == 0 else 1 - core, j)
            group = pl.ds(pl.multiple_of((op >> 3) << 3, 8), 8)
            copies.append(
                pltpu.make_async_copy(
                    weights.at[j, :, group, :], buf.at[2 * k + j], sems.at[2 * k + j]
                )
            )
            copies[-1].start()
    for k, out in enumerate((own, oth)):
        for j in range(2):
            op = picked(meta, core if k == 0 else 1 - core, j)
            copies[2 * k + j].wait()
            wide[...] = buf[2 * k + j].astype(F32)
            for r in range(12):
                rows[k, pl.ds(12 * j + r, 1), :] = wide[r, pl.ds(op & 7, 1), :]
        out[...] = rows[k].astype(BF)


def tap_kernel(meta, kernels, kown, koth, kbuf, kwide, krows, sems):
    core = meta[1]
    copies = []
    for k in range(2):
        for j in range(2):
            op = picked(meta, core if k == 0 else 1 - core, j)
            group = pl.ds(pl.multiple_of((op >> 3) << 3, 8), 8)
            i = 2 * k + j
            copies.append(
                pltpu.make_async_copy(kernels.at[j, :, group, :], kbuf.at[i], sems.at[i])
            )
            copies[-1].start()
    for k, out in enumerate((kown, koth)):
        for j in range(2):
            lane = picked(meta, core if k == 0 else 1 - core, j) & 7
            copies[2 * k + j].wait()
            kwide[...] = kbuf[2 * k + j].astype(F32)
            for r in range(25):
                krows[pl.ds(r, 1), :] = kwide[r, pl.ds(lane, 1), :]
            out[j] = krows[...].astype(BF)


def moment_kernel(meta, first, second, fown, foth, sown, soth, mbuf, sems):
    core = meta[1]
    chosen = []
    for k, (fout, sout) in enumerate(((fown, sown), (foth, soth))):
        for j in range(2):
            op = picked(meta, core if k == 0 else 1 - core, j)
            group = pl.ds(pl.multiple_of((op >> 3) << 3, 8), 8)
            i = 2 * k + j
            copies = [
                pltpu.make_async_copy(first.at[j, :, group, :], mbuf.at[i], sems.at[i]),
                pltpu.make_async_copy(second.at[j, :, group, :], mbuf.at[4 + i], sems.at[4 + i]),
            ]
            chosen.append((copies, op & 7, fout, sout, i, j))
            for c in copies:
                c.start()
    for copies, lane, fout, sout, i, j in chosen:
        for c in copies:
            c.wait()
        for r in range(12):
            fout[pl.ds(2 * r + j, 1), :] = mbuf[i, r, pl.ds(lane, 1), :]
            sout[pl.ds(2 * r + j, 1), :] = mbuf[4 + i, r, pl.ds(lane, 1), :]


def stack_kernel(*refs):
    out = refs[-1]
    for i, ref in enumerate(refs[:-1]):
        out[i] = ref[...]


def gather_kernel(own, ahead, back, out):
    for refs, shifts in ((own, (1, 0, 7)), (ahead, (4, 3, 2)), (back, (6, 5))):
        for i, shift in enumerate(shifts):
            out[shift] = refs[i]


def join_kernel(own, recv, out):
    out[pl.ds(0, 24), :] = own[...]
    out[pl.ds(24, 24), :] = recv[...]


def near_sum_kernel(a, b, c, d, own, plus, minus):
    for ref, shifts in ((own, (7, 0, 1)), (plus, (2, 3, 4)), (minus, (5, 6))):
        for i, k in enumerate(shifts):
            total = (a[k].astype(F32) + b[k].astype(F32)) + (c[k].astype(F32) + d[k].astype(F32))
            ref[i] = total.astype(ref.dtype)


def middle_sum_kernel(own, plus, minus, down, stays, up):
    for i, ref in enumerate((down, stays, up)):
        total = own[i] + plus[i].astype(F32)
        if i > 0:
            total = total + minus[i - 1].astype(F32)
        ref[...] = total.astype(ref.dtype)


def sum_kernel(near, *refs):
    own, other, wide = refs[-3:]
    total = near[...]
    for ref in refs[:-3]:
        total = total + ref[...].astype(F32)
    wide[...] = total
    for o, out in enumerate((own, other)):
        for j in range(2):
            for r in range(12):
                out[pl.ds(2 * r + j, 1), :] = wide[pl.ds(24 * o + 12 * j + r, 1), :]


def adam_kernel(total_rows, meta, mine, theirs, wown, woth, fown, foth, sown, soth,
                new_w, new_f, new_s, wide):
    core = meta[1]
    count = jnp.where(core == 0, meta[2], meta[3])
    odd = (lax.broadcasted_iota(jnp.int32, mine.shape, 0) & 1) == 1
    same_first = jnp.where(picked(meta, 0, 0) == picked(meta, 1, 0), 1.0, 0.0)
    same_second = jnp.where(picked(meta, 0, 1) == picked(meta, 1, 1), 1.0, 0.0)
    same = jnp.where(odd, same_second, same_first) > 0.5
    live = jnp.where(odd, count, 2) == 2
    for k, (wref, fref, sref) in enumerate(((wown, fown, sown), (woth, foth, soth))):
        n = core if k == 0 else 1 - core
        grad, rest = (mine[...], theirs[...]) if k == 0 else (theirs[...], mine[...])
        grad = (grad + jnp.where(same, rest, jnp.zeros_like(rest))) / total_rows
        source = wref[...].astype(F32)
        for j in range(2):
            for r in range(12):
                wide[pl.ds(2 * r + j, 1), :] = source[12 * j + r : 12 * j + r + 1, :]
        weight, one, two = wide[...], fref[...], sref[...]
        next_one = first_decay * one + (1.0 - first_decay) * grad
        next_two = second_decay * two + (1.0 - second_decay) * grad * grad
        next_weight = weight - learn_rate * (next_one / first_bias) / (
            jnp.sqrt(next_two / second_bias) + adam_epsilon
        )
        out_w = jnp.where(live, next_weight, weight)
        out_f = jnp.where(live, next_one, one)
        out_s = jnp.where(live, next_two, two)
        for r in range(12):
            new_w[n, r] = out_w[2 * r : 2 * r + 2].astype(BF)
            new_f[n, r] = out_f[2 * r : 2 * r + 2]
            new_s[n, r] = out_s[2 * r : 2 * r + 2]


def body(images, cotangent, picks, section_sizes, kernels, weights, first_moment, second_moment):
    width = images.shape[-1]
    own_segment = lax.axis_index("segment")
    segments = lax.axis_size("segment")
    parts = lax.axis_size("dp")
    total_rows = images.shape[0] * images.shape[1] * images.shape[2] * parts
    swap = [(s, s ^ 1) for s in range(segments)]
    ahead = [(s, (s + 2) % segments) for s in range(segments)]
    behind = [(s, (s - 2) % segments) for s in range(segments)]

    def along(value, dz, dy):
        pairs = [
            (4 * z + y, 4 * ((z + dz) % 8) + (y + dy) % 4) for z in range(8) for y in range(4)
        ]
        return lax.ppermute(value, "dp", pairs)


    DMA = pltpu.SemaphoreType.DMA
    V = pltpu.VMEM
    state = (4, ROWS, width)
    flat_shape = (ROWS, width)
    s_pad = V((3, PADDED, LANES), F32)
    pair, square, tap_shape = (24, width), (4, width, width), (4, 25, width)

    core = own_segment & 1
    part = lax.axis_index("dp")
    place = lax.broadcasted_iota(jnp.int32, (10,), 0)
    early = jnp.pad(picks.reshape(4), (6, 0))
    for i, value in ((0, own_segment >> 1), (1, core), (4, part >> 2), (5, part & 3)):
        early = jnp.where(place == i, value, early)
    early = lax.optimization_barrier(early)

    wown, woth = call(
        weight_kernel,
        [(pair, BF), (pair, BF)],
        [SMEM, HBM],
        [V((4, 12, 8, width), BF), V((12, 8, width), F32), V((2, 24, width), F32), DMA((4,))],
        cost=1000,
    )(early, weights.transpose(0, 2, 1, 3))
    wrecv = lax.ppermute(woth, "segment", swap)
    (message,) = call(join_kernel, [((48, width), BF)], [VMEM, VMEM], [], cost=1000)(wown, wrecv)
    (triple,) = call(stack_kernel, [((3, 48, width), BF)], [VMEM] * 3, [], cost=1000)(
        along(message, 1, 0), message, along(message, 7, 0)
    )
    after, sizes, triple = lax.optimization_barrier((early, section_sizes, triple))
    (near,) = call(gather_kernel, [((8, 48, width), BF)], [VMEM] * 3, [], cost=1000)(
        triple, along(triple, 3, 0), along(triple, 5, 0)
    )
    kown, kother = call(
        tap_kernel,
        [((2, 25, width), BF)] * 2,
        [SMEM, HBM],
        [V((4, 25, 8, width), BF), V((25, 8, width), F32), V((25, width), F32), DMA((4,))],
    )(after, kernels.transpose(0, 2, 1, 3))
    koth = lax.ppermute(kother, "segment", swap)
    sizes_other = lax.ppermute(sizes, "segment", swap)
    near, koth, kown, sizes_other = lax.optimization_barrier((near, koth, kown, sizes_other))
    columns = {0: near}
    for dy in (2, 1, 3):
        columns[dy] = along(near, 0, dy)
    size_low = jnp.where(core == 0, section_sizes[0], sizes_other[0])
    size_high = jnp.where(core == 0, sizes_other[0], section_sizes[0])
    meta = jnp.where(place == 2, size_low, jnp.where(place == 3, size_high, early))
    edges = ((0, 0), (0, PITCH - SIDE), (0, 0))
    img = jnp.pad(images[0], edges).reshape(flat_shape)
    y, wall, taps, hs, ds = call(
        first_kernel,
        [(flat_shape, BF), (square, BF), (tap_shape, F32), (state, BF), (state, F32)],
        [SMEM] + [VMEM] * 7,
        [s_pad, V((4, 8, 48, width), BF)],
    )(meta, img, *[columns[i] for i in range(4)], kown, koth)
    y, late, cotangent = lax.optimization_barrier((y, early, cotangent))
    cur = lax.ppermute(y, "segment", ahead)
    chosen = lax.dynamic_index_in_dim(cotangent[:, 0], core, 0, keepdims=False)
    cot = jnp.pad(chosen, edges).reshape(flat_shape)
    fown, foth, sown, soth = call(
        moment_kernel,
        [(pair, F32)] * 4,
        [SMEM, HBM, HBM],
        [V((8, 12, 8, width), F32), DMA((8,))],
    )(late, first_moment.transpose(0, 2, 1, 3), second_moment.transpose(0, 2, 1, 3))
    cur, cot, fown = lax.optimization_barrier((cur, cot, fown))
    for step in (1, 2):
        y, hs, ds = call(
            functools.partial(forward_kernel, step),
            [(flat_shape, BF), (state, BF), (state, F32)],
            [SMEM] + [VMEM] * 5,
            [s_pad],
            {4: 1, 5: 2},
        )(meta, cur, wall, taps, hs, ds)
        cur = lax.ppermute(y, "segment", ahead)
    y, hs, ys, ds = call(
        functools.partial(middle_kernel, 3),
        [(flat_shape, BF), (state, BF), (state, BF), (state, F32)],
        [SMEM] + [VMEM] * 6,
        [s_pad],
        {5: 1, 6: 3},
    )(meta, cur, cot, wall, taps, hs, ds)
    cur = lax.ppermute(y, "segment", behind)
    for step in (2, 1):
        y, ys = call(
            functools.partial(backward_kernel, step),
            [(flat_shape, BF), (state, BF)],
            [SMEM] + [VMEM] * 5,
            [s_pad],
            {5: 1},
        )(meta, cur, wall, taps, ds, ys)
        cur = lax.ppermute(y, "segment", behind)
    column = (8, 48, width)
    *sends, _ = call(
        last_kernel,
        [(column, BF)] * 4 + [(state, BF)],
        [SMEM] + [VMEM] * 6,
        [V(flat_shape, BF), s_pad, V((2, width, width), F32), V((4, 8, 48, width), BF)],
        {6: 4},
    )(meta, cur, wall, taps, ds, hs, ys)
    came = [along(sends[dy], 0, dy) for dy in (2, 1, 3)]
    triple_shape, single = (3, 48, width), (48, width)
    inner, plus, minus = call(
        near_sum_kernel,
        [(triple_shape, F32), (triple_shape, BF), ((2, 48, width), BF)],
        [VMEM] * 4,
        [],
        cost=1000,
    )(sends[0], *came)
    down, stays, up = call(
        middle_sum_kernel, [(single, BF), (single, F32), (single, BF)], [VMEM] * 3, [], cost=1000
    )(inner, along(plus, 3, 0), along(minus, 5, 0))
    own, for_other = call(
        sum_kernel, [(pair, F32), (pair, F32)], [VMEM] * 3, [V((48, width), F32)], cost=1000
    )(stays, along(up, 1, 0), along(down, 7, 0))
    other = lax.ppermute(for_other, "segment", swap)
    rows = (2, 12, 2, width)
    news = call(
        functools.partial(adam_kernel, float(total_rows)),
        [(rows, BF), (rows, F32), (rows, F32)],
        [SMEM] + [VMEM] * 8,
        [V(pair, F32)],
    )(meta, own, other, wown, woth, fown, foth, sown, soth)
    return tuple(new.transpose(0, 2, 1, 3) for new in news)


def solution(mesh):
    return jax.shard_map(
        body,
        mesh=mesh,
        in_specs=(
            P("dp", None, None, None),
            P(None, "dp", None, None, None),
            P(None, "segment"),
            P("segment"),
            P("segment", None, None, None),
            P("segment", None, "dp", None),
            P("segment", None, "dp", None),
            P("segment", None, "dp", None),
        ),
        out_specs=(
            P(None, "segment", "dp", None),
            P(None, "segment", "dp", None),
            P(None, "segment", "dp", None),
        ),
        check_vma=False,
    )
```

```python
import functools

import jax
import jax.numpy as jnp
from jax import lax
from jax.experimental import pallas as pl
from jax.experimental.pallas import tpu as pltpu
from jax.sharding import PartitionSpec as P

first_decay = 0.9
second_decay = 0.999
learn_rate = 0.01
adam_epsilon = 1e-08
first_bias = 1.0 - 0.9**10
second_bias = 1.0 - 0.999**10

SIDE = 14
PITCH = 16
ROWS = SIDE * PITCH
LANES = 128
HEAD = 8 + 2 * PITCH
PADDED = 8 + (SIDE + 4) * PITCH + 8
BF = jnp.bfloat16
F32 = jnp.float32

HBM = pl.BlockSpec(memory_space=pltpu.HBM)
SMEM = pl.BlockSpec(memory_space=pltpu.SMEM)


VMEM = pl.BlockSpec(memory_space=pltpu.VMEM)


def call(kernel, outs, in_specs, scratch, aliases=None, cost=2_000_000_000, grant=8 << 20):
    return pl.pallas_call(
        kernel,
        out_shape=[jax.ShapeDtypeStruct(s, d) for s, d in outs],
        in_specs=in_specs,
        out_specs=[VMEM] * len(outs),
        scratch_shapes=scratch,
        input_output_aliases=aliases or {},
        compiler_params=pltpu.CompilerParams(vmem_limit_bytes=grant),
        cost_estimate=pl.CostEstimate(flops=cost, bytes_accessed=1_000_000, transcendentals=0),
    )


def keep_mask(shape):
    return (lax.broadcasted_iota(jnp.int32, shape, 0) & (PITCH - 1)) < SIDE


def shift_rows(pad, shifted, group):
    for e in range(-2, 3):
        for p in range(SIDE):
            rows = pl.ds(PITCH * p, PITCH)
            window = pad[group, pl.ds(HEAD + PITCH * p + e, PITCH), :]
            shifted[group, e + 2, rows, :] = window.astype(BF)


def conv_rows(shifted, taps, group, flipped, emit):
    sign = -1 if flipped else 1
    cols = pl.ds(group * LANES, LANES)
    weights = [
        jnp.broadcast_to(taps[pl.ds(i, 1), cols], (PITCH, LANES)).astype(BF) for i in range(25)
    ]
    for p in range(0, SIDE, 1):
        totals = [None] * 1
        for columns in ((-2, -1), (0,), (1, 2)):
            partial = [None] * 1
            for e in columns:
                for da in range(-2, 2 + 1):
                    if not 0 <= p + da < SIDE:
                        continue
                    window = shifted[group, e + 2, pl.ds(PITCH * (p + da), PITCH), :]
                    for k in range(1):
                        a = da - k
                        if -2 <= a <= 2:
                            tap = (sign * a + 2) * 5 + (sign * e + 2)
                            term = weights[tap] * window
                            partial[k] = term if partial[k] is None else partial[k] + term
            for k in range(1):
                wide = partial[k].astype(F32)
                totals[k] = wide if totals[k] is None else totals[k] + wide
        for k in range(1):
            emit(p + k, totals[k])


def clear_pad(pad):
    for g in range(3):
        pad[g, pl.ds(0, HEAD), :] = jnp.zeros((HEAD, LANES), F32)
        pad[g, pl.ds(HEAD + ROWS, PADDED - HEAD - ROWS), :] = jnp.zeros(
            (PADDED - HEAD - ROWS, LANES), F32
        )


def fill_pad(pad, value):
    for g in range(3):
        pad[g, pl.ds(HEAD, ROWS), :] = value[:, g * LANES : (g + 1) * LANES]


def live_of(meta, t):
    odd = (t & 1) == 1
    count = jnp.where(t < 2, meta[2], meta[3])
    return jnp.logical_or(jnp.logical_not(odd), count == 2)


def run_forward(meta, pad, shifted, flat, wall, taps, hs, ds, skip_last):
    last = jnp.where(meta[3] == 2, 3, 2)
    fill_pad(pad, flat[...].astype(F32))

    def slot(t, carry):
        @pl.when(live_of(meta, t))
        def _():
            early = None
            for g in range(3):
                if g == 2:
                    early = jnp.dot(
                        hs[t, :, pl.ds(0, 2 * LANES)],
                        wall[t, pl.ds(0, 2 * LANES), :],
                        preferred_element_type=F32,
                    )

                def emit(p, u, g=g):
                    rows, cols = pl.ds(p * PITCH, PITCH), pl.ds(g * LANES, LANES)
                    s = 0.5 * jnp.tanh(0.5 * u) + 0.5
                    us = u * s
                    hs[t, rows, cols] = us.astype(BF)
                    ds[t, rows, cols] = s * (1.0 + (u - us))

                shift_rows(pad, shifted, g)
                conv_rows(shifted, taps.at[t], g, False, emit)

            def update():
                value = early + jnp.dot(
                    hs[t, :, pl.ds(2 * LANES, LANES)],
                    wall[t, pl.ds(2 * LANES, LANES), :],
                    preferred_element_type=F32,
                )
                value = flat[...].astype(F32) + value
                rounded = jnp.where(keep_mask(value.shape), value, 0.0).astype(BF)
                flat[...] = rounded
                fill_pad(pad, rounded.astype(F32))

            if skip_last:
                pl.when(t != last)(update)
            else:
                update()

        return carry

    lax.fori_loop(0, 4, slot, 0)


def run_backward(meta, pad, shifted, flat, wall, taps, ds, ys, skip_first):
    def slot(i, carry):
        t = 3 - i

        @pl.when(live_of(meta, t))
        def _():
            ys[t] = flat[...]

            def chain():
                for g in range(3):
                    part = pl.ds(g * LANES, LANES)
                    dh = lax.dot_general(
                        ys[t], wall[t, part, :], (((1,), (1,)), ((), ())), preferred_element_type=F32
                    )
                    pad[g, pl.ds(HEAD, ROWS), :] = dh * ds[t, :, part]

                    def emit(p, total, g=g):
                        rows, cols = pl.ds(p * PITCH, PITCH), pl.ds(g * LANES, LANES)
                        value = ys[t, rows, cols].astype(F32) + total
                        keep = lax.broadcasted_iota(jnp.int32, value.shape, 0) < SIDE
                        flat[rows, cols] = jnp.where(keep, value, 0.0).astype(BF)

                    shift_rows(pad, shifted, g)
                    conv_rows(shifted, taps.at[t], g, True, emit)

            if skip_first:
                pl.when(t != 0)(chain)
            else:
                chain()

        return carry

    lax.fori_loop(0, 4, slot, 0)


def first_kernel(meta, img, *refs):
    columns, (kown, koth, y, wall, taps, hs, ds, pad, shifted, packed) = refs[:4], refs[4:]
    core, z, yy = meta[1], meta[4], meta[5]
    for i, ref in enumerate(columns):
        packed[(yy - i) & 3] = ref[...]
    for o, kref in enumerate((kown, koth)):
        for j in range(2):
            taps[(2 * o + j + 2 * core) & 3] = kref[j].astype(F32)
    for o in range(2):
        base = (2 * o + 2 * core) & 3
        place = pl.ds(24 * o, 24)
        for i in range(16):
            shift = (z - i // 2) & 7
            one = packed[2 * (i % 2), shift, place, :].astype(F32)
            two = packed[2 * (i % 2) + 1, shift, place, :].astype(F32)
            rows = pl.ds(24 * i, 24)
            wall[base, rows, :] = jnp.concatenate([one[:12], two[:12]], axis=0).astype(BF)
            wall[base + 1, rows, :] = jnp.concatenate([one[12:], two[12:]], axis=0).astype(BF)

    @pl.when(meta[0] == 0)
    def _():
        clear_pad(pad)
        y[...] = img[...]
        run_forward(meta, pad, shifted, y, wall, taps, hs, ds, False)


def forward_kernel(step, meta, cur, wall, taps, hin, din, y, hs, ds, pad, shifted):
    del hin, din

    @pl.when(meta[0] == step)
    def _():
        clear_pad(pad)
        y[...] = cur[...]
        run_forward(meta, pad, shifted, y, wall, taps, hs, ds, False)


def middle_kernel(step, meta, cur, cot, wall, taps, hin, din, y, hs, ys, ds, pad, shifted):
    del hin, din

    @pl.when(meta[0] == step)
    def _():
        clear_pad(pad)
        y[...] = cur[...]
        run_forward(meta, pad, shifted, y, wall, taps, hs, ds, True)
        y[...] = cot[...]
        run_backward(meta, pad, shifted, y, wall, taps, ds, ys, False)


def backward_kernel(step, meta, cur, wall, taps, ds, yin, y, ys, pad, shifted):
    del yin

    @pl.when(meta[0] == step)
    def _():
        clear_pad(pad)
        y[...] = cur[...]
        run_backward(meta, pad, shifted, y, wall, taps, ds, ys, False)


def last_kernel(meta, cur, wall, taps, ds, hs, yin, near, ahead1, ahead2, ahead3, ys,
                flat, pad, shifted, total, send):
    del yin
    core, z, yy = meta[1], meta[4], meta[5]

    @pl.when(meta[0] == 0)
    def _():
        clear_pad(pad)
        flat[...] = cur[...]
        run_backward(meta, pad, shifted, flat, wall, taps, ds, ys, True)

    def term(t):
        return lax.dot_general(
            hs[t], ys[t], (((0,), (0,)), ((), ())), preferred_element_type=F32
        )

    for o in range(2):
        base = (2 * o + 2 * core) & 3
        live = live_of(meta, base + 1)
        total[0] = term(base)

        @pl.when(live)
        def _():
            total[1] = term(base + 1)

        @pl.when(jnp.logical_not(live))
        def _():
            total[1] = jnp.zeros(total.shape[1:], F32)

        for i in range(16):
            rows = pl.ds(24 * i, 24)
            one, two = total[0, rows, :], total[1, rows, :]
            place = pl.ds(24 * o, 24)
            shift = (i // 2 - z) & 7
            send[2 * (i % 2), shift, place, :] = jnp.concatenate(
                [one[:12], two[:12]], axis=0
            ).astype(BF)
            send[2 * (i % 2) + 1, shift, place, :] = jnp.concatenate(
                [one[12:], two[12:]], axis=0
            ).astype(BF)
    for shift, ref in enumerate((near, ahead1, ahead2, ahead3)):
        ref[...] = send[(yy + shift) & 3]


def picked(meta, n, j):
    return meta[6 + 2 * n + j]


def weight_kernel(meta, weights, own, oth, buf, wide, rows, sems):
    core = meta[1]
    copies = []
    for k, out in enumerate((own, oth)):
        for j in range(2):
            op = picked(meta, core if k == 0 else 1 - core, j)
            group = pl.ds(pl.multiple_of((op >> 3) << 3, 8), 8)
            copies.append(
                pltpu.make_async_copy(
                    weights.at[j, :, group, :], buf.at[2 * k + j], sems.at[2 * k + j]
                )
            )
            copies[-1].start()
    for k, out in enumerate((own, oth)):
        for j in range(2):
            op = picked(meta, core if k == 0 else 1 - core, j)
            copies[2 * k + j].wait()
            wide[...] = buf[2 * k + j].astype(F32)
            for r in range(12):
                rows[k, pl.ds(12 * j + r, 1), :] = wide[r, pl.ds(op & 7, 1), :]
        out[...] = rows[k].astype(BF)


def tap_kernel(meta, kernels, kown, koth, kbuf, kwide, krows, sems):
    core = meta[1]
    copies = []
    for k in range(2):
        for j in range(2):
            op = picked(meta, core if k == 0 else 1 - core, j)
            group = pl.ds(pl.multiple_of((op >> 3) << 3, 8), 8)
            i = 2 * k + j
            copies.append(
                pltpu.make_async_copy(kernels.at[j, :, group, :], kbuf.at[i], sems.at[i])
            )
            copies[-1].start()
    for k, out in enumerate((kown, koth)):
        for j in range(2):
            lane = picked(meta, core if k == 0 else 1 - core, j) & 7
            copies[2 * k + j].wait()
            kwide[...] = kbuf[2 * k + j].astype(F32)
            for r in range(25):
                krows[pl.ds(r, 1), :] = kwide[r, pl.ds(lane, 1), :]
            out[j] = krows[...].astype(BF)


def moment_kernel(meta, first, second, fown, foth, sown, soth, mbuf, sems):
    core = meta[1]
    chosen = []
    for k, (fout, sout) in enumerate(((fown, sown), (foth, soth))):
        for j in range(2):
            op = picked(meta, core if k == 0 else 1 - core, j)
            group = pl.ds(pl.multiple_of((op >> 3) << 3, 8), 8)
            i = 2 * k + j
            copies = [
                pltpu.make_async_copy(first.at[j, :, group, :], mbuf.at[i], sems.at[i]),
                pltpu.make_async_copy(second.at[j, :, group, :], mbuf.at[4 + i], sems.at[4 + i]),
            ]
            chosen.append((copies, op & 7, fout, sout, i, j))
            for c in copies:
                c.start()
    for copies, lane, fout, sout, i, j in chosen:
        for c in copies:
            c.wait()
        for r in range(12):
            fout[pl.ds(2 * r + j, 1), :] = mbuf[i, r, pl.ds(lane, 1), :]
            sout[pl.ds(2 * r + j, 1), :] = mbuf[4 + i, r, pl.ds(lane, 1), :]


def stack_kernel(*refs):
    out = refs[-1]
    for i, ref in enumerate(refs[:-1]):
        out[i] = ref[...]


def gather_kernel(own, ahead, back, out):
    for refs, shifts in ((own, (1, 0, 7)), (ahead, (4, 3, 2)), (back, (6, 5))):
        for i, shift in enumerate(shifts):
            out[shift] = refs[i]


def join_kernel(own, recv, out):
    out[pl.ds(0, 24), :] = own[...]
    out[pl.ds(24, 24), :] = recv[...]


def near_sum_kernel(a, b, c, d, own, plus, minus):
    for ref, shifts in ((own, (7, 0, 1)), (plus, (2, 3, 4)), (minus, (5, 6))):
        for i, k in enumerate(shifts):
            total = (a[k].astype(F32) + b[k].astype(F32)) + (c[k].astype(F32) + d[k].astype(F32))
            ref[i] = total.astype(ref.dtype)


def middle_sum_kernel(own, plus, minus, down, stays, up):
    for i, ref in enumerate((down, stays, up)):
        total = own[i] + plus[i].astype(F32)
        if i > 0:
            total = total + minus[i - 1].astype(F32)
        ref[...] = total.astype(ref.dtype)


def sum_kernel(near, *refs):
    own, other, wide = refs[-3:]
    total = near[...]
    for ref in refs[:-3]:
        total = total + ref[...].astype(F32)
    wide[...] = total
    for o, out in enumerate((own, other)):
        for j in range(2):
            for r in range(12):
                out[pl.ds(2 * r + j, 1), :] = wide[pl.ds(24 * o + 12 * j + r, 1), :]


def adam_kernel(total_rows, meta, mine, theirs, wown, woth, fown, foth, sown, soth,
                new_w, new_f, new_s, wide):
    core = meta[1]
    count = jnp.where(core == 0, meta[2], meta[3])
    odd = (lax.broadcasted_iota(jnp.int32, mine.shape, 0) & 1) == 1
    same_first = jnp.where(picked(meta, 0, 0) == picked(meta, 1, 0), 1.0, 0.0)
    same_second = jnp.where(picked(meta, 0, 1) == picked(meta, 1, 1), 1.0, 0.0)
    same = jnp.where(odd, same_second, same_first) > 0.5
    live = jnp.where(odd, count, 2) == 2
    for k, (wref, fref, sref) in enumerate(((wown, fown, sown), (woth, foth, soth))):
        n = core if k == 0 else 1 - core
        grad, rest = (mine[...], theirs[...]) if k == 0 else (theirs[...], mine[...])
        grad = (grad + jnp.where(same, rest, jnp.zeros_like(rest))) / total_rows
        source = wref[...].astype(F32)
        for j in range(2):
            for r in range(12):
                wide[pl.ds(2 * r + j, 1), :] = source[12 * j + r : 12 * j + r + 1, :]
        weight, one, two = wide[...], fref[...], sref[...]
        next_one = first_decay * one + (1.0 - first_decay) * grad
        next_two = second_decay * two + (1.0 - second_decay) * grad * grad
        next_weight = weight - learn_rate * (next_one / first_bias) / (
            jnp.sqrt(next_two / second_bias) + adam_epsilon
        )
        out_w = jnp.where(live, next_weight, weight)
        out_f = jnp.where(live, next_one, one)
        out_s = jnp.where(live, next_two, two)
        for r in range(12):
            new_w[n, r] = out_w[2 * r : 2 * r + 2].astype(BF)
            new_f[n, r] = out_f[2 * r : 2 * r + 2]
            new_s[n, r] = out_s[2 * r : 2 * r + 2]


def body(images, cotangent, picks, section_sizes, kernels, weights, first_moment, second_moment):
    width = images.shape[-1]
    own_segment = lax.axis_index("segment")
    segments = lax.axis_size("segment")
    parts = lax.axis_size("dp")
    total_rows = images.shape[0] * images.shape[1] * images.shape[2] * parts
    swap = [(s, s ^ 1) for s in range(segments)]
    ahead = [(s, (s + 2) % segments) for s in range(segments)]
    behind = [(s, (s - 2) % segments) for s in range(segments)]

    def along(value, dz, dy):
        pairs = [
            (4 * z + y, 4 * ((z + dz) % 8) + (y + dy) % 4) for z in range(8) for y in range(4)
        ]
        return lax.ppermute(value, "dp", pairs)


    DMA = pltpu.SemaphoreType.DMA
    V = pltpu.VMEM
    state = (4, ROWS, width)
    flat_shape = (ROWS, width)
    s_pad = V((3, PADDED, LANES), F32)
    s_shift = V((3, 5, ROWS, LANES), BF)
    pair, square, tap_shape = (24, width), (4, width, width), (4, 25, width)

    core = own_segment & 1
    part = lax.axis_index("dp")
    place = lax.broadcasted_iota(jnp.int32, (10,), 0)
    early = jnp.pad(picks.reshape(4), (6, 0))
    for i, value in ((0, own_segment >> 1), (1, core), (4, part >> 2), (5, part & 3)):
        early = jnp.where(place == i, value, early)
    early = lax.optimization_barrier(early)

    wown, woth = call(
        weight_kernel,
        [(pair, BF), (pair, BF)],
        [SMEM, HBM],
        [V((4, 12, 8, width), BF), V((12, 8, width), F32), V((2, 24, width), F32), DMA((4,))],
        cost=1000,
    )(early, weights.transpose(0, 2, 1, 3))
    wrecv = lax.ppermute(woth, "segment", swap)
    (message,) = call(join_kernel, [((48, width), BF)], [VMEM, VMEM], [], cost=1000)(wown, wrecv)
    (triple,) = call(stack_kernel, [((3, 48, width), BF)], [VMEM] * 3, [], cost=1000)(
        along(message, 1, 0), message, along(message, 7, 0)
    )
    after, sizes, triple = lax.optimization_barrier((early, section_sizes, triple))
    (near,) = call(gather_kernel, [((8, 48, width), BF)], [VMEM] * 3, [], cost=1000)(
        triple, along(triple, 3, 0), along(triple, 5, 0)
    )
    kown, kother = call(
        tap_kernel,
        [((2, 25, width), BF)] * 2,
        [SMEM, HBM],
        [V((4, 25, 8, width), BF), V((25, 8, width), F32), V((25, width), F32), DMA((4,))],
    )(after, kernels.transpose(0, 2, 1, 3))
    koth = lax.ppermute(kother, "segment", swap)
    sizes_other = lax.ppermute(sizes, "segment", swap)
    near, koth, kown, sizes_other = lax.optimization_barrier((near, koth, kown, sizes_other))
    columns = {0: near}
    for dy in (2, 1, 3):
        columns[dy] = along(near, 0, dy)
    size_low = jnp.where(core == 0, section_sizes[0], sizes_other[0])
    size_high = jnp.where(core == 0, sizes_other[0], section_sizes[0])
    meta = jnp.where(place == 2, size_low, jnp.where(place == 3, size_high, early))
    edges = ((0, 0), (0, PITCH - SIDE), (0, 0))
    img = jnp.pad(images[0], edges).reshape(flat_shape)
    y, wall, taps, hs, ds = call(
        first_kernel,
        [(flat_shape, BF), (square, BF), (tap_shape, F32), (state, BF), (state, F32)],
        [SMEM] + [VMEM] * 7,
        [s_pad, s_shift, V((4, 8, 48, width), BF)],
    )(meta, img, *[columns[i] for i in range(4)], kown, koth)
    y, late, cotangent = lax.optimization_barrier((y, early, cotangent))
    cur = lax.ppermute(y, "segment", ahead)
    chosen = lax.dynamic_index_in_dim(cotangent[:, 0], core, 0, keepdims=False)
    cot = jnp.pad(chosen, edges).reshape(flat_shape)
    fown, foth, sown, soth = call(
        moment_kernel,
        [(pair, F32)] * 4,
        [SMEM, HBM, HBM],
        [V((8, 12, 8, width), F32), DMA((8,))],
    )(late, first_moment.transpose(0, 2, 1, 3), second_moment.transpose(0, 2, 1, 3))
    cur, cot, fown = lax.optimization_barrier((cur, cot, fown))
    for step in (1, 2):
        y, hs, ds = call(
            functools.partial(forward_kernel, step),
            [(flat_shape, BF), (state, BF), (state, F32)],
            [SMEM] + [VMEM] * 5,
            [s_pad, s_shift],
            {4: 1, 5: 2},
        )(meta, cur, wall, taps, hs, ds)
        cur = lax.ppermute(y, "segment", ahead)
    y, hs, ys, ds = call(
        functools.partial(middle_kernel, 3),
        [(flat_shape, BF), (state, BF), (state, BF), (state, F32)],
        [SMEM] + [VMEM] * 6,
        [s_pad, s_shift],
        {5: 1, 6: 3},
    )(meta, cur, cot, wall, taps, hs, ds)
    cur = lax.ppermute(y, "segment", behind)
    for step in (2, 1):
        y, ys = call(
            functools.partial(backward_kernel, step),
            [(flat_shape, BF), (state, BF)],
            [SMEM] + [VMEM] * 5,
            [s_pad, s_shift],
            {5: 1},
        )(meta, cur, wall, taps, ds, ys)
        cur = lax.ppermute(y, "segment", behind)
    column = (8, 48, width)
    *sends, _ = call(
        last_kernel,
        [(column, BF)] * 4 + [(state, BF)],
        [SMEM] + [VMEM] * 6,
        [V(flat_shape, BF), s_pad, s_shift, V((2, width, width), F32), V((4, 8, 48, width), BF)],
        {6: 4},
    )(meta, cur, wall, taps, ds, hs, ys)
    came = [along(sends[dy], 0, dy) for dy in (2, 1, 3)]
    triple_shape, single = (3, 48, width), (48, width)
    inner, plus, minus = call(
        near_sum_kernel,
        [(triple_shape, F32), (triple_shape, BF), ((2, 48, width), BF)],
        [VMEM] * 4,
        [],
        cost=1000,
    )(sends[0], *came)
    down, stays, up = call(
        middle_sum_kernel, [(single, BF), (single, F32), (single, BF)], [VMEM] * 3, [], cost=1000
    )(inner, along(plus, 3, 0), along(minus, 5, 0))
    own, for_other = call(
        sum_kernel, [(pair, F32), (pair, F32)], [VMEM] * 3, [V((48, width), F32)], cost=1000
    )(stays, along(up, 1, 0), along(down, 7, 0))
    other = lax.ppermute(for_other, "segment", swap)
    rows = (2, 12, 2, width)
    news = call(
        functools.partial(adam_kernel, float(total_rows)),
        [(rows, BF), (rows, F32), (rows, F32)],
        [SMEM] + [VMEM] * 8,
        [V(pair, F32)],
    )(meta, own, other, wown, woth, fown, foth, sown, soth)
    return tuple(new.transpose(0, 2, 1, 3) for new in news)


def solution(mesh):
    return jax.shard_map(
        body,
        mesh=mesh,
        in_specs=(
            P("dp", None, None, None),
            P(None, "dp", None, None, None),
            P(None, "segment"),
            P("segment"),
            P("segment", None, None, None),
            P("segment", None, "dp", None),
            P("segment", None, "dp", None),
            P("segment", None, "dp", None),
        ),
        out_specs=(
            P(None, "segment", "dp", None),
            P(None, "segment", "dp", None),
            P(None, "segment", "dp", None),
        ),
        check_vma=False,
    )
```

```python
import functools

import jax
import jax.numpy as jnp
from jax import lax
from jax.experimental import pallas as pl
from jax.experimental.pallas import tpu as pltpu
from jax.sharding import PartitionSpec as P

first_decay = 0.9
second_decay = 0.999
learn_rate = 0.01
adam_epsilon = 1e-08
first_bias = 1.0 - 0.9**10
second_bias = 1.0 - 0.999**10

SIDE = 14
PITCH = 16
ROWS = SIDE * PITCH
LANES = 128
HEAD = 8 + 2 * PITCH
PADDED = 8 + (SIDE + 4) * PITCH + 8
BF = jnp.bfloat16
F32 = jnp.float32

HBM = pl.BlockSpec(memory_space=pltpu.HBM)
SMEM = pl.BlockSpec(memory_space=pltpu.SMEM)


VMEM = pl.BlockSpec(memory_space=pltpu.VMEM)


def call(kernel, outs, in_specs, scratch, aliases=None, cost=2_000_000_000, grant=8 << 20):
    return pl.pallas_call(
        kernel,
        out_shape=[jax.ShapeDtypeStruct(s, d) for s, d in outs],
        in_specs=in_specs,
        out_specs=[VMEM] * len(outs),
        scratch_shapes=scratch,
        input_output_aliases=aliases or {},
        compiler_params=pltpu.CompilerParams(vmem_limit_bytes=grant),
        cost_estimate=pl.CostEstimate(flops=cost, bytes_accessed=1_000_000, transcendentals=0),
    )


def keep_mask(shape):
    return (lax.broadcasted_iota(jnp.int32, shape, 0) & (PITCH - 1)) < SIDE


def shift_rows(pad, shifted, group):
    for e in range(-2, 3):
        for p in range(SIDE):
            rows = pl.ds(PITCH * p, PITCH)
            window = pad[group, pl.ds(HEAD + PITCH * p + e, PITCH), :]
            shifted[group, e + 2, rows, :] = window.astype(BF)


def conv_rows(shifted, taps, group, flipped, emit):
    sign = -1 if flipped else 1
    cols = pl.ds(group * LANES, LANES)
    weights = [
        jnp.broadcast_to(taps[pl.ds(i, 1), cols], (PITCH, LANES)).astype(BF) for i in range(25)
    ]
    for p in range(0, SIDE, 1):
        totals = [None] * 1
        for columns in ((-2, -1), (0,), (1, 2)):
            partial = [None] * 1
            for e in columns:
                for da in range(-2, 2 + 1):
                    if not 0 <= p + da < SIDE:
                        continue
                    window = shifted[group, e + 2, pl.ds(PITCH * (p + da), PITCH), :]
                    for k in range(1):
                        a = da - k
                        if -2 <= a <= 2:
                            tap = (sign * a + 2) * 5 + (sign * e + 2)
                            term = weights[tap] * window
                            partial[k] = term if partial[k] is None else partial[k] + term
            for k in range(1):
                wide = partial[k].astype(F32)
                totals[k] = wide if totals[k] is None else totals[k] + wide
        for k in range(1):
            emit(p + k, totals[k])


def clear_pad(pad):
    for g in range(3):
        pad[g, pl.ds(0, HEAD), :] = jnp.zeros((HEAD, LANES), F32)
        pad[g, pl.ds(HEAD + ROWS, PADDED - HEAD - ROWS), :] = jnp.zeros(
            (PADDED - HEAD - ROWS, LANES), F32
        )


def fill_pad(pad, value):
    for g in range(3):
        pad[g, pl.ds(HEAD, ROWS), :] = value[:, g * LANES : (g + 1) * LANES]


def live_of(meta, t):
    odd = (t & 1) == 1
    count = jnp.where(t < 2, meta[2], meta[3])
    return jnp.logical_or(jnp.logical_not(odd), count == 2)


def run_forward(meta, pad, shifted, flat, wall, taps, hs, ds, skip_last):
    last = jnp.where(meta[3] == 2, 3, 2)
    fill_pad(pad, flat[...].astype(F32))

    def slot(t, carry):
        @pl.when(live_of(meta, t))
        def _():
            early = None
            for g in range(3):
                if g == 2:
                    early = jnp.dot(
                        hs[t, :, pl.ds(0, 2 * LANES)],
                        wall[t, pl.ds(0, 2 * LANES), :],
                        preferred_element_type=F32,
                    )

                def emit(p, u, g=g):
                    rows, cols = pl.ds(p * PITCH, PITCH), pl.ds(g * LANES, LANES)
                    s = 0.5 * jnp.tanh(0.5 * u) + 0.5
                    us = u * s
                    hs[t, rows, cols] = us.astype(BF)
                    ds[t, rows, cols] = s * (1.0 + (u - us))

                shift_rows(pad, shifted, g)
                conv_rows(shifted, taps.at[t], g, False, emit)

            def update():
                value = early + jnp.dot(
                    hs[t, :, pl.ds(2 * LANES, LANES)],
                    wall[t, pl.ds(2 * LANES, LANES), :],
                    preferred_element_type=F32,
                )
                value = flat[...].astype(F32) + value
                rounded = jnp.where(keep_mask(value.shape), value, 0.0).astype(BF)
                flat[...] = rounded
                fill_pad(pad, rounded.astype(F32))

            if skip_last:
                pl.when(t != last)(update)
            else:
                update()

        return carry

    lax.fori_loop(0, 4, slot, 0)


def run_backward(meta, pad, shifted, flat, wall, taps, ds, ys, skip_first):
    def slot(i, carry):
        t = 3 - i

        @pl.when(live_of(meta, t))
        def _():
            ys[t] = flat[...]

            def chain():
                for g in range(3):
                    part = pl.ds(g * LANES, LANES)
                    dh = lax.dot_general(
                        ys[t], wall[t, part, :], (((1,), (1,)), ((), ())), preferred_element_type=F32
                    )
                    pad[g, pl.ds(HEAD, ROWS), :] = dh * ds[t, :, part]

                    def emit(p, total, g=g):
                        rows, cols = pl.ds(p * PITCH, PITCH), pl.ds(g * LANES, LANES)
                        value = ys[t, rows, cols].astype(F32) + total
                        keep = lax.broadcasted_iota(jnp.int32, value.shape, 0) < SIDE
                        flat[rows, cols] = jnp.where(keep, value, 0.0).astype(BF)

                    shift_rows(pad, shifted, g)
                    conv_rows(shifted, taps.at[t], g, True, emit)

            if skip_first:
                pl.when(t != 0)(chain)
            else:
                chain()

        return carry

    lax.fori_loop(0, 4, slot, 0)


def first_kernel(meta, img, *refs):
    inner, outer, (kown, koth, y, wall, taps, hs, ds, pad, shifted, packed) = refs[:4], refs[4:8], refs[8:]
    core, z, yy = meta[1], meta[4], meta[5]
    for i in range(4):
        row = (yy - i) & 3
        for k, shift in enumerate((1, 0, 7)):
            packed[row, shift] = inner[i][k]
        packed[row, pl.ds(2, 5)] = outer[i][...]
    for o, kref in enumerate((kown, koth)):
        for j in range(2):
            taps[(2 * o + j + 2 * core) & 3] = kref[j].astype(F32)
    for o in range(2):
        base = (2 * o + 2 * core) & 3
        place = pl.ds(24 * o, 24)
        for i in range(16):
            shift = (z - i // 2) & 7
            one = packed[2 * (i % 2), shift, place, :].astype(F32)
            two = packed[2 * (i % 2) + 1, shift, place, :].astype(F32)
            rows = pl.ds(24 * i, 24)
            wall[base, rows, :] = jnp.concatenate([one[:12], two[:12]], axis=0).astype(BF)
            wall[base + 1, rows, :] = jnp.concatenate([one[12:], two[12:]], axis=0).astype(BF)

    @pl.when(meta[0] == 0)
    def _():
        clear_pad(pad)
        y[...] = img[...]
        run_forward(meta, pad, shifted, y, wall, taps, hs, ds, False)


def forward_kernel(step, meta, cur, wall, taps, hin, din, y, hs, ds, pad, shifted):
    del hin, din

    @pl.when(meta[0] == step)
    def _():
        clear_pad(pad)
        y[...] = cur[...]
        run_forward(meta, pad, shifted, y, wall, taps, hs, ds, False)


def middle_kernel(step, meta, cur, cot, wall, taps, hin, din, y, hs, ys, ds, pad, shifted):
    del hin, din

    @pl.when(meta[0] == step)
    def _():
        clear_pad(pad)
        y[...] = cur[...]
        run_forward(meta, pad, shifted, y, wall, taps, hs, ds, True)
        y[...] = cot[...]
        run_backward(meta, pad, shifted, y, wall, taps, ds, ys, False)


def backward_kernel(step, meta, cur, wall, taps, ds, yin, y, ys, pad, shifted):
    del yin

    @pl.when(meta[0] == step)
    def _():
        clear_pad(pad)
        y[...] = cur[...]
        run_backward(meta, pad, shifted, y, wall, taps, ds, ys, False)


def last_kernel(meta, cur, wall, taps, ds, hs, yin, inner0, inner1, inner2, inner3,
                outer0, outer1, outer2, outer3, ys, flat, pad, shifted, total, send):
    del yin
    core, z, yy = meta[1], meta[4], meta[5]

    @pl.when(meta[0] == 0)
    def _():
        clear_pad(pad)
        flat[...] = cur[...]
        run_backward(meta, pad, shifted, flat, wall, taps, ds, ys, True)

    def term(t):
        return lax.dot_general(
            hs[t], ys[t], (((0,), (0,)), ((), ())), preferred_element_type=F32
        )

    for o in range(2):
        base = (2 * o + 2 * core) & 3
        live = live_of(meta, base + 1)
        total[0] = term(base)

        @pl.when(live)
        def _():
            total[1] = term(base + 1)

        @pl.when(jnp.logical_not(live))
        def _():
            total[1] = jnp.zeros(total.shape[1:], F32)

        for i in range(16):
            rows = pl.ds(24 * i, 24)
            one, two = total[0, rows, :], total[1, rows, :]
            place = pl.ds(24 * o, 24)
            shift = (i // 2 - z) & 7
            send[2 * (i % 2), shift, place, :] = jnp.concatenate(
                [one[:12], two[:12]], axis=0
            ).astype(BF)
            send[2 * (i % 2) + 1, shift, place, :] = jnp.concatenate(
                [one[12:], two[12:]], axis=0
            ).astype(BF)
    for i, (inner, outer) in enumerate(
        ((inner0, outer0), (inner1, outer1), (inner2, outer2), (inner3, outer3))
    ):
        row = (yy + i) & 3
        for k, shift in enumerate((7, 0, 1)):
            inner[k] = send[row, shift]
        outer[...] = send[row, pl.ds(2, 5)]


def picked(meta, n, j):
    return meta[6 + 2 * n + j]


def weight_kernel(meta, weights, own, oth, buf, wide, rows, sems):
    core = meta[1]
    copies = []
    for k, out in enumerate((own, oth)):
        for j in range(2):
            op = picked(meta, core if k == 0 else 1 - core, j)
            group = pl.ds(pl.multiple_of((op >> 3) << 3, 8), 8)
            copies.append(
                pltpu.make_async_copy(
                    weights.at[j, :, group, :], buf.at[2 * k + j], sems.at[2 * k + j]
                )
            )
            copies[-1].start()
    for k, out in enumerate((own, oth)):
        for j in range(2):
            op = picked(meta, core if k == 0 else 1 - core, j)
            copies[2 * k + j].wait()
            wide[...] = buf[2 * k + j].astype(F32)
            for r in range(12):
                rows[k, pl.ds(12 * j + r, 1), :] = wide[r, pl.ds(op & 7, 1), :]
        out[...] = rows[k].astype(BF)


def tap_kernel(meta, kernels, kown, koth, kbuf, kwide, krows, sems):
    core = meta[1]
    copies = []
    for k in range(2):
        for j in range(2):
            op = picked(meta, core if k == 0 else 1 - core, j)
            group = pl.ds(pl.multiple_of((op >> 3) << 3, 8), 8)
            i = 2 * k + j
            copies.append(
                pltpu.make_async_copy(kernels.at[j, :, group, :], kbuf.at[i], sems.at[i])
            )
            copies[-1].start()
    for k, out in enumerate((kown, koth)):
        for j in range(2):
            lane = picked(meta, core if k == 0 else 1 - core, j) & 7
            copies[2 * k + j].wait()
            kwide[...] = kbuf[2 * k + j].astype(F32)
            for r in range(25):
                krows[pl.ds(r, 1), :] = kwide[r, pl.ds(lane, 1), :]
            out[j] = krows[...].astype(BF)


def moment_kernel(meta, first, second, fown, foth, sown, soth, mbuf, sems):
    core = meta[1]
    chosen = []
    for k, (fout, sout) in enumerate(((fown, sown), (foth, soth))):
        for j in range(2):
            op = picked(meta, core if k == 0 else 1 - core, j)
            group = pl.ds(pl.multiple_of((op >> 3) << 3, 8), 8)
            i = 2 * k + j
            copies = [
                pltpu.make_async_copy(first.at[j, :, group, :], mbuf.at[i], sems.at[i]),
                pltpu.make_async_copy(second.at[j, :, group, :], mbuf.at[4 + i], sems.at[4 + i]),
            ]
            chosen.append((copies, op & 7, fout, sout, i, j))
            for c in copies:
                c.start()
    for copies, lane, fout, sout, i, j in chosen:
        for c in copies:
            c.wait()
        for r in range(12):
            fout[pl.ds(2 * r + j, 1), :] = mbuf[i, r, pl.ds(lane, 1), :]
            sout[pl.ds(2 * r + j, 1), :] = mbuf[4 + i, r, pl.ds(lane, 1), :]


def stack_kernel(*refs):
    out = refs[-1]
    for i, ref in enumerate(refs[:-1]):
        out[i] = ref[...]


def gather_kernel(ahead, back, out):
    for refs, shifts in ((ahead, (4, 3, 2)), (back, (6, 5))):
        for i, shift in enumerate(shifts):
            out[shift - 2] = refs[i]


def join_kernel(own, recv, out):
    out[pl.ds(0, 24), :] = own[...]
    out[pl.ds(24, 24), :] = recv[...]


def four(refs, i):
    a, b, c, d = refs
    return (a[i].astype(F32) + b[i].astype(F32)) + (c[i].astype(F32) + d[i].astype(F32))


def outer_sum_kernel(a, b, c, d, plus, minus):
    for i in range(5):
        ref = plus if i < 3 else minus
        ref[i % 3] = four((a, b, c, d), i).astype(ref.dtype)


def inner_sum_kernel(a, b, c, d, plus, minus, down, stays, up):
    for i, ref in enumerate((down, stays, up)):
        total = four((a, b, c, d), i) + plus[i].astype(F32)
        if i > 0:
            total = total + minus[i - 1].astype(F32)
        ref[...] = total.astype(ref.dtype)


def sum_kernel(near, *refs):
    own, other, wide = refs[-3:]
    total = near[...]
    for ref in refs[:-3]:
        total = total + ref[...].astype(F32)
    wide[...] = total
    for o, out in enumerate((own, other)):
        for j in range(2):
            for r in range(12):
                out[pl.ds(2 * r + j, 1), :] = wide[pl.ds(24 * o + 12 * j + r, 1), :]


def adam_kernel(total_rows, meta, mine, theirs, wown, woth, fown, foth, sown, soth,
                new_w, new_f, new_s, wide):
    core = meta[1]
    count = jnp.where(core == 0, meta[2], meta[3])
    odd = (lax.broadcasted_iota(jnp.int32, mine.shape, 0) & 1) == 1
    same_first = jnp.where(picked(meta, 0, 0) == picked(meta, 1, 0), 1.0, 0.0)
    same_second = jnp.where(picked(meta, 0, 1) == picked(meta, 1, 1), 1.0, 0.0)
    same = jnp.where(odd, same_second, same_first) > 0.5
    live = jnp.where(odd, count, 2) == 2
    for k, (wref, fref, sref) in enumerate(((wown, fown, sown), (woth, foth, soth))):
        n = core if k == 0 else 1 - core
        grad, rest = (mine[...], theirs[...]) if k == 0 else (theirs[...], mine[...])
        grad = (grad + jnp.where(same, rest, jnp.zeros_like(rest))) / total_rows
        source = wref[...].astype(F32)
        for j in range(2):
            for r in range(12):
                wide[pl.ds(2 * r + j, 1), :] = source[12 * j + r : 12 * j + r + 1, :]
        weight, one, two = wide[...], fref[...], sref[...]
        next_one = first_decay * one + (1.0 - first_decay) * grad
        next_two = second_decay * two + (1.0 - second_decay) * grad * grad
        next_weight = weight - learn_rate * (next_one / first_bias) / (
            jnp.sqrt(next_two / second_bias) + adam_epsilon
        )
        out_w = jnp.where(live, next_weight, weight)
        out_f = jnp.where(live, next_one, one)
        out_s = jnp.where(live, next_two, two)
        for r in range(12):
            new_w[n, r] = out_w[2 * r : 2 * r + 2].astype(BF)
            new_f[n, r] = out_f[2 * r : 2 * r + 2]
            new_s[n, r] = out_s[2 * r : 2 * r + 2]


def body(images, cotangent, picks, section_sizes, kernels, weights, first_moment, second_moment):
    width = images.shape[-1]
    own_segment = lax.axis_index("segment")
    segments = lax.axis_size("segment")
    parts = lax.axis_size("dp")
    total_rows = images.shape[0] * images.shape[1] * images.shape[2] * parts
    swap = [(s, s ^ 1) for s in range(segments)]
    ahead = [(s, (s + 2) % segments) for s in range(segments)]
    behind = [(s, (s - 2) % segments) for s in range(segments)]

    def along(value, dz, dy):
        pairs = [
            (4 * z + y, 4 * ((z + dz) % 8) + (y + dy) % 4) for z in range(8) for y in range(4)
        ]
        return lax.ppermute(value, "dp", pairs)


    DMA = pltpu.SemaphoreType.DMA
    V = pltpu.VMEM
    state = (4, ROWS, width)
    flat_shape = (ROWS, width)
    s_pad = V((3, PADDED, LANES), F32)
    s_shift = V((3, 5, ROWS, LANES), BF)
    pair, square, tap_shape = (24, width), (4, width, width), (4, 25, width)

    core = own_segment & 1
    part = lax.axis_index("dp")
    place = lax.broadcasted_iota(jnp.int32, (10,), 0)
    early = jnp.pad(picks.reshape(4), (6, 0))
    for i, value in ((0, own_segment >> 1), (1, core), (4, part >> 2), (5, part & 3)):
        early = jnp.where(place == i, value, early)
    early = lax.optimization_barrier(early)

    wown, woth = call(
        weight_kernel,
        [(pair, BF), (pair, BF)],
        [SMEM, HBM],
        [V((4, 12, 8, width), BF), V((12, 8, width), F32), V((2, 24, width), F32), DMA((4,))],
        cost=1000,
    )(early, weights.transpose(0, 2, 1, 3))
    wrecv = lax.ppermute(woth, "segment", swap)
    (message,) = call(join_kernel, [((48, width), BF)], [VMEM, VMEM], [], cost=1000)(wown, wrecv)
    (triple,) = call(stack_kernel, [((3, 48, width), BF)], [VMEM] * 3, [], cost=1000)(
        along(message, 1, 0), message, along(message, 7, 0)
    )
    came_ahead, came_back = along(triple, 3, 0), along(triple, 5, 0)
    columns = [triple] + [along(triple, 0, dy) for dy in (1, 2, 3)]
    (outer,) = call(gather_kernel, [((5, 48, width), BF)], [VMEM] * 2, [], cost=1000)(
        came_ahead, came_back
    )
    after, sizes, outer = lax.optimization_barrier((early, section_sizes, outer))
    columns += [outer] + [along(outer, 0, dy) for dy in (1, 2, 3)]
    kown, kother = call(
        tap_kernel,
        [((2, 25, width), BF)] * 2,
        [SMEM, HBM],
        [V((4, 25, 8, width), BF), V((25, 8, width), F32), V((25, width), F32), DMA((4,))],
    )(after, kernels.transpose(0, 2, 1, 3))
    koth = lax.ppermute(kother, "segment", swap)
    sizes_other = lax.ppermute(sizes, "segment", swap)
    size_low = jnp.where(core == 0, section_sizes[0], sizes_other[0])
    size_high = jnp.where(core == 0, sizes_other[0], section_sizes[0])
    meta = jnp.where(place == 2, size_low, jnp.where(place == 3, size_high, early))
    edges = ((0, 0), (0, PITCH - SIDE), (0, 0))
    img = jnp.pad(images[0], edges).reshape(flat_shape)
    y, wall, taps, hs, ds = call(
        first_kernel,
        [(flat_shape, BF), (square, BF), (tap_shape, F32), (state, BF), (state, F32)],
        [SMEM] + [VMEM] * 11,
        [s_pad, s_shift, V((4, 8, 48, width), BF)],
    )(meta, img, *columns, kown, koth)
    y, late, cotangent = lax.optimization_barrier((y, early, cotangent))
    cur = lax.ppermute(y, "segment", ahead)
    chosen = lax.dynamic_index_in_dim(cotangent[:, 0], core, 0, keepdims=False)
    cot = jnp.pad(chosen, edges).reshape(flat_shape)
    fown, foth, sown, soth = call(
        moment_kernel,
        [(pair, F32)] * 4,
        [SMEM, HBM, HBM],
        [V((8, 12, 8, width), F32), DMA((8,))],
    )(late, first_moment.transpose(0, 2, 1, 3), second_moment.transpose(0, 2, 1, 3))
    cur, cot, fown = lax.optimization_barrier((cur, cot, fown))
    for step in (1, 2):
        y, hs, ds = call(
            functools.partial(forward_kernel, step),
            [(flat_shape, BF), (state, BF), (state, F32)],
            [SMEM] + [VMEM] * 5,
            [s_pad, s_shift],
            {4: 1, 5: 2},
        )(meta, cur, wall, taps, hs, ds)
        cur = lax.ppermute(y, "segment", ahead)
    y, hs, ys, ds = call(
        functools.partial(middle_kernel, 3),
        [(flat_shape, BF), (state, BF), (state, BF), (state, F32)],
        [SMEM] + [VMEM] * 6,
        [s_pad, s_shift],
        {5: 1, 6: 3},
    )(meta, cur, cot, wall, taps, hs, ds)
    cur = lax.ppermute(y, "segment", behind)
    for step in (2, 1):
        y, ys = call(
            functools.partial(backward_kernel, step),
            [(flat_shape, BF), (state, BF)],
            [SMEM] + [VMEM] * 5,
            [s_pad, s_shift],
            {5: 1},
        )(meta, cur, wall, taps, ds, ys)
        cur = lax.ppermute(y, "segment", behind)
    inner_shape, outer_shape, single = (3, 48, width), (5, 48, width), (48, width)
    *sends, _ = call(
        last_kernel,
        [(inner_shape, BF)] * 4 + [(outer_shape, BF)] * 4 + [(state, BF)],
        [SMEM] + [VMEM] * 6,
        [V(flat_shape, BF), s_pad, s_shift, V((2, width, width), F32), V((4, 8, 48, width), BF)],
        {6: 8},
    )(meta, cur, wall, taps, ds, hs, ys)
    outer_came = [along(sends[4 + dy], 0, dy) for dy in (1, 2, 3)]
    inner_came = [along(sends[dy], 0, dy) for dy in (1, 2, 3)]
    plus, minus = call(
        outer_sum_kernel,
        [(inner_shape, BF), ((2, 48, width), BF)],
        [VMEM] * 4,
        [],
        cost=1000,
    )(sends[4], *outer_came)
    down, stays, up = call(
        inner_sum_kernel, [(single, BF), (single, F32), (single, BF)], [VMEM] * 6, [], cost=1000
    )(sends[0], *inner_came, along(plus, 3, 0), along(minus, 5, 0))
    own, for_other = call(
        sum_kernel, [(pair, F32), (pair, F32)], [VMEM] * 3, [V((48, width), F32)], cost=1000
    )(stays, along(up, 1, 0), along(down, 7, 0))
    other = lax.ppermute(for_other, "segment", swap)
    rows = (2, 12, 2, width)
    news = call(
        functools.partial(adam_kernel, float(total_rows)),
        [(rows, BF), (rows, F32), (rows, F32)],
        [SMEM] + [VMEM] * 8,
        [V(pair, F32)],
    )(meta, own, other, wown, woth, fown, foth, sown, soth)
    return tuple(new.transpose(0, 2, 1, 3) for new in news)


def solution(mesh):
    return jax.shard_map(
        body,
        mesh=mesh,
        in_specs=(
            P("dp", None, None, None),
            P(None, "dp", None, None, None),
            P(None, "segment"),
            P("segment"),
            P("segment", None, None, None),
            P("segment", None, "dp", None),
            P("segment", None, "dp", None),
            P("segment", None, "dp", None),
        ),
        out_specs=(
            P(None, "segment", "dp", None),
            P(None, "segment", "dp", None),
            P(None, "segment", "dp", None),
        ),
        check_vma=False,
    )
```

```python
import functools

import jax
import jax.numpy as jnp
from jax import lax
from jax.experimental import pallas as pl
from jax.experimental.pallas import tpu as pltpu
from jax.sharding import PartitionSpec as P

first_decay = 0.9
second_decay = 0.999
learn_rate = 0.01
adam_epsilon = 1e-08
first_bias = 1.0 - 0.9**10
second_bias = 1.0 - 0.999**10

SIDE = 14
PITCH = 16
ROWS = SIDE * PITCH
LANES = 128
HEAD = 8 + 2 * PITCH
PADDED = 8 + (SIDE + 4) * PITCH + 8
BF = jnp.bfloat16
F32 = jnp.float32

HBM = pl.BlockSpec(memory_space=pltpu.HBM)
SMEM = pl.BlockSpec(memory_space=pltpu.SMEM)


VMEM = pl.BlockSpec(memory_space=pltpu.VMEM)


def call(kernel, outs, in_specs, scratch, aliases=None, cost=2_000_000_000, grant=8 << 20):
    return pl.pallas_call(
        kernel,
        out_shape=[jax.ShapeDtypeStruct(s, d) for s, d in outs],
        in_specs=in_specs,
        out_specs=[VMEM] * len(outs),
        scratch_shapes=scratch,
        input_output_aliases=aliases or {},
        compiler_params=pltpu.CompilerParams(vmem_limit_bytes=grant),
        cost_estimate=pl.CostEstimate(flops=cost, bytes_accessed=1_000_000, transcendentals=0),
    )


def keep_mask(shape):
    return (lax.broadcasted_iota(jnp.int32, shape, 0) & (PITCH - 1)) < SIDE


def shift_rows(pad, shifted, group):
    for e in range(-2, 3):
        for p in range(SIDE):
            rows = pl.ds(PITCH * p, PITCH)
            window = pad[group, pl.ds(HEAD + PITCH * p + e, PITCH), :]
            shifted[group, e + 2, rows, :] = window.astype(BF)


def conv_rows(shifted, taps, group, flipped, emit):
    sign = -1 if flipped else 1
    cols = pl.ds(group * LANES, LANES)
    weights = [
        jnp.broadcast_to(taps[pl.ds(i, 1), cols], (PITCH, LANES)).astype(BF) for i in range(25)
    ]
    for p in range(0, SIDE, 1):
        totals = [None] * 1
        for columns in ((-2, -1), (0,), (1, 2)):
            partial = [None] * 1
            for e in columns:
                for da in range(-2, 2 + 1):
                    if not 0 <= p + da < SIDE:
                        continue
                    window = shifted[group, e + 2, pl.ds(PITCH * (p + da), PITCH), :]
                    for k in range(1):
                        a = da - k
                        if -2 <= a <= 2:
                            tap = (sign * a + 2) * 5 + (sign * e + 2)
                            term = weights[tap] * window
                            partial[k] = term if partial[k] is None else partial[k] + term
            for k in range(1):
                wide = partial[k].astype(F32)
                totals[k] = wide if totals[k] is None else totals[k] + wide
        for k in range(1):
            emit(p + k, totals[k])


def clear_pad(pad):
    for g in range(3):
        pad[g, pl.ds(0, HEAD), :] = jnp.zeros((HEAD, LANES), F32)
        pad[g, pl.ds(HEAD + ROWS, PADDED - HEAD - ROWS), :] = jnp.zeros(
            (PADDED - HEAD - ROWS, LANES), F32
        )


def fill_pad(pad, value):
    for g in range(3):
        pad[g, pl.ds(HEAD, ROWS), :] = value[:, g * LANES : (g + 1) * LANES]


def live_of(meta, t):
    odd = (t & 1) == 1
    count = jnp.where(t < 2, meta[2], meta[3])
    return jnp.logical_or(jnp.logical_not(odd), count == 2)


def run_forward(meta, pad, shifted, flat, wall, taps, hs, ds, skip_last):
    last = jnp.where(meta[3] == 2, 3, 2)
    fill_pad(pad, flat[...].astype(F32))

    def slot(t, carry):
        @pl.when(live_of(meta, t))
        def _():
            early = None
            for g in range(3):
                if g == 2:
                    early = jnp.dot(
                        hs[t, :, pl.ds(0, 2 * LANES)],
                        wall[t, pl.ds(0, 2 * LANES), :],
                        preferred_element_type=F32,
                    )

                def emit(p, u, g=g):
                    rows, cols = pl.ds(p * PITCH, PITCH), pl.ds(g * LANES, LANES)
                    s = 0.5 * jnp.tanh(0.5 * u) + 0.5
                    us = u * s
                    hs[t, rows, cols] = us.astype(BF)
                    ds[t, rows, cols] = s * (1.0 + (u - us))

                shift_rows(pad, shifted, g)
                conv_rows(shifted, taps.at[t], g, False, emit)

            def update():
                value = early + jnp.dot(
                    hs[t, :, pl.ds(2 * LANES, LANES)],
                    wall[t, pl.ds(2 * LANES, LANES), :],
                    preferred_element_type=F32,
                )
                value = flat[...].astype(F32) + value
                rounded = jnp.where(keep_mask(value.shape), value, 0.0).astype(BF)
                flat[...] = rounded
                fill_pad(pad, rounded.astype(F32))

            if skip_last:
                pl.when(t != last)(update)
            else:
                update()

        return carry

    lax.fori_loop(0, 4, slot, 0)


def run_backward(meta, pad, shifted, flat, wall, taps, ds, ys, skip_first):
    def slot(i, carry):
        t = 3 - i

        @pl.when(live_of(meta, t))
        def _():
            ys[t] = flat[...]

            def chain():
                for g in range(3):
                    part = pl.ds(g * LANES, LANES)
                    dh = lax.dot_general(
                        ys[t], wall[t, part, :], (((1,), (1,)), ((), ())), preferred_element_type=F32
                    )
                    pad[g, pl.ds(HEAD, ROWS), :] = dh * ds[t, :, part]

                    def emit(p, total, g=g):
                        rows, cols = pl.ds(p * PITCH, PITCH), pl.ds(g * LANES, LANES)
                        value = ys[t, rows, cols].astype(F32) + total
                        keep = lax.broadcasted_iota(jnp.int32, value.shape, 0) < SIDE
                        flat[rows, cols] = jnp.where(keep, value, 0.0).astype(BF)

                    shift_rows(pad, shifted, g)
                    conv_rows(shifted, taps.at[t], g, True, emit)

            if skip_first:
                pl.when(t != 0)(chain)
            else:
                chain()

        return carry

    lax.fori_loop(0, 4, slot, 0)


def first_kernel(meta, img, *refs):
    inner, outer, (kown, koth, y, wall, taps, hs, ds, pad, shifted, packed) = refs[:4], refs[4:8], refs[8:]
    core, z, yy = meta[1], meta[4], meta[5]
    for i in range(4):
        row = (yy - i) & 3
        for k, shift in enumerate((1, 0, 7)):
            packed[row, shift] = inner[i][k]
        packed[row, pl.ds(2, 5)] = outer[i][...]
    for o, kref in enumerate((kown, koth)):
        for j in range(2):
            taps[(2 * o + j + 2 * core) & 3] = kref[j].astype(F32)
    for o in range(2):
        base = (2 * o + 2 * core) & 3
        place = pl.ds(24 * o, 24)
        for i in range(16):
            shift = (z - i // 2) & 7
            one = packed[2 * (i % 2), shift, place, :].astype(F32)
            two = packed[2 * (i % 2) + 1, shift, place, :].astype(F32)
            rows = pl.ds(24 * i, 24)
            wall[base, rows, :] = jnp.concatenate([one[:12], two[:12]], axis=0).astype(BF)
            wall[base + 1, rows, :] = jnp.concatenate([one[12:], two[12:]], axis=0).astype(BF)

    @pl.when(meta[0] == 0)
    def _():
        clear_pad(pad)
        y[...] = img[...]
        run_forward(meta, pad, shifted, y, wall, taps, hs, ds, False)


def forward_kernel(step, meta, cur, wall, taps, hin, din, y, hs, ds, pad, shifted):
    del hin, din

    @pl.when(meta[0] == step)
    def _():
        clear_pad(pad)
        y[...] = cur[...]
        run_forward(meta, pad, shifted, y, wall, taps, hs, ds, False)


def middle_kernel(step, meta, cur, cot, wall, taps, hin, din, y, hs, ys, ds, pad, shifted):
    del hin, din

    @pl.when(meta[0] == step)
    def _():
        clear_pad(pad)
        y[...] = cur[...]
        run_forward(meta, pad, shifted, y, wall, taps, hs, ds, True)
        y[...] = cot[...]
        run_backward(meta, pad, shifted, y, wall, taps, ds, ys, False)


def backward_kernel(step, meta, cur, wall, taps, ds, yin, y, ys, pad, shifted):
    del yin

    @pl.when(meta[0] == step)
    def _():
        clear_pad(pad)
        y[...] = cur[...]
        run_backward(meta, pad, shifted, y, wall, taps, ds, ys, False)


def last_kernel(meta, cur, wall, taps, ds, hs, yin, inner0, inner1, inner2, inner3,
                outer0, outer1, outer2, outer3, ys, flat, pad, shifted, total, send):
    del yin
    core, z, yy = meta[1], meta[4], meta[5]

    @pl.when(meta[0] == 0)
    def _():
        clear_pad(pad)
        flat[...] = cur[...]
        run_backward(meta, pad, shifted, flat, wall, taps, ds, ys, True)

    def term(t):
        return lax.dot_general(
            hs[t], ys[t], (((0,), (0,)), ((), ())), preferred_element_type=F32
        )

    for o in range(2):
        base = (2 * o + 2 * core) & 3
        live = live_of(meta, base + 1)
        total[0] = term(base)

        @pl.when(live)
        def _():
            total[1] = term(base + 1)

        @pl.when(jnp.logical_not(live))
        def _():
            total[1] = jnp.zeros(total.shape[1:], F32)

        for i in range(16):
            rows = pl.ds(24 * i, 24)
            one, two = total[0, rows, :], total[1, rows, :]
            place = pl.ds(24 * o, 24)
            shift = (i // 2 - z) & 7
            send[2 * (i % 2), shift, place, :] = jnp.concatenate(
                [one[:12], two[:12]], axis=0
            ).astype(BF)
            send[2 * (i % 2) + 1, shift, place, :] = jnp.concatenate(
                [one[12:], two[12:]], axis=0
            ).astype(BF)
    for i, (inner, outer) in enumerate(
        ((inner0, outer0), (inner1, outer1), (inner2, outer2), (inner3, outer3))
    ):
        row = (yy + i) & 3
        for k, shift in enumerate((7, 0, 1)):
            inner[k] = send[row, shift]
        outer[...] = send[row, pl.ds(2, 5)]


def picked(meta, n, j):
    return meta[6 + 2 * n + j]


def weight_kernel(meta, weights, own, oth, buf, wide, rows, sems):
    core = meta[1]
    copies = []
    for k, out in enumerate((own, oth)):
        for j in range(2):
            op = picked(meta, core if k == 0 else 1 - core, j)
            group = pl.ds(pl.multiple_of((op >> 3) << 3, 8), 8)
            copies.append(
                pltpu.make_async_copy(
                    weights.at[j, :, group, :], buf.at[2 * k + j], sems.at[2 * k + j]
                )
            )
            copies[-1].start()
    for k, out in enumerate((own, oth)):
        for j in range(2):
            op = picked(meta, core if k == 0 else 1 - core, j)
            copies[2 * k + j].wait()
            wide[...] = buf[2 * k + j].astype(F32)
            for r in range(12):
                rows[k, pl.ds(12 * j + r, 1), :] = wide[r, pl.ds(op & 7, 1), :]
        out[...] = rows[k].astype(BF)


def tap_kernel(meta, kernels, kown, koth, kbuf, kwide, krows, sems):
    core = meta[1]
    copies = []
    for k in range(2):
        for j in range(2):
            op = picked(meta, core if k == 0 else 1 - core, j)
            group = pl.ds(pl.multiple_of((op >> 3) << 3, 8), 8)
            i = 2 * k + j
            copies.append(
                pltpu.make_async_copy(kernels.at[j, :, group, :], kbuf.at[i], sems.at[i])
            )
            copies[-1].start()
    for k, out in enumerate((kown, koth)):
        for j in range(2):
            lane = picked(meta, core if k == 0 else 1 - core, j) & 7
            copies[2 * k + j].wait()
            kwide[...] = kbuf[2 * k + j].astype(F32)
            for r in range(25):
                krows[pl.ds(r, 1), :] = kwide[r, pl.ds(lane, 1), :]
            out[j] = krows[...].astype(BF)


def moment_kernel(meta, first, second, fown, foth, sown, soth, mbuf, sems):
    core = meta[1]
    chosen = []
    for k, (fout, sout) in enumerate(((fown, sown), (foth, soth))):
        for j in range(2):
            op = picked(meta, core if k == 0 else 1 - core, j)
            group = pl.ds(pl.multiple_of((op >> 3) << 3, 8), 8)
            i = 2 * k + j
            copies = [
                pltpu.make_async_copy(first.at[j, :, group, :], mbuf.at[i], sems.at[i]),
                pltpu.make_async_copy(second.at[j, :, group, :], mbuf.at[4 + i], sems.at[4 + i]),
            ]
            chosen.append((copies, op & 7, fout, sout, i, j))
            for c in copies:
                c.start()
    for copies, lane, fout, sout, i, j in chosen:
        for c in copies:
            c.wait()
        for r in range(12):
            fout[pl.ds(2 * r + j, 1), :] = mbuf[i, r, pl.ds(lane, 1), :]
            sout[pl.ds(2 * r + j, 1), :] = mbuf[4 + i, r, pl.ds(lane, 1), :]


def stack_kernel(*refs):
    out = refs[-1]
    for i, ref in enumerate(refs[:-1]):
        out[i] = ref[...]


def gather_kernel(ahead, back, out):
    for refs, shifts in ((ahead, (4, 3, 2)), (back, (6, 5))):
        for i, shift in enumerate(shifts):
            out[shift - 2] = refs[i]


def join_kernel(own, recv, out):
    out[pl.ds(0, 24), :] = own[...]
    out[pl.ds(24, 24), :] = recv[...]


def four(refs, i):
    a, b, c, d = refs
    return (a[i].astype(F32) + b[i].astype(F32)) + (c[i].astype(F32) + d[i].astype(F32))


def outer_sum_kernel(a, b, c, d, plus, minus):
    for i in range(5):
        ref = plus if i < 3 else minus
        ref[i % 3] = four((a, b, c, d), i).astype(ref.dtype)


def inner_sum_kernel(a, b, c, d, plus, minus, down, stays, up):
    for i, ref in enumerate((down, stays, up)):
        total = four((a, b, c, d), i) + plus[i].astype(F32)
        if i > 0:
            total = total + minus[i - 1].astype(F32)
        ref[...] = total.astype(ref.dtype)


def sum_kernel(near, *refs):
    own, other, wide = refs[-3:]
    total = near[...]
    for ref in refs[:-3]:
        total = total + ref[...].astype(F32)
    wide[...] = total
    for o, out in enumerate((own, other)):
        for j in range(2):
            for r in range(12):
                out[pl.ds(2 * r + j, 1), :] = wide[pl.ds(24 * o + 12 * j + r, 1), :]


def adam_kernel(total_rows, meta, mine, theirs, wown, woth, fown, foth, sown, soth,
                new_w, new_f, new_s, wide):
    core = meta[1]
    count = jnp.where(core == 0, meta[2], meta[3])
    odd = (lax.broadcasted_iota(jnp.int32, mine.shape, 0) & 1) == 1
    same_first = jnp.where(picked(meta, 0, 0) == picked(meta, 1, 0), 1.0, 0.0)
    same_second = jnp.where(picked(meta, 0, 1) == picked(meta, 1, 1), 1.0, 0.0)
    same = jnp.where(odd, same_second, same_first) > 0.5
    live = jnp.where(odd, count, 2) == 2
    for k, (wref, fref, sref) in enumerate(((wown, fown, sown), (woth, foth, soth))):
        n = core if k == 0 else 1 - core
        grad, rest = (mine[...], theirs[...]) if k == 0 else (theirs[...], mine[...])
        grad = (grad + jnp.where(same, rest, jnp.zeros_like(rest))) / total_rows
        source = wref[...].astype(F32)
        for j in range(2):
            for r in range(12):
                wide[pl.ds(2 * r + j, 1), :] = source[12 * j + r : 12 * j + r + 1, :]
        weight, one, two = wide[...], fref[...], sref[...]
        next_one = first_decay * one + (1.0 - first_decay) * grad
        next_two = second_decay * two + (1.0 - second_decay) * grad * grad
        next_weight = weight - learn_rate * (next_one / first_bias) / (
            jnp.sqrt(next_two / second_bias) + adam_epsilon
        )
        out_w = jnp.where(live, next_weight, weight)
        out_f = jnp.where(live, next_one, one)
        out_s = jnp.where(live, next_two, two)
        for r in range(12):
            new_w[n, r] = out_w[2 * r : 2 * r + 2].astype(BF)
            new_f[n, r] = out_f[2 * r : 2 * r + 2]
            new_s[n, r] = out_s[2 * r : 2 * r + 2]


def body(images, cotangent, picks, section_sizes, kernels, weights, first_moment, second_moment):
    width = images.shape[-1]
    own_segment = lax.axis_index("segment")
    segments = lax.axis_size("segment")
    parts = lax.axis_size("dp")
    total_rows = images.shape[0] * images.shape[1] * images.shape[2] * parts
    swap = [(s, s ^ 1) for s in range(segments)]
    ahead = [(s, (s + 2) % segments) for s in range(segments)]
    behind = [(s, (s - 2) % segments) for s in range(segments)]

    def along(value, dz, dy):
        pairs = [
            (4 * z + y, 4 * ((z + dz) % 8) + (y + dy) % 4) for z in range(8) for y in range(4)
        ]
        return lax.ppermute(value, "dp", pairs)


    DMA = pltpu.SemaphoreType.DMA
    V = pltpu.VMEM
    state = (4, ROWS, width)
    flat_shape = (ROWS, width)
    s_pad = V((3, PADDED, LANES), F32)
    s_shift = V((3, 5, ROWS, LANES), BF)
    pair, square, tap_shape = (24, width), (4, width, width), (4, 25, width)

    core = own_segment & 1
    part = lax.axis_index("dp")
    place = lax.broadcasted_iota(jnp.int32, (10,), 0)
    early = jnp.pad(picks.reshape(4), (6, 0))
    for i, value in ((0, own_segment >> 1), (1, core), (4, part >> 2), (5, part & 3)):
        early = jnp.where(place == i, value, early)
    early = lax.optimization_barrier(early)

    wown, woth = call(
        weight_kernel,
        [(pair, BF), (pair, BF)],
        [SMEM, HBM],
        [V((4, 12, 8, width), BF), V((12, 8, width), F32), V((2, 24, width), F32), DMA((4,))],
        cost=1000,
    )(early, weights.transpose(0, 2, 1, 3))
    wrecv = lax.ppermute(woth, "segment", swap)
    (message,) = call(join_kernel, [((48, width), BF)], [VMEM, VMEM], [], cost=1000)(wown, wrecv)
    (triple,) = call(stack_kernel, [((3, 48, width), BF)], [VMEM] * 3, [], cost=1000)(
        along(message, 1, 0), message, along(message, 7, 0)
    )
    came_ahead, came_back = along(triple, 3, 0), along(triple, 5, 0)
    two = along(triple, 0, 2)
    one, three = along(triple, 0, 1), along(triple, 0, 3)

    def outer_of(came_ahead, came_back):
        return call(gather_kernel, [((5, 48, width), BF)], [VMEM] * 2, [], cost=1000)(
            came_ahead, came_back
        )[0]

    outer = outer_of(came_ahead, came_back)
    after, sizes, outer, two = lax.optimization_barrier((early, section_sizes, outer, two))
    outer_two = outer_of(along(two, 3, 0), along(two, 5, 0))
    columns = [triple, one, two, three]
    columns += [outer, along(outer, 0, 1), outer_two, along(outer, 0, 3)]
    kown, kother = call(
        tap_kernel,
        [((2, 25, width), BF)] * 2,
        [SMEM, HBM],
        [V((4, 25, 8, width), BF), V((25, 8, width), F32), V((25, width), F32), DMA((4,))],
    )(after, kernels.transpose(0, 2, 1, 3))
    koth = lax.ppermute(kother, "segment", swap)
    sizes_other = lax.ppermute(sizes, "segment", swap)
    size_low = jnp.where(core == 0, section_sizes[0], sizes_other[0])
    size_high = jnp.where(core == 0, sizes_other[0], section_sizes[0])
    meta = jnp.where(place == 2, size_low, jnp.where(place == 3, size_high, early))
    edges = ((0, 0), (0, PITCH - SIDE), (0, 0))
    img = jnp.pad(images[0], edges).reshape(flat_shape)
    y, wall, taps, hs, ds = call(
        first_kernel,
        [(flat_shape, BF), (square, BF), (tap_shape, F32), (state, BF), (state, F32)],
        [SMEM] + [VMEM] * 11,
        [s_pad, s_shift, V((4, 8, 48, width), BF)],
    )(meta, img, *columns, kown, koth)
    y, late, cotangent = lax.optimization_barrier((y, early, cotangent))
    cur = lax.ppermute(y, "segment", ahead)
    chosen = lax.dynamic_index_in_dim(cotangent[:, 0], core, 0, keepdims=False)
    cot = jnp.pad(chosen, edges).reshape(flat_shape)
    fown, foth, sown, soth = call(
        moment_kernel,
        [(pair, F32)] * 4,
        [SMEM, HBM, HBM],
        [V((8, 12, 8, width), F32), DMA((8,))],
    )(late, first_moment.transpose(0, 2, 1, 3), second_moment.transpose(0, 2, 1, 3))
    cur, cot, fown = lax.optimization_barrier((cur, cot, fown))
    for step in (1, 2):
        y, hs, ds = call(
            functools.partial(forward_kernel, step),
            [(flat_shape, BF), (state, BF), (state, F32)],
            [SMEM] + [VMEM] * 5,
            [s_pad, s_shift],
            {4: 1, 5: 2},
        )(meta, cur, wall, taps, hs, ds)
        cur = lax.ppermute(y, "segment", ahead)
    y, hs, ys, ds = call(
        functools.partial(middle_kernel, 3),
        [(flat_shape, BF), (state, BF), (state, BF), (state, F32)],
        [SMEM] + [VMEM] * 6,
        [s_pad, s_shift],
        {5: 1, 6: 3},
    )(meta, cur, cot, wall, taps, hs, ds)
    cur = lax.ppermute(y, "segment", behind)
    for step in (2, 1):
        y, ys = call(
            functools.partial(backward_kernel, step),
            [(flat_shape, BF), (state, BF)],
            [SMEM] + [VMEM] * 5,
            [s_pad, s_shift],
            {5: 1},
        )(meta, cur, wall, taps, ds, ys)
        cur = lax.ppermute(y, "segment", behind)
    inner_shape, outer_shape, single = (3, 48, width), (5, 48, width), (48, width)
    *sends, _ = call(
        last_kernel,
        [(inner_shape, BF)] * 4 + [(outer_shape, BF)] * 4 + [(state, BF)],
        [SMEM] + [VMEM] * 6,
        [V(flat_shape, BF), s_pad, s_shift, V((2, width, width), F32), V((4, 8, 48, width), BF)],
        {6: 8},
    )(meta, cur, wall, taps, ds, hs, ys)
    outer_came = [along(sends[4 + dy], 0, dy) for dy in (1, 2, 3)]
    inner_came = [along(sends[dy], 0, dy) for dy in (1, 2, 3)]
    plus, minus = call(
        outer_sum_kernel,
        [(inner_shape, BF), ((2, 48, width), BF)],
        [VMEM] * 4,
        [],
        cost=1000,
    )(sends[4], *outer_came)
    down, stays, up = call(
        inner_sum_kernel, [(single, BF), (single, F32), (single, BF)], [VMEM] * 6, [], cost=1000
    )(sends[0], *inner_came, along(plus, 3, 0), along(minus, 5, 0))
    own, for_other = call(
        sum_kernel, [(pair, F32), (pair, F32)], [VMEM] * 3, [V((48, width), F32)], cost=1000
    )(stays, along(up, 1, 0), along(down, 7, 0))
    other = lax.ppermute(for_other, "segment", swap)
    rows = (2, 12, 2, width)
    news = call(
        functools.partial(adam_kernel, float(total_rows)),
        [(rows, BF), (rows, F32), (rows, F32)],
        [SMEM] + [VMEM] * 8,
        [V(pair, F32)],
    )(meta, own, other, wown, woth, fown, foth, sown, soth)
    return tuple(new.transpose(0, 2, 1, 3) for new in news)


def solution(mesh):
    return jax.shard_map(
        body,
        mesh=mesh,
        in_specs=(
            P("dp", None, None, None),
            P(None, "dp", None, None, None),
            P(None, "segment"),
            P("segment"),
            P("segment", None, None, None),
            P("segment", None, "dp", None),
            P("segment", None, "dp", None),
            P("segment", None, "dp", None),
        ),
        out_specs=(
            P(None, "segment", "dp", None),
            P(None, "segment", "dp", None),
            P(None, "segment", "dp", None),
        ),
        check_vma=False,
    )
```
